32 devices in a mesh: fsdp: 8 (over y, x, core), tensor: 4 (over z).
Axes of the slice: x: 2, y: 2, z: 4, core: 2. Of those that a mesh axis runs over, the one named last changes fastest.
Arguments:
- tokens: bfloat16 [16, 448, 1024], P('fsdp'), may hold values from -6 to 6
- encoder: bfloat16 [16, 1500, 1024], P('fsdp'), may hold values from -6 to 6
- cotangent: bfloat16 [16, 448, 1024], P('fsdp'), may hold values from -8 to 8
- self_weights: bfloat16 [3, 1024, 1024], P(None, 'fsdp', 'tensor'), may hold values from -0.1875 to 0.1875
- self_biases: bfloat16 [2, 4, 256], P(None, 'tensor', 'fsdp'), may hold values from -0.3125 to 0.3125
- self_output: bfloat16 [1024, 1024], P('tensor', 'fsdp'), may hold values from -3 to 3
- cross_query: bfloat16 [1024, 1024], P('fsdp', 'tensor'), may hold values from -0.1875 to 0.1875
- cross_memory: bfloat16 [2, 1024, 1024], P(None, 'fsdp', 'tensor'), may hold values from -0.1875 to 0.1875
- cross_biases: bfloat16 [2, 4, 256], P(None, 'tensor', 'fsdp'), may hold values from -0.1875 to 0.1875
- cross_output: bfloat16 [1024, 1024], P('tensor', 'fsdp'), may hold values from -6 to 6
- hidden_weight: bfloat16 [1024, 4096], P('fsdp', 'tensor'), may hold values from -0.1875 to 0.1875
- hidden_bias: bfloat16 [4, 1024], P('tensor', 'fsdp'), may hold values from -3 to 3
- reduce_weight: bfloat16 [4096, 1024], P('tensor', 'fsdp'), may hold values from -0.09375 to 0.09375
- norm_gains: bfloat16 [3, 1024], P(None, 'fsdp'), may hold values from 0.5 to 1.5
- norm_shifts: bfloat16 [3, 1024], P(None, 'fsdp'), may hold values from -1.75 to 1.75
- branch_biases: bfloat16 [3, 1024], P(None, 'fsdp'), may hold values from -1.75 to 1.75
Outputs:
- layer_output: bfloat16 [16, 448, 1024], P('fsdp')
- tokens_gradient: bfloat16 [16, 448, 1024], P('fsdp')
- encoder_gradient: bfloat16 [16, 1500, 1024], P('fsdp', 'tensor')
- self_weights_gradient: float32 [3, 1024, 1024], P(None, 'fsdp', 'tensor')
- self_biases_gradient: float32 [2, 4, 256], P(None, 'tensor', 'fsdp')
- self_output_gradient: float32 [1024, 1024], P('tensor', 'fsdp')
- cross_query_gradient: float32 [1024, 1024], P('fsdp', 'tensor')
- cross_memory_gradient: float32 [2, 1024, 1024], P(None, 'fsdp', 'tensor')
- cross_biases_gradient: float32 [2, 4, 256], P(None, 'tensor', 'fsdp')
- cross_output_gradient: float32 [1024, 1024], P('tensor', 'fsdp')
- hidden_weight_gradient: float32 [1024, 4096], P('fsdp', 'tensor')
- hidden_bias_gradient: float32 [4, 1024], P('tensor', 'fsdp')
- reduce_weight_gradient: float32 [4096, 1024], P('tensor', 'fsdp')
- norm_gains_gradient: float32 [3, 1024], P(None, 'fsdp')
- norm_shifts_gradient: float32 [3, 1024], P(None, 'fsdp')
- branch_biases_gradient: float32 [3, 1024], P(None, 'fsdp')
The draws below stay inside these ranges and needn't reach their ends.
All inputs are finite; a program needn't handle non-finite values.
Results may differ from the reference program's by a relative error of at most 0.035.
Values may be sent and summed in bfloat16 or wider, within the bound.
A program may use at most 128 MiB of HBM per device.

```python
import jax
import jax.numpy as jnp
from jax import lax

D = 1024
HEADS = 16
HEAD_DIM = 64
FF = 4096
LEN = 448
FRAMES = 1500
SEQS = 16
N_TENSOR = 4


def strengthened(result, key, source, target, blocks, factor):
    owner, partner = [(jnp.arange(result.shape[position]) // (result.shape[position] // blocks)).reshape([-1 if axis == position else 1 for axis in range(result.ndim)]) for position in (source, target)]
    chosen = jax.random.permutation(key, blocks)[partner]
    strong = (owner == chosen) | (owner == (partner + blocks // 2) % blocks)
    return jnp.where(strong, factor * result, result)


def levels(stream_key, dims, shards, low, top_value):
    level, own = 1.0, jax.random.fold_in(stream_key, 6)
    for axis_at, parts in shards:
        draws = jnp.exp(jax.random.uniform(jax.random.fold_in(own, axis_at), (parts,), jnp.float32, low / len(shards), top_value / len(shards)))
        level = level * jnp.repeat(draws, dims[axis_at] // parts).reshape([-1 if axis == axis_at else 1 for axis in range(len(dims))])
    return level


def noise(stream_key, extent, scale, bound, cuts=(), held_as=jnp.bfloat16):
    array = scale * jax.random.normal(stream_key, extent, jnp.float32)
    if cuts:
        array = array * levels(stream_key, extent, cuts, -0.22, 0.18)
    return jnp.clip(array, -bound, bound).astype(held_as)


def gaussian_with(stream_key, extent, scale, most, cuts, heavy, held_as=jnp.bfloat16):
    array = scale * jax.random.normal(stream_key, extent, jnp.float32)
    if cuts:
        array = array * levels(stream_key, extent, cuts, -0.22, 0.18)
    return jnp.clip(strengthened(array, jax.random.fold_in(stream_key, 3), *heavy), -most, most).astype(held_as)


def setup_inputs(seed: int = 0) -> dict:
    arg_keys = jax.random.split(jax.random.key(seed), 17)
    return {
        "tokens": noise(arg_keys[0], (SEQS, LEN, D), 1.0, 6.0, ((0, 8),)),
        "encoder": noise(arg_keys[1], (SEQS, FRAMES, D), 1.0, 6.0, ((0, 8),)),
        "cotangent": gaussian_with(arg_keys[2], (SEQS, LEN, D), 1.0, 8.0, ((0, 8),), (0, 2, 8, 2.0)),
        "self_weights": noise(arg_keys[3], (3, D, D), D ** -0.5, 0.1875, ((1, 8), (2, 4))),
        "self_biases": noise(arg_keys[4], (2, N_TENSOR, D // N_TENSOR), 0.05, 0.3125, ((1, 4), (2, 8))),
        "self_output": noise(arg_keys[5], (D, D), (2 * D // LEN) ** -0.5, 3.0, ((0, 4), (1, 8))),
        "cross_query": noise(arg_keys[6], (D, D), D ** -0.5, 0.1875, ((0, 8), (1, 4))),
        "cross_memory": noise(arg_keys[7], (2, D, D), D ** -0.5, 0.1875, ((1, 8), (2, 4))),
        "cross_biases": noise(arg_keys[8], (2, N_TENSOR, D // N_TENSOR), 0.03, 0.1875, ((1, 4), (2, 8))),
        "cross_output": noise(arg_keys[9], (D, D), (max(1, D // FRAMES)) ** -0.5, 6.0, ((0, 4), (1, 8))),
        "hidden_weight": noise(arg_keys[10], (D, FF), D ** -0.5, 0.1875, ((0, 8), (1, 4))),
        "hidden_bias": noise(arg_keys[11], (N_TENSOR, FF // N_TENSOR), 0.5, 3.0, ((0, 4), (1, 8))),
        "reduce_weight": noise(arg_keys[12], (FF, D), FF ** -0.5, 0.09375, ((0, 4), (1, 8))),
        "norm_gains": jnp.clip(1.0 + 0.1 * jax.random.normal(arg_keys[13], (3, D), jnp.float32), 0.5, 1.5).astype(jnp.bfloat16),
        "norm_shifts": noise(arg_keys[14], (3, D), 0.3, 1.75, ((1, 8),)),
        "branch_biases": noise(arg_keys[15], (3, D), 0.3, 1.75, ((1, 8),)),
    }


highest = lax.Precision.HIGHEST
epsilon = 1e-05
masked_score = -1000000000.0

@jax.custom_vjp
def low(v):
    return lax.optimization_barrier(v.astype(jnp.bfloat16)).astype(jnp.float32)

@jax.custom_vjp
def low_back(v):
    return v

def low_keep(v):
    return (low(v), None)

def low_pass(kept, grad):
    return (grad,)

def back_keep(v):
    return (v, None)

def back_low(kept, grad):
    return (low(grad),)
low.defvjp(low_keep, low_pass)
low_back.defvjp(back_keep, back_low)

def rounded(values):
    return low(low_back(values))

def matmul(left, right):
    return jnp.dot(left, right, precision=highest)

def layer_norm(values, gain, shift):
    centre = values - lax.optimization_barrier(jnp.mean(values, axis=-1, keepdims=True))
    spread = lax.optimization_barrier(jnp.mean(centre * centre, axis=-1, keepdims=True))
    return centre * lax.rsqrt(spread + epsilon) * gain + shift

def grouped(mixed, weight):
    count = weight.shape[0] // N_TENSOR
    pieces = jnp.einsum('slgc,gcd->gsld', mixed.reshape(mixed.shape[0], mixed.shape[1], N_TENSOR, count), weight.reshape(N_TENSOR, count, weight.shape[1]), precision=highest)
    return lax.optimization_barrier(jnp.sum(low(pieces), axis=0))

def attention(queries, keys, values, causal):
    scale = HEAD_DIM ** (-0.5)

    def one_clip(blocks):
        query_clip, key_clip, value_clip = blocks
        query_heads = query_clip.reshape(query_clip.shape[0], HEADS, HEAD_DIM)
        key_heads = key_clip.reshape(key_clip.shape[0], HEADS, HEAD_DIM)
        value_heads = value_clip.reshape(value_clip.shape[0], HEADS, HEAD_DIM)
        scores = low_back(jnp.einsum('qhd,khd->hqk', query_heads, key_heads, precision=highest) * scale)
        if causal:
            rows = lax.broadcasted_iota(jnp.int32, scores.shape[1:], 0)
            columns = lax.broadcasted_iota(jnp.int32, scores.shape[1:], 1)
            scores = jnp.where(columns <= rows, scores, masked_score)
        chance = low(jax.nn.softmax(scores, axis=-1))
        mixed = jnp.einsum('hqk,khd->qhd', chance, value_heads, precision=highest)
        return mixed.reshape(query_clip.shape[0], D)
    return lax.map(jax.checkpoint(one_clip), (queries, keys, values))

def forward(params, start, memory):
    self_weights, self_biases, self_output, cross_query, cross_memory, cross_biases, cross_output, hidden_weight, hidden_bias, reduce_weight, norm_gains, norm_shifts, branch_biases = params
    self_bias = self_biases.reshape(2, D)
    cross_bias = cross_biases.reshape(2, D)
    normed_one = low(layer_norm(start, norm_gains[0], norm_shifts[0]))
    queries = low(low_back(matmul(normed_one, self_weights[0])) + self_bias[0])
    keys = rounded(matmul(normed_one, self_weights[1]))
    values = low(low_back(matmul(normed_one, self_weights[2])) + self_bias[1])
    mixed_one = rounded(attention(queries, keys, values, True))
    middle = start + low_back(grouped(mixed_one, self_output)) + branch_biases[0]
    normed_two = low(layer_norm(middle, norm_gains[1], norm_shifts[1]))
    cross_queries = low(low_back(matmul(normed_two, cross_query)) + cross_bias[0])
    cross_keys = rounded(matmul(memory, cross_memory[0]))
    cross_values = low(low_back(matmul(memory, cross_memory[1])) + cross_bias[1])
    mixed_two = rounded(attention(cross_queries, cross_keys, cross_values, False))
    later = middle + low_back(grouped(mixed_two, cross_output)) + branch_biases[1]
    normed_three = low(layer_norm(later, norm_gains[2], norm_shifts[2]))
    expanded = low_back(matmul(normed_three, hidden_weight)) + hidden_bias.reshape(FF)
    activated = low(jax.nn.gelu(expanded, approximate=False))
    return later + low_back(grouped(activated, reduce_weight)) + branch_biases[2]

def reference(tokens, encoder, cotangent, self_weights, self_biases, self_output, cross_query, cross_memory, cross_biases, cross_output, hidden_weight, hidden_bias, reduce_weight, norm_gains, norm_shifts, branch_biases):
    params = tuple((piece.astype(jnp.float32) for piece in (self_weights, self_biases, self_output, cross_query, cross_memory, cross_biases, cross_output, hidden_weight, hidden_bias, reduce_weight, norm_gains, norm_shifts, branch_biases)))
    start = tokens.astype(jnp.float32)
    memory = encoder.astype(jnp.float32)
    output, pullback = jax.vjp(forward, params, start, memory)
    grads, start_grad, memory_grad = pullback(cotangent.astype(jnp.float32))
    return (output.astype(jnp.bfloat16), start_grad.astype(jnp.bfloat16), memory_grad.astype(jnp.bfloat16), grads[0], grads[1], grads[2], grads[3], grads[4], grads[5], grads[6], grads[7], grads[8], grads[9], grads[10], grads[11], grads[12])
```

```python
import functools
import math

import jax
import jax.numpy as jnp
from jax import lax
from jax.experimental import pallas as pl
from jax.experimental.pallas import tpu as pltpu
from jax.sharding import PartitionSpec as P

HEAD_DIM = 64
PAIR = 2 * HEAD_DIM
GROUPS = 4
EPSILON = 1e-05
MASKED = -1e9
F32 = jnp.float32
BF16 = jnp.bfloat16
VMEM_LIMIT = 60 * 1024 * 1024


def params(**extra):
    return pltpu.CompilerParams(vmem_limit_bytes=VMEM_LIMIT, **extra)


def call(kernel, name, grid, ins, outs, args, scratch=(), flops=0, scalars=1, aliases=None):
    in_specs = [pl.BlockSpec(block, index) for block, index in ins]
    out_specs = [pl.BlockSpec(block, index) for _, _, block, index in outs]
    out_shape = [jax.ShapeDtypeStruct(shape, dtype) for shape, dtype, _, _ in outs]
    moved = sum(a.size * a.dtype.itemsize for a in args) + sum(
        math.prod(o.shape) * jnp.dtype(o.dtype).itemsize for o in out_shape
    )
    result = pl.pallas_call(
        kernel,
        name=name,
        out_shape=out_shape,
        grid_spec=pltpu.PrefetchScalarGridSpec(
            num_scalar_prefetch=scalars,
            grid=grid,
            in_specs=in_specs,
            out_specs=out_specs,
            scratch_shapes=list(scratch),
        ),
        compiler_params=params(),
        cost_estimate=pl.CostEstimate(flops=int(flops), bytes_accessed=int(moved), transcendentals=0),
    )(*args)
    return result


def fill_weights(g_ref, pieces, buffer):
    rows = pieces[0].shape[-2]
    g = g_ref[0]
    for j, piece in enumerate(pieces):
        buffer[pl.ds(pl.multiple_of((g ^ j) * rows, rows), rows), :] = piece[...]


def nn_kernel(mode, g_ref, *refs):
    x_ref, pieces, rest = refs[0], refs[1:5], refs[5:]
    *extra, buffer = rest
    fill_weights(g_ref, pieces, buffer)
    acc = jnp.dot(x_ref[...], buffer[...], preferred_element_type=F32)
    if mode == "plain":
        (out,) = extra
        out[...] = acc.astype(out.dtype)
    elif mode == "bias":
        bias, out = extra
        out[...] = (acc + bias[...]).astype(out.dtype)
    elif mode == "gelu":
        bias, out, slope = extra
        expanded = acc + bias[...]
        phi = 0.5 * (1.0 + lax.erf(expanded * (0.5**0.5)))
        out[...] = (expanded * phi).astype(out.dtype)
        density = jnp.exp(expanded * expanded * -0.5) * ((2.0 * math.pi) ** -0.5)
        slope[...] = (phi + expanded * density).astype(slope.dtype)
    elif mode == "slope":
        slope, out, sums = extra
        grad = acc * slope[...].astype(F32)
        out[...] = grad.astype(out.dtype)
        sums[...] = jnp.broadcast_to(jnp.sum(grad, axis=0, keepdims=True), sums.shape)


def mm_nn(name, g, x, pieces, width, col, mode="plain", bias=None, slope=None):
    m, d = x.shape
    slots, rows, _ = pieces[0].shape
    ins = [((m, d), lambda s, g: (0, 0))]
    ins += [((None, rows, width), lambda s, g: (s, 0, col))] * GROUPS
    args = [g, x, *pieces]
    outs = [((m, slots * width), BF16, (m, width), lambda s, g: (0, s))]
    if mode in ("bias", "gelu"):
        ins.append(((None, 1, width), lambda s, g: (s, 0, 0)))
        args.append(bias)
    if mode == "gelu":
        outs.append(((m, slots * width), F32, (m, width), lambda s, g: (0, s)))
    if mode == "slope":
        ins.append(((m, width), lambda s, g: (0, s)))
        args.append(slope)
        outs.append(((slots, 8, width), F32, (None, 8, width), lambda s, g: (s, 0, 0)))
    return call(
        functools.partial(nn_kernel, mode), name, (slots,), ins, outs, args,
        scratch=[pltpu.VMEM((rows * GROUPS, width), BF16)],
        flops=2 * m * d * slots * width,
    )


def nt_kernel(slots, g_ref, *refs):
    x_ref, pieces, (out, acc, buffer) = refs[0], refs[1:5], refs[5:]
    s = pl.program_id(0)
    fill_weights(g_ref, pieces, buffer)
    part = lax.dot_general(
        x_ref[...], buffer[...], (((1,), (1,)), ((), ())), preferred_element_type=F32
    )

    @pl.when(s == 0)
    def _():
        acc[...] = part

    @pl.when(jnp.logical_and(s > 0, s < slots - 1))
    def _():
        acc[...] += part

    @pl.when(s == slots - 1)
    def _():
        out[...] = (acc[...] + part).astype(out.dtype)


def mm_nt(name, g, x, pieces, width, col):
    m = x.shape[0]
    slots, rows, _ = pieces[0].shape
    d = rows * GROUPS
    ins = [((m, width), lambda s, g: (0, s))]
    ins += [((None, rows, width), lambda s, g: (s, 0, col))] * GROUPS
    outs = [((m, d), BF16, (m, d), lambda s, g: (0, 0))]
    return call(
        functools.partial(nt_kernel, slots), name, (slots,), ins, outs, [g, x, *pieces],
        scratch=[pltpu.VMEM((m, d), F32), pltpu.VMEM((d, width), BF16)],
        flops=2 * m * d * slots * width,
    )[0]


def tn_kernel(g_ref, x_ref, y_ref, *refs):
    outs, buffer = refs[:GROUPS], refs[GROUPS]
    rows = outs[0].shape[-2]
    g = g_ref[0]
    buffer[...] = lax.dot_general(
        x_ref[...], y_ref[...], (((0,), (0,)), ((), ())), preferred_element_type=F32
    ).astype(BF16)
    for j, out in enumerate(outs):
        out[...] = buffer[pl.ds(pl.multiple_of((g ^ j) * rows, rows), rows), :]


def mm_tn(name, g, x, y, slots):
    m, d = x.shape
    width = y.shape[1] // slots
    rows = d // GROUPS
    ins = [((m, d), lambda s, g: (0, 0)), ((m, width), lambda s, g: (0, s))]
    outs = [((slots, rows, width), BF16, (None, rows, width), lambda s, g: (s, 0, 0))] * GROUPS
    return call(
        tn_kernel, name, (slots,), ins, outs, [g, x, y],
        scratch=[pltpu.VMEM((d, width), BF16)],
        flops=2 * m * d * slots * width,
    )


def scores_of(keys, queries, causal, valid):
    scores = lax.dot_general(keys, queries, (((1,), (1,)), ((), ())), preferred_element_type=F32)
    if causal:
        key_at = lax.broadcasted_iota(jnp.int32, scores.shape, 0)
        query_at = lax.broadcasted_iota(jnp.int32, scores.shape, 1)
        scores = jnp.where(key_at <= query_at, scores, MASKED)
    if valid < scores.shape[0]:
        key_at = lax.broadcasted_iota(jnp.int32, scores.shape, 0)
        scores = jnp.where(key_at < valid, scores, -jnp.inf)
    return scores


def head_mask(shape, h):
    lane = lax.broadcasted_iota(jnp.int32, shape, 1)
    return (lane // HEAD_DIM) == h


def attend_kernel(causal, blocks, valid, shared, *refs):
    if shared:
        qkv_ref, out_ref, log_ref, score_buf = refs
        q_all = qkv_ref[:, :PAIR]
    else:
        q_ref, kv_ref, out_ref, log_ref, score_buf = refs
        q_all = q_ref[...]
    h = pl.program_id(1)
    chosen = head_mask(q_all.shape, h)
    queries = jnp.where(chosen, q_all.astype(F32) * (HEAD_DIM**-0.5), 0.0).astype(BF16)
    size = score_buf.shape[0] // blocks

    def keys_at(i):
        at = pl.ds(pl.multiple_of(i * size, size), size)
        return (qkv_ref[at, PAIR : 2 * PAIR] if shared else kv_ref[at, :PAIR]), (
            qkv_ref[at, 2 * PAIR :] if shared else kv_ref[at, PAIR:]
        )

    top = None
    for i in range(blocks):
        scores = scores_of(keys_at(i)[0], queries, causal, valid)
        score_buf[i * size : (i + 1) * size, :] = scores
        now = jnp.max(scores, axis=0, keepdims=True)
        top = now if top is None else jnp.maximum(top, now)
    total = jnp.zeros_like(top)
    mixed = None
    for i in range(blocks):
        raised = jnp.exp(score_buf[i * size : (i + 1) * size, :] - top)
        total += jnp.sum(raised, axis=0, keepdims=True)
        part = lax.dot_general(
            keys_at(i)[1], raised.astype(BF16), (((0,), (0,)), ((), ())), preferred_element_type=F32
        )
        mixed = part if mixed is None else mixed + part
    log_ref[...] = jnp.broadcast_to(top + jnp.log(total), log_ref.shape)
    mixed = jnp.transpose(mixed / total).astype(BF16)

    @pl.when(h == 0)
    def _():
        out_ref[...] = mixed

    @pl.when(h == 1)
    def _():
        out_ref[...] = jnp.where(chosen, mixed, out_ref[...])


def attend(name, q, kv, causal, blocks, valid):
    shared = kv is None
    m = q.shape[0]
    slots = q.shape[1] // (3 * PAIR if shared else PAIR)
    n = m if shared else kv.shape[0]
    ins = [((m, (3 if shared else 1) * PAIR), lambda s, h: (0, s))]
    args = [q]
    if not shared:
        ins.append(((n, 2 * PAIR), lambda s, h: (0, s)))
        args.append(kv)
    outs = [
        ((m, slots * PAIR), BF16, (m, PAIR), lambda s, h: (0, s)),
        ((slots * 2, 8, m), F32, (None, 8, m), lambda s, h: (s * 2 + h, 0, 0)),
    ]
    return call(
        functools.partial(attend_kernel, causal, blocks, valid, shared), name, (slots, 2), ins, outs, args,
        scratch=[pltpu.VMEM((n, m), F32)],
        flops=4 * m * n * HEAD_DIM * 2 * slots, scalars=0,
    )


def attend_back_kernel(causal, blocks, valid, shared, *refs):
    if shared:
        qkv_ref, up_ref, log_ref, out_ref, sums_ref, chance_buf, grad_buf = refs
        q_all = qkv_ref[:, :PAIR]
    else:
        q_ref, kv_ref, up_ref, log_ref, out_q, out_ref, sums_ref, chance_buf, grad_buf = refs
        q_all = q_ref[...]
    h = pl.program_id(1)
    chosen = head_mask(q_all.shape, h)
    queries = jnp.where(chosen, q_all.astype(F32) * (HEAD_DIM**-0.5), 0.0).astype(BF16)
    upstream = jnp.where(chosen, up_ref[...].astype(F32), 0.0).astype(BF16)
    log_total = log_ref[0:1, :]
    size = chance_buf.shape[0] // blocks

    def keys_at(i):
        at = slice(i * size, (i + 1) * size)
        return (qkv_ref[at, PAIR : 2 * PAIR] if shared else kv_ref[at, :PAIR]), (
            qkv_ref[at, 2 * PAIR :] if shared else kv_ref[at, PAIR:]
        )

    def put(at, columns, value):
        keep = head_mask(value.shape, h)

        @pl.when(h == 0)
        def _():
            out_ref[at, columns] = value.astype(BF16)

        @pl.when(h == 1)
        def _():
            out_ref[at, columns] = jnp.where(keep, value.astype(BF16), out_ref[at, columns])

    first = PAIR if shared else 0
    inner = None
    value_sum = None
    for i in range(blocks):
        at = slice(i * size, (i + 1) * size)
        keys, values = keys_at(i)
        chance = jnp.exp(scores_of(keys, queries, causal, valid) - log_total)
        grad = lax.dot_general(values, upstream, (((1,), (1,)), ((), ())), preferred_element_type=F32)
        chance_buf[at, :] = chance
        grad_buf[at, :] = grad
        now = jnp.sum(chance * grad, axis=0, keepdims=True)
        inner = now if inner is None else inner + now
        value_grad = jnp.dot(chance.astype(BF16), upstream, preferred_element_type=F32)
        now = jnp.sum(value_grad, axis=0, keepdims=True)
        value_sum = now if value_sum is None else value_sum + now
        put(at, slice(first + PAIR, first + 2 * PAIR), value_grad)
    query_grad = None
    for i in range(blocks):
        at = slice(i * size, (i + 1) * size)
        keys, values = keys_at(i)
        score_grad = (chance_buf[at, :] * (grad_buf[at, :] - inner)).astype(BF16)
        put(at, slice(first, first + PAIR), jnp.dot(score_grad, queries, preferred_element_type=F32))
        part = lax.dot_general(keys, score_grad, (((0,), (0,)), ((), ())), preferred_element_type=F32)
        query_grad = part if query_grad is None else query_grad + part
    query_grad = jnp.transpose(query_grad) * (HEAD_DIM**-0.5)
    query_sum = jnp.sum(query_grad, axis=0, keepdims=True)
    row = lax.broadcasted_iota(jnp.int32, (8, PAIR), 0)
    sums = jnp.where(row == 0, query_sum, jnp.where(row == 1, value_sum, 0.0))
    target = out_ref if shared else out_q
    keep = head_mask(query_grad.shape, h)

    @pl.when(h == 0)
    def _():
        target[:, :PAIR] = query_grad.astype(BF16)
        sums_ref[...] = sums

    @pl.when(h == 1)
    def _():
        target[:, :PAIR] = jnp.where(keep, query_grad.astype(BF16), target[:, :PAIR])
        sums_ref[...] = jnp.where(head_mask(sums.shape, h), sums, sums_ref[...])


def attend_back(name, q, kv, upstream, logs, causal, blocks, valid):
    shared = kv is None
    m = q.shape[0]
    slots = upstream.shape[1] // PAIR
    n = m if shared else kv.shape[0]
    ins = [((m, (3 if shared else 1) * PAIR), lambda s, h: (0, s))]
    args = [q]
    outs = []
    if not shared:
        ins.append(((n, 2 * PAIR), lambda s, h: (0, s)))
        args.append(kv)
        outs.append(((m, slots * PAIR), BF16, (m, PAIR), lambda s, h: (0, s)))
    ins.append(((m, PAIR), lambda s, h: (0, s)))
    ins.append(((None, 8, m), lambda s, h: (s * 2 + h, 0, 0)))
    args += [upstream, logs]
    wide = (3 if shared else 2) * PAIR
    outs.append(((n, slots * wide), BF16, (n, wide), lambda s, h: (0, s)))
    outs.append(((slots, 8, PAIR), F32, (None, 8, PAIR), lambda s, h: (s, 0, 0)))
    return call(
        functools.partial(attend_back_kernel, causal, blocks, valid, shared), name, (slots, 2), ins, outs, args,
        scratch=[pltpu.VMEM((n, m), F32), pltpu.VMEM((n, m), F32)],
        flops=10 * m * n * HEAD_DIM * 2 * slots, scalars=0,
    )


def row_blocks(m):
    for count in (4, 2):
        if m % (16 * count) == 0:
            return count
    return 1


def normal(values):
    centre = values - jnp.mean(values, axis=-1, keepdims=True)
    inverse = lax.rsqrt(jnp.mean(centre * centre, axis=-1, keepdims=True) + EPSILON)
    return centre * inverse, inverse


def norm_kernel(parts, normed, *refs):
    base, rest = refs[0], refs[1:]
    value = base[...].astype(F32)
    if parts:
        own, came, bias = rest[:3]
        rest = rest[3:]
        value = value + (own[...].astype(F32) + came[...].astype(F32)) + bias[...]
    if normed:
        gain, shift = rest[:2]
        rest = rest[2:]
        rest[-1][...] = (normal(value)[0] * gain[...] + shift[...]).astype(BF16)
    if parts:
        rest[0][...] = value.astype(rest[0].dtype)


def norm_forward(name, base, own=None, came=None, bias=None, gain=None, shift=None, kept=F32):
    m, d = base.shape
    count = row_blocks(m)
    block = ((m // count, d), lambda i: (i, 0))
    line = ((1, d), lambda i: (0, 0))
    ins, args, outs = [block], [base], []
    if own is not None:
        ins += [block, block, line]
        args += [own, came, bias]
        outs.append(((m, d), kept, *block))
    if gain is not None:
        ins += [line, line]
        args += [gain, shift]
        outs.append(((m, d), BF16, *block))
    return call(
        functools.partial(norm_kernel, own is not None, gain is not None), name, (count,), ins, outs, args,
        flops=20 * m * d, scalars=0,
    )


def norm_back_kernel(want_low, own, came, values, gain, upstream, *outs):
    grad_ref, sums = outs[0], outs[-1]
    q = own[...].astype(F32) + came[...].astype(F32)
    n, inverse = normal(values[...].astype(F32))
    up = upstream[...].astype(F32)
    g = q * gain[...]
    back = inverse * (g - jnp.mean(g, axis=-1, keepdims=True) - n * jnp.mean(g * n, axis=-1, keepdims=True))
    grad = up + back
    grad_ref[...] = grad.astype(grad_ref.dtype)
    if want_low:
        outs[1][...] = grad.astype(BF16)
    row = lax.broadcasted_iota(jnp.int32, sums.shape, 0)
    now = jnp.zeros(sums.shape, F32)
    for at, term in enumerate((q * n, q, grad, up)):
        now = jnp.where(row == at, jnp.sum(term, axis=0, keepdims=True), now)

    @pl.when(pl.program_id(0) == 0)
    def _():
        sums[...] = now

    @pl.when(pl.program_id(0) > 0)
    def _():
        sums[...] += now


def norm_back(name, own, came, values, gain, upstream, want_low):
    m, d = values.shape
    count = row_blocks(m)
    block = ((m // count, d), lambda i: (i, 0))
    line = ((1, d), lambda i: (0, 0))
    outs = [((m, d), F32 if want_low else BF16, *block)]
    if want_low:
        outs.append(((m, d), BF16, *block))
    outs.append(((8, d), F32, (8, d), lambda i: (0, 0)))
    return call(
        functools.partial(norm_back_kernel, want_low), name, (count,), [block, block, block, line, block], outs,
        [own, came, values, gain, upstream], flops=30 * m * d, scalars=0,
    )


def flip(x, bit, size):
    return lax.ppermute(x, "fsdp", [(i, i ^ (1 << bit)) for i in range(size)])


def turn(x, step, size):
    return lax.ppermute(x, "tensor", [(i, (i + step) % size) for i in range(size)])


def half(x, index, axis):
    size = x.shape[axis] // 2
    return lax.dynamic_slice_in_dim(x, index * size, size, axis=axis)


def on_device(
    n_f, n_t,
    tokens, encoder, cotangent, self_weights, self_biases, self_output, cross_query, cross_memory,
    cross_biases, cross_output, hidden_weight, hidden_bias, reduce_weight, norm_gains, norm_shifts, branch_biases,
):
    bits = n_f.bit_length() - 1
    f = lax.axis_index("fsdp")
    z = lax.axis_index("tensor")
    core = f % 2
    group = f >> (bits - 2)
    g = group.astype(jnp.int32).reshape(1)
    length, d = tokens.shape[1], tokens.shape[2]
    frames = encoder.shape[1]
    own_clips = tokens.shape[0]
    assert own_clips * 2 == n_t and bits >= 3

    per = d // n_f
    units = hidden_bias.shape[1] * n_f
    heads_wide = self_biases.shape[2] * n_f

    def spread_features(v):
        wide = jnp.zeros((v.shape[0], d), BF16)
        return lax.dynamic_update_slice(wide, v, (0, f * per))

    def spread_units(v, total):
        v = v.reshape(v.shape[0], 1, -1)
        wide = jnp.zeros((v.shape[0], n_t, total), BF16)
        return lax.dynamic_update_slice(wide, v, (0, z, f * v.shape[2]))

    first = jnp.where(z == 0, 1, 0).astype(BF16)
    feature_rows = spread_features(jnp.concatenate([norm_gains, norm_shifts, branch_biases])) * first
    unit_rows = [
        spread_units(hidden_bias, units),
        spread_units(self_biases.reshape(2, -1), heads_wide),
        spread_units(cross_biases.reshape(2, -1), heads_wide),
    ]
    packed = jnp.concatenate([feature_rows.reshape(-1)] + [u.reshape(-1) for u in unit_rows]).reshape(-1, 1024)
    for bit in range(bits):
        packed = packed + flip(packed, bit, n_f)
    for step in (1, 2):
        packed = packed + lax.ppermute(packed, "tensor", [(i, i ^ step) for i in range(n_t)])
    packed = packed.reshape(-1).astype(F32)
    feature_all = packed[: 9 * d].reshape(9, d)
    at = 9 * d
    hidden_all = packed[at : at + n_t * units].reshape(1, n_t, units)
    at += n_t * units
    self_all = packed[at : at + 2 * n_t * heads_wide].reshape(2, n_t, heads_wide)
    at += 2 * n_t * heads_wide
    cross_all = packed[at : at + 2 * n_t * heads_wide].reshape(2, n_t, heads_wide)
    gains, shifts, branch = feature_all[0:3], feature_all[3:6], feature_all[6:9]

    def to_slots(v):
        mine = half(v, core, 2)
        return jnp.stack(
            [lax.dynamic_index_in_dim(mine, (z - s) % n_t, axis=1, keepdims=False) for s in range(n_t)]
        )

    hidden_slots = to_slots(hidden_all)
    self_slots = to_slots(self_all)
    cross_slots = to_slots(cross_all)
    zero_slots = jnp.zeros_like(self_slots[:, :1])
    qkv_bias = jnp.concatenate([self_slots[:, :1], zero_slots, self_slots[:, 1:]], axis=2)
    cq_bias = cross_slots[:, :1]
    ckv_bias = jnp.concatenate([zero_slots, cross_slots[:, 1:]], axis=2)

    mine = core == z // own_clips

    def take_clip(x):
        x = lax.dynamic_index_in_dim(x, z % own_clips, axis=0, keepdims=False)
        return jnp.where(mine, x, flip(x, 0, n_f))

    part_frames = frames // n_t
    part_pad = -(-part_frames // 128) * 128
    start = take_clip(tokens)
    upstream_low = take_clip(cotangent)
    memory = jnp.pad(
        take_clip(encoder).reshape(n_t, part_frames, d), ((0, 0), (0, part_pad - part_frames), (0, 0))
    ).reshape(n_t * part_pad, d)

    def gather(weights, through):
        keep = jnp.concatenate([half(w, core, 1) for w in weights], axis=1)
        send = jnp.concatenate([half(w, 1 - core, 1) for w in weights], axis=1)
        came = flip(send, 0, n_f)
        now = jnp.where(core == 0, jnp.concatenate([keep, came]), jnp.concatenate([came, keep]))
        for bit in range(1, bits - 2):
            came = flip(now, bit, n_f)
            low = (f >> bit) % 2 == 0
            now = jnp.where(low, jnp.concatenate([now, came]), jnp.concatenate([came, now]))
        slots = [now]
        for _ in range(n_t - 1):
            slots.append(turn(slots[-1], 1, n_t))
        zero = jnp.stack(slots)
        one = flip(zero, bits - 2, n_f)
        two = flip(zero, bits - 1, n_f)
        three = flip(one, bits - 1, n_f) if through == 1 else flip(two, bits - 2, n_f)
        return (zero, one, two, three)

    w_qkv = gather([self_weights[0], self_weights[1], self_weights[2]], 1)
    w_mid = gather([self_output.T, cross_query], 2)
    w_cross = gather([cross_memory[0], cross_memory[1], cross_output.T], 2)
    w_hidden = gather([hidden_weight], 1)
    w_reduce = gather([reduce_weight.T], 2)

    def scatter(pieces, through):
        zero, one, two, three = pieces

        def slot_sum(a, b):
            return (a.astype(F32) + b.astype(F32)).astype(BF16)

        if through == 1:
            two, three = flip(two, bits - 1, n_f), flip(three, bits - 1, n_f)
            zero, one = slot_sum(zero, two), slot_sum(one, three)
            other = flip(one, bits - 2, n_f)
        else:
            one, three = flip(one, bits - 2, n_f), flip(three, bits - 2, n_f)
            zero, two = slot_sum(zero, one), slot_sum(two, three)
            other = flip(two, bits - 1, n_f)
        slots = [slot_sum(zero[s], other[s]) for s in range(n_t)]
        now = slots[-1]
        for s in range(n_t - 2, -1, -1):
            now = turn(now, -1, n_t)
            now = slots[s].astype(F32) + now.astype(F32)
            if s:
                now = now.astype(BF16)
        for bit in range(bits - 3, 0, -1):
            up = (f >> bit) % 2
            keep, send = half(now, up, 0), half(now, 1 - up, 0)
            now = keep + flip(send.astype(BF16), bit, n_f).astype(F32)
        keep, send = half(now, core, 0), half(now, 1 - core, 0)
        came = flip(send, 0, n_f)
        return keep, came

    def unpack(shares, widths):
        keep, came = shares
        result, at = [], 0
        for width in widths:
            a, b = keep[:, at : at + width], came[:, at : at + width]
            result.append(jnp.where(core == 0, jnp.concatenate([a, b], 1), jnp.concatenate([b, a], 1)))
            at += width
        return result

    line = lambda rows, at: rows[at : at + 1]
    (normed_one,) = norm_forward("norm_one", start, gain=line(gains, 0), shift=line(shifts, 0))
    (qkv,) = mm_nn("qkv", g, normed_one, w_qkv, 3 * PAIR, 0, "bias", bias=qkv_bias)
    mixed_one, log_one = attend("self_attention", qkv, None, True, 1, length)
    part = mm_nt("self_out", g, mixed_one, w_mid, PAIR, 0)
    (cross_kv,) = mm_nn("cross_kv", g, memory, w_cross, 2 * PAIR, 0, "bias", bias=ckv_bias)
    middle, normed_two = norm_forward(
        "norm_two", start, part, flip(part, 0, n_f), line(branch, 0), line(gains, 1), line(shifts, 1)
    )
    (cross_q,) = mm_nn("cross_q", g, normed_two, w_mid, PAIR, 1, "bias", bias=cq_bias)
    mixed_two, log_two = attend("cross_attention", cross_q, cross_kv, False, n_t, part_frames)
    part = mm_nt("cross_out", g, mixed_two, w_cross, PAIR, 2)
    later, normed_three = norm_forward(
        "norm_three", middle, part, flip(part, 0, n_f), line(branch, 1), line(gains, 2), line(shifts, 2)
    )
    activated, slope = mm_nn("hidden", g, normed_three, w_hidden, units // 2, 0, "gelu", bias=hidden_slots)
    part = mm_nt("reduce", g, activated, w_reduce, units // 2, 0)
    (output,) = norm_forward("output", later, part, flip(part, 0, n_f), line(branch, 2), kept=BF16)

    g_reduce = mm_tn("reduce_grad", g, upstream_low, activated, n_t)
    expanded_low, hidden_sums = mm_nn("expanded_grad", g, upstream_low, w_reduce, units // 2, 0, "slope", slope=slope)
    part = mm_nt("normed_three_grad", g, expanded_low, w_hidden, units // 2, 0)
    g_hidden = mm_tn("hidden_grad", g, normed_three, expanded_low, n_t)
    later_grad, later_low, sums_three = norm_back(
        "norm_three_back", part, flip(part, 0, n_f), later, line(gains, 2), upstream_low, True
    )
    (mixed_two_grad,) = mm_nn("mixed_two_grad", g, later_low, w_cross, PAIR, 2)
    cq_low, ckv_low, cross_sums = attend_back(
        "cross_attention_back", cross_q, cross_kv, mixed_two_grad, log_two, False, n_t, part_frames
    )
    part = mm_nt("normed_two_grad", g, cq_low, w_mid, PAIR, 1)
    g_cross_out = mm_tn("cross_out_grad", g, later_low, mixed_two, n_t)
    g_cross_q = mm_tn("cross_q_grad", g, normed_two, cq_low, n_t)
    g_cross_kv = mm_tn("cross_kv_grad", g, memory, ckv_low, n_t)
    memory_part = mm_nt("memory_grad", g, ckv_low, w_cross, 2 * PAIR, 0)
    middle_grad, middle_low, sums_two = norm_back(
        "norm_two_back", part, flip(part, 0, n_f), middle, line(gains, 1), later_grad, True
    )
    (mixed_one_grad,) = mm_nn("mixed_one_grad", g, middle_low, w_mid, PAIR, 0)
    qkv_low, self_sums = attend_back("self_attention_back", qkv, None, mixed_one_grad, log_one, True, 1, length)
    part = mm_nt("normed_one_grad", g, qkv_low, w_qkv, 3 * PAIR, 0)
    g_self_out = mm_tn("self_out_grad", g, middle_low, mixed_one, n_t)
    g_qkv = mm_tn("qkv_grad", g, normed_one, qkv_low, n_t)
    start_grad, sums_one = norm_back(
        "norm_one_back", part, flip(part, 0, n_f), start, line(gains, 0), middle_grad, False
    )

    (reduce_t,) = unpack(scatter(g_reduce, 1), [units // 2])
    (hidden_share,) = unpack(scatter(g_hidden, 2), [units // 2])
    (cross_out_t,) = unpack(scatter(g_cross_out, 1), [PAIR])
    (cross_q_share,) = unpack(scatter(g_cross_q, 2), [PAIR])
    ck_share, cv_share = unpack(scatter(g_cross_kv, 1), [PAIR, PAIR])
    (self_out_t,) = unpack(scatter(g_self_out, 2), [PAIR])
    q_share, k_share, v_share = unpack(scatter(g_qkv, 2), [PAIR, PAIR, PAIR])

    lead = jnp.where(core == 0, 1.0, 0.0).astype(F32)
    feature_sums = jnp.stack(
        [sums_one[0], sums_two[0], sums_three[0], sums_one[1], sums_two[1], sums_three[1],
         sums_two[2], sums_three[2], sums_three[3]]
    ) * lead

    def from_slots(v):
        natural = jnp.stack(
            [lax.dynamic_index_in_dim(v, (z - at) % n_t, axis=0, keepdims=False) for at in range(n_t)], axis=1
        )
        wide = jnp.zeros((*natural.shape[:2], 2 * natural.shape[2]), F32)
        return lax.dynamic_update_slice(wide, natural, (0, 0, core * natural.shape[2]))

    unit_sums = [from_slots(hidden_sums[:, :1]), from_slots(self_sums[:, :2]), from_slots(cross_sums[:, :2])]
    packed = jnp.concatenate([feature_sums.reshape(-1)] + [u.reshape(-1) for u in unit_sums]).reshape(-1, 1024)
    for bit in range(bits):
        packed = packed + flip(packed, bit, n_f)
    for step in (1, 2):
        packed = packed + lax.ppermute(packed, "tensor", [(i, i ^ step) for i in range(n_t)])
    packed = packed.reshape(-1)
    feature_share = lax.dynamic_slice(packed[: 9 * d].reshape(9, d), (0, f * per), (9, per))

    def unit_share(at, rows, total):
        block = packed[at : at + rows * n_t * total].reshape(rows, n_t, total)
        return lax.dynamic_slice(block, (0, z, f * (total // n_f)), (rows, 1, total // n_f))

    at = 9 * d
    hidden_bias_share = unit_share(at, 1, units)[0]
    at += n_t * units
    self_bias_share = unit_share(at, 2, heads_wide)
    at += 2 * n_t * heads_wide
    cross_bias_share = unit_share(at, 2, heads_wide)

    def spread_clip(x):
        slots = [half(x, core, 0)]
        for _ in range(n_t - 1):
            slots.append(turn(slots[-1], 1, n_t))
        stacked = jnp.stack(slots)

        def clips(c):
            return jnp.stack(
                [
                    lax.dynamic_index_in_dim(stacked, (z - c * own_clips - i) % n_t, axis=0, keepdims=False)
                    for i in range(own_clips)
                ]
            )

        keep, came = clips(core), flip(clips(1 - core), 0, n_f)
        return jnp.where(core == 0, jnp.concatenate([keep, came], 1), jnp.concatenate([came, keep], 1))

    keep, send = half(memory_part, core, 1), half(memory_part, 1 - core, 1)
    summed = (keep.astype(F32) + flip(send, 0, n_f).astype(F32)).astype(BF16)
    summed = summed.reshape(n_t, part_pad, d // 2)
    slots = []
    for s in range(n_t):
        block = lax.dynamic_index_in_dim(summed, (z + s) % n_t, axis=0, keepdims=False)
        slots.append(turn(block, s, n_t) if s else block)
    stacked = jnp.stack(slots)

    def memory_clips(c):
        return jnp.stack(
            [
                lax.dynamic_index_in_dim(stacked, (z - c * own_clips - i) % n_t, axis=0, keepdims=False)
                for i in range(own_clips)
            ]
        )

    keep, came = memory_clips(core), flip(memory_clips(1 - core), 0, n_f)
    memory_share = jnp.where(core == 0, jnp.concatenate([keep, came], 2), jnp.concatenate([came, keep], 2))

    return (
        spread_clip(output),
        spread_clip(start_grad),
        memory_share[:, :part_frames],
        jnp.stack([q_share, k_share, v_share]),
        self_bias_share,
        self_out_t.T,
        cross_q_share,
        jnp.stack([ck_share, cv_share]),
        cross_bias_share,
        cross_out_t.T,
        hidden_share,
        hidden_bias_share,
        reduce_t.T,
        feature_share[0:3],
        feature_share[3:6],
        feature_share[6:9],
    )


def solution(mesh):
    n_f, n_t = mesh.shape["fsdp"], mesh.shape["tensor"]
    clips = P("fsdp", None, None)
    stacked = P(None, "fsdp", "tensor")
    biases = P(None, "tensor", "fsdp")
    up, down, rows = P("fsdp", "tensor"), P("tensor", "fsdp"), P(None, "fsdp")
    return jax.shard_map(
        functools.partial(on_device, n_f, n_t),
        mesh=mesh,
        in_specs=(
            clips, clips, clips, stacked, biases, down, up, stacked, biases, down, up, down, down, rows, rows, rows,
        ),
        out_specs=(
            clips, clips, P("fsdp", "tensor", None), stacked, biases, down, up, stacked, biases, down, up, down,
            down, rows, rows, rows,
        ),
        check_vma=False,
    )
```

```python
import functools
import math

import jax
import jax.numpy as jnp
from jax import lax
from jax.experimental import pallas as pl
from jax.experimental.pallas import tpu as pltpu
from jax.sharding import PartitionSpec as P

HEAD_DIM = 64
PAIR = 2 * HEAD_DIM
GROUPS = 4
EPSILON = 1e-05
MASKED = -1e9
SCALE = HEAD_DIM**-0.5
F32 = jnp.float32
BF16 = jnp.bfloat16
VMEM_LIMIT = 63 * 1024 * 1024
NT = (((1,), (1,)), ((), ()))
TN = (((0,), (0,)), ((), ()))


def call(kernel, name, outs, args, scratch=(), flops=0, grid=(1,), specs=None, out_specs=None):
    def whole(shape):
        return pl.BlockSpec(shape, lambda *_: (0,) * len(shape))

    in_specs = [whole(a.shape) for a in args[1:]] if specs is None else specs(whole)
    out_shape = [jax.ShapeDtypeStruct(shape, dtype) for shape, dtype in outs]
    moved = sum(a.size * a.dtype.itemsize for a in args) + sum(
        math.prod(o.shape) * jnp.dtype(o.dtype).itemsize for o in out_shape
    )
    return pl.pallas_call(
        kernel,
        name=name,
        out_shape=out_shape,
        grid_spec=pltpu.PrefetchScalarGridSpec(
            num_scalar_prefetch=1,
            grid=grid,
            in_specs=in_specs,
            out_specs=[whole(o.shape) for o in out_shape] if out_specs is None else out_specs(whole),
            scratch_shapes=list(scratch),
        ),
        compiler_params=pltpu.CompilerParams(vmem_limit_bytes=VMEM_LIMIT),
        cost_estimate=pl.CostEstimate(flops=int(flops), bytes_accessed=int(moved), transcendentals=0),
    )(*args)


def dot(a, b, dims=None):
    if dims is None:
        return jnp.dot(a, b, preferred_element_type=F32)
    return lax.dot_general(a, b, dims, preferred_element_type=F32)


def part_rows(g, j, rows):
    return pl.ds(pl.multiple_of((g ^ j) * rows, rows), rows)


def fill(g, halves, buffer, columns):
    rows = buffer.shape[0] // GROUPS
    for at_half, pieces in enumerate(halves):
        for j, piece in enumerate(pieces):
            to = part_rows(g, j, rows)
            for i in range(2):
                s = 2 * at_half + i
                for which, at in columns:
                    buffer[to, at + s * PAIR : at + (s + 1) * PAIR] = piece[
                        i, :rows, which * PAIR : (which + 1) * PAIR
                    ]


def unfill(g, halves, buffer, columns):
    rows = buffer.shape[0] // GROUPS
    for at_half, pieces in enumerate(halves):
        for j, piece in enumerate(pieces):
            to = part_rows(g, j, rows)
            for i in range(2):
                s = 2 * at_half + i
                for which, at in columns:
                    piece[i, :, which * PAIR : (which + 1) * PAIR] = buffer[
                        to, at + s * PAIR : at + (s + 1) * PAIR
                    ]


def row_step(m):
    return m // 4 if m % 64 == 0 else m


def over_rows(m, body):
    step = row_step(m)

    def run(i, carry):
        return body(pl.ds(pl.multiple_of(i * step, step), step), carry)

    return lambda carry: lax.fori_loop(0, m // step, run, carry)


def normal(values):
    centre = values - jnp.mean(values, axis=-1, keepdims=True)
    inverse = lax.rsqrt(jnp.mean(centre * centre, axis=-1, keepdims=True) + EPSILON)
    return centre * inverse, inverse


def norm_rows(value_at, gain, shift, normed, kept=None):
    gain_row, shift_row = gain[...], shift[...]

    def body(at, carry):
        value = value_at(at)
        if kept is not None:
            kept[at, :] = value
        normed[at, :] = (normal(value)[0] * gain_row + shift_row).astype(BF16)
        return carry

    over_rows(normed.shape[0], body)(0)


def norm_back_rows(own, came, values, gain, upstream, grad_ref, low_ref, sums):
    gain_row = gain[...]
    wide = values.shape[1]

    def body(at, carry):
        q = own[at, :].astype(F32) + came[at, :].astype(F32)
        n, inverse = normal(values[at, :].astype(F32))
        up = upstream[at, :].astype(F32)
        v = q * gain_row
        back = inverse * (v - jnp.mean(v, axis=-1, keepdims=True) - n * jnp.mean(v * n, axis=-1, keepdims=True))
        grad = up + back
        grad_ref[at, :] = grad.astype(grad_ref.dtype)
        if low_ref is not None:
            low_ref[at, :] = grad.astype(BF16)
        terms = (q * n, q, grad, up)
        return tuple(c + jnp.sum(t, axis=0, keepdims=True) for c, t in zip(carry, terms))

    totals = over_rows(values.shape[0], body)(tuple(jnp.zeros((1, wide), F32) for _ in range(4)))
    row = lax.broadcasted_iota(jnp.int32, sums.shape, 0)
    value = jnp.zeros(sums.shape, F32)
    for at, total in enumerate(totals):
        value = jnp.where(row == at, total, value)
    sums[...] = value


def lane_mask(shape, h):
    return (lax.broadcasted_iota(jnp.int32, shape, 1) // HEAD_DIM) == h


def mask_scores(scores, causal, valid):
    size = scores.shape[0]
    if causal:
        key_at = lax.broadcasted_iota(jnp.int32, scores.shape, 0)
        query_at = lax.broadcasted_iota(jnp.int32, scores.shape, 1)
        return jnp.where(key_at <= query_at, scores, MASKED)
    if valid < size:
        edge = valid // 8 * 8
        tail = scores[edge:, :]
        key_at = lax.broadcasted_iota(jnp.int32, tail.shape, 0) + edge
        return jnp.concatenate([scores[:edge, :], jnp.where(key_at < valid, tail, -jnp.inf)], axis=0)
    return scores


def attend(q_ref, k_ref, v_ref, mixed_ref, log_ref, score_buf, causal, blocks, valid):
    size = k_ref.shape[0] // blocks
    pairs = q_ref.shape[1] // PAIR

    def one_pair(p, carry):
        at = pl.ds(pl.multiple_of(p * PAIR, PAIR), PAIR)
        q_all = q_ref[:, at].astype(F32) * SCALE
        result = None
        for h in range(2):
            queries = jnp.where(lane_mask(q_all.shape, h), q_all, 0.0).astype(BF16)
            top = None
            for i in range(blocks):
                rows = slice(i * size, (i + 1) * size)
                scores = mask_scores(dot(k_ref[rows, at], queries, NT), causal, valid)
                score_buf[rows, :] = scores
                now = jnp.max(scores, axis=0, keepdims=True)
                top = now if top is None else jnp.maximum(top, now)
            total, mixed = None, None
            for i in range(blocks):
                rows = slice(i * size, (i + 1) * size)
                raised = jnp.exp(score_buf[rows, :] - top)
                now = jnp.sum(raised, axis=0, keepdims=True)
                total = now if total is None else total + now
                now = dot(v_ref[rows, at], raised.astype(BF16), TN)
                mixed = now if mixed is None else mixed + now
            log_ref[2 * p + h] = jnp.broadcast_to(top + jnp.log(total), log_ref.shape[1:])
            mixed = mixed / total
            if result is None:
                result = mixed
            else:
                row = lax.broadcasted_iota(jnp.int32, mixed.shape, 0)
                result = jnp.where(row < HEAD_DIM, result, mixed)
        mixed_ref[:, at] = jnp.transpose(result).astype(BF16)
        return carry

    lax.fori_loop(0, pairs, one_pair, 0)


def attend_back(q_ref, k_ref, v_ref, up_ref, mixed_ref, log_ref, dq_ref, dk_ref, dv_ref, sums, causal, blocks, valid):
    size = k_ref.shape[0] // blocks
    pairs = q_ref.shape[1] // PAIR

    def one_pair(p, carry):
        at = pl.ds(pl.multiple_of(p * PAIR, PAIR), PAIR)
        q_all = q_ref[:, at].astype(F32) * SCALE
        up_all = up_ref[:, at].astype(F32)
        product = up_all * mixed_ref[:, at].astype(F32)
        queries, upstream, inner, logs = [], [], [], []
        for h in range(2):
            chosen = lane_mask(q_all.shape, h)
            queries.append(jnp.where(chosen, q_all, 0.0).astype(BF16))
            upstream.append(jnp.where(chosen, up_all, 0.0).astype(BF16))
            ones = jnp.where(lane_mask((8, PAIR), h), 1.0, 0.0)
            inner.append(
                lax.dot_general(ones, product, NT, precision=lax.Precision.HIGHEST, preferred_element_type=F32)[0:1, :]
            )
            logs.append(log_ref[2 * p + h][0:1, :])
        query_grads = [None, None]
        value_sum = None
        for i in range(blocks):
            rows = slice(i * size, (i + 1) * size)
            keys, values = k_ref[rows, at], v_ref[rows, at]
            key_grad, value_grad = None, None
            for h in range(2):
                chance = jnp.exp(mask_scores(dot(keys, queries[h], NT), causal, valid) - logs[h])
                now = dot(chance.astype(BF16), upstream[h])
                value_grad = now if value_grad is None else value_grad + now
                grad = dot(values, upstream[h], NT)
                score_grad = (chance * (grad - inner[h])).astype(BF16)
                now = dot(score_grad, queries[h])
                key_grad = now if key_grad is None else key_grad + now
                now = dot(keys, score_grad, TN)
                query_grads[h] = now if query_grads[h] is None else query_grads[h] + now
            dk_ref[rows, at] = key_grad.astype(BF16)
            dv_ref[rows, at] = value_grad.astype(BF16)
            now = jnp.sum(value_grad, axis=0, keepdims=True)
            value_sum = now if value_sum is None else value_sum + now
        row = lax.broadcasted_iota(jnp.int32, query_grads[0].shape, 0)
        query_grad = jnp.transpose(jnp.where(row < HEAD_DIM, query_grads[0], query_grads[1])) * SCALE
        dq_ref[:, at] = query_grad.astype(BF16)
        query_sum = jnp.sum(query_grad, axis=0, keepdims=True)
        row = lax.broadcasted_iota(jnp.int32, (8, PAIR), 0)
        sums[:, at] = jnp.where(row == 0, query_sum, jnp.where(row == 1, value_sum, 0.0))
        return carry

    lax.fori_loop(0, pairs, one_pair, 0)


def self_forward_kernel(g_ref, start, gain, shift, bias, *refs):
    halves, (normed, qkv, mixed, logs, part), (w_in, w_out, score_buf) = (refs[0:4], refs[4:8]), refs[8:13], refs[13:]
    g, wide = g_ref[0], mixed.shape[1]
    norm_rows(lambda at: start[at, :].astype(F32), gain, shift, normed)
    fill(g, halves, w_in, [(0, 0), (1, wide), (2, 2 * wide)])
    fill(g, halves, w_out, [(3, 0)])
    qkv[...] = (dot(normed[...], w_in[...]) + bias[...]).astype(BF16)
    q, k, v = (qkv.at[:, i * wide : (i + 1) * wide] for i in range(3))
    attend(q, k, v, mixed, logs, score_buf, True, 1, start.shape[0])
    part[...] = dot(mixed[...], w_out[...], NT).astype(BF16)


def self_forward(g, start, gain, shift, bias, weights):
    m, d = start.shape
    wide = bias.shape[1] // 3
    heads = wide // HEAD_DIM
    return call(
        self_forward_kernel, "self_forward",
        [((m, d), BF16), ((m, 3 * wide), BF16), ((m, wide), BF16), ((heads, 8, m), F32), ((m, d), BF16)],
        [g, start, gain, shift, bias, *weights[0], *weights[1]],
        scratch=[pltpu.VMEM((d, 3 * wide), BF16), pltpu.VMEM((d, wide), BF16), pltpu.VMEM((m, m), F32)],
        flops=2 * m * d * 4 * wide + 4 * m * m * wide * 2,
    )


def cross_kv_kernel(g_ref, memory, bias, *refs):
    halves, kv, w_in = (refs[0:4], refs[4:8]), refs[8], refs[9]
    wide = kv.shape[1] // 2

    @pl.when(pl.program_id(0) == 0)
    def _():
        fill(g_ref[0], halves, w_in, [(1, 0), (2, wide)])

    kv[...] = (dot(memory[...], w_in[...]) + bias[...]).astype(BF16)


def cross_kv(g, memory, bias, weights, blocks):
    n, d = memory.shape
    wide = bias.shape[1]
    block = pl.BlockSpec((n // blocks, d), lambda i, _: (i, 0))
    return call(
        cross_kv_kernel, "cross_kv", [((n, wide), BF16)], [g, memory, bias, *weights[0], *weights[1]],
        scratch=[pltpu.VMEM((d, wide), BF16)], flops=2 * n * d * wide, grid=(blocks,),
        specs=lambda whole: [block, whole(bias.shape)] + [whole(w.shape) for w in (*weights[0], *weights[1])],
        out_specs=lambda whole: [pl.BlockSpec((n // blocks, wide), lambda i, _: (i, 0))],
    )[0]


def cross_forward_kernel(blocks, valid, g_ref, start, own, came, branch, gain, shift, bias, kv, *refs):
    halves, (middle, normed, q, mixed, logs, part), (w_in, w_out, score_buf) = (
        (refs[0:4], refs[4:8]), refs[8:14], refs[14:],
    )
    g, wide = g_ref[0], mixed.shape[1]
    branch_row = branch[...]
    norm_rows(
        lambda at: start[at, :].astype(F32) + (own[at, :].astype(F32) + came[at, :].astype(F32)) + branch_row,
        gain, shift, normed, middle,
    )
    fill(g, halves, w_in, [(0, 0)])
    fill(g, halves, w_out, [(3, 0)])
    q[...] = (dot(normed[...], w_in[...]) + bias[...]).astype(BF16)
    attend(q, kv.at[:, :wide], kv.at[:, wide:], mixed, logs, score_buf, False, blocks, valid)
    part[...] = dot(mixed[...], w_out[...], NT).astype(BF16)


def cross_forward(g, start, own, came, branch, gain, shift, bias, kv, weights, blocks, valid):
    m, d = start.shape
    n, wide = kv.shape[0], bias.shape[1]
    heads = wide // HEAD_DIM
    return call(
        functools.partial(cross_forward_kernel, blocks, valid), "cross_forward",
        [((m, d), F32), ((m, d), BF16), ((m, wide), BF16), ((m, wide), BF16), ((heads, 8, m), F32), ((m, d), BF16)],
        [g, start, own, came, branch, gain, shift, bias, kv, *weights[0], *weights[1]],
        scratch=[pltpu.VMEM((d, wide), BF16), pltpu.VMEM((d, wide), BF16), pltpu.VMEM((n, m), F32)],
        flops=2 * m * d * 2 * wide + 4 * m * n * wide * 2,
    )


def feed_kernel(slots, g_ref, middle, own, came, branch, gain, shift, upstream, bias, *refs):
    hidden, reduce = refs[0:4], refs[4:8]
    later, out_part, grad_part, sums = refs[8:12]
    g_hidden, g_reduce = refs[12:16], refs[16:20]
    normed, w_hidden, w_reduce, out_acc, grad_acc, result = refs[20:]
    g, s = g_ref[0], pl.program_id(0)
    rows = w_hidden.shape[0] // GROUPS

    @pl.when(s == 0)
    def _():
        branch_row = branch[...]
        norm_rows(
            lambda at: middle[at, :] + (own[at, :].astype(F32) + came[at, :].astype(F32)) + branch_row,
            gain, shift, normed, later,
        )

    for j in range(GROUPS):
        to = part_rows(g, j, rows)
        w_hidden[to, :] = hidden[j][...]
        w_reduce[to, :] = reduce[j][...]
    expanded = dot(normed[...], w_hidden[...]) + bias[...]
    phi = 0.5 * (1.0 + lax.erf(expanded * (0.5**0.5)))
    activated = (expanded * phi).astype(BF16)
    density = jnp.exp(expanded * expanded * -0.5) * ((2.0 * math.pi) ** -0.5)
    slope = phi + expanded * density
    expanded_grad = dot(upstream[...], w_reduce[...]) * slope
    expanded_low = expanded_grad.astype(BF16)
    sums[...] = jnp.broadcast_to(jnp.sum(expanded_grad, axis=0, keepdims=True), sums.shape)
    out_now = dot(activated, w_reduce[...], NT)
    grad_now = dot(expanded_low, w_hidden[...], NT)

    @pl.when(s == 0)
    def _():
        out_acc[...] = out_now
        grad_acc[...] = grad_now

    @pl.when(jnp.logical_and(s > 0, s < slots - 1))
    def _():
        out_acc[...] += out_now
        grad_acc[...] += grad_now

    @pl.when(s == slots - 1)
    def _():
        out_part[...] = (out_acc[...] + out_now).astype(BF16)
        grad_part[...] = (grad_acc[...] + grad_now).astype(BF16)

    result[...] = dot(normed[...], expanded_low, TN).astype(BF16)
    for j in range(GROUPS):
        g_hidden[j][...] = result[part_rows(g, j, rows), :]
    result[...] = dot(upstream[...], activated, TN).astype(BF16)
    for j in range(GROUPS):
        g_reduce[j][...] = result[part_rows(g, j, rows), :]


def feed(g, middle, own, came, branch, gain, shift, upstream, bias, hidden, reduce):
    m, d = middle.shape
    slots, _, width = bias.shape
    rows = d // GROUPS
    piece = pl.BlockSpec((None, rows, width), lambda s, _: (s, 0, 0))
    args = [middle, own, came, branch, gain, shift, upstream]
    return call(
        functools.partial(feed_kernel, slots), "feed_forward_and_back",
        [((m, d), F32), ((m, d), BF16), ((m, d), BF16), ((slots, 8, width), F32)]
        + [((slots, rows, width), BF16)] * (2 * GROUPS),
        [g, *args, bias, *hidden, *reduce],
        scratch=[
            pltpu.VMEM((m, d), BF16), pltpu.VMEM((d, width), BF16), pltpu.VMEM((d, width), BF16),
            pltpu.VMEM((m, d), F32), pltpu.VMEM((m, d), F32), pltpu.VMEM((d, width), BF16),
        ],
        flops=12 * m * d * slots * width, grid=(slots,),
        specs=lambda whole: [whole(a.shape) for a in args]
        + [pl.BlockSpec((None, 1, width), lambda s, _: (s, 0, 0))] + [piece] * (2 * GROUPS),
        out_specs=lambda whole: [whole((m, d))] * 3
        + [pl.BlockSpec((None, 8, width), lambda s, _: (s, 0, 0))] + [piece] * (2 * GROUPS),
    )


def output_kernel(g_ref, later, own, came, branch, out):
    branch_row = branch[...]

    def body(at, carry):
        out[at, :] = (later[at, :] + (own[at, :].astype(F32) + came[at, :].astype(F32)) + branch_row).astype(BF16)
        return carry

    over_rows(out.shape[0], body)(0)


def cross_back_kernel(blocks, valid, g_ref, own, came, later, gain, upstream, q, kv, mixed, logs, *refs):
    halves = (refs[0:4], refs[4:8])
    later_grad, later_low, sums, dq, dkv, head_sums, part = refs[8:15]
    w_out, w_in, mixed_grad = refs[15:]
    g, wide = g_ref[0], q.shape[1]
    fill(g, halves, w_out, [(3, 0)])
    fill(g, halves, w_in, [(0, 0)])
    norm_back_rows(own, came, later, gain, upstream, later_grad, later_low, sums)
    mixed_grad[...] = dot(later_low[...], w_out[...]).astype(BF16)
    attend_back(
        q, kv.at[:, :wide], kv.at[:, wide:], mixed_grad, mixed, logs, dq, dkv.at[:, :wide], dkv.at[:, wide:],
        head_sums, False, blocks, valid,
    )
    part[...] = dot(dq[...], w_in[...], NT).astype(BF16)


def cross_back(g, own, came, later, gain, upstream, q, kv, mixed, logs, weights, blocks, valid):
    m, d = later.shape
    n, wide = kv.shape[0], q.shape[1]
    return call(
        functools.partial(cross_back_kernel, blocks, valid), "cross_back",
        [((m, d), F32), ((m, d), BF16), ((8, d), F32), ((m, wide), BF16), ((n, 2 * wide), BF16), ((8, wide), F32),
         ((m, d), BF16)],
        [g, own, came, later, gain, upstream, q, kv, mixed, logs, *weights[0], *weights[1]],
        scratch=[pltpu.VMEM((d, wide), BF16), pltpu.VMEM((d, wide), BF16), pltpu.VMEM((m, wide), BF16)],
        flops=4 * m * d * wide + 10 * m * n * wide * 2,
    )


def cross_grads_kernel(blocks, g_ref, later_low, mixed, normed, dq, memory, dkv, *refs):
    halves, grads = (refs[0:4], refs[4:8]), (refs[8:12], refs[12:16])
    keep, send, w_in, result, piece = refs[16:]
    g, core, wide = g_ref[0], g_ref[1], dq.shape[1]
    n, d = memory.shape
    fill(g, halves, w_in, [(1, 0), (2, wide)])
    size = n // blocks
    for i in range(blocks):
        rows = slice(i * size, (i + 1) * size)
        piece[...] = dot(dkv[rows, :], w_in[...], NT).astype(BF16)
        keep[rows, :] = piece[:, pl.ds(pl.multiple_of(core * (d // 2), d // 2), d // 2)]
        send[rows, :] = piece[:, pl.ds(pl.multiple_of((1 - core) * (d // 2), d // 2), d // 2)]
    for which, left, right in (
        (3, later_low[...], mixed[...]), (0, normed[...], dq[...]),
        (1, memory[...], dkv[:, :wide]), (2, memory[...], dkv[:, wide:]),
    ):
        result[...] = dot(left, right, TN).astype(BF16)
        unfill(g, grads, result, [(which, 0)])


def cross_grads(g, later_low, mixed, normed, dq, memory, dkv, weights, blocks):
    m, d = later_low.shape
    n, wide = memory.shape[0], dq.shape[1]
    rows = d // GROUPS
    return call(
        functools.partial(cross_grads_kernel, blocks), "cross_grads",
        [((2, rows, 4 * PAIR), BF16)] * (2 * GROUPS) + [((n, d // 2), BF16)] * 2,
        [g, later_low, mixed, normed, dq, memory, dkv, *weights[0], *weights[1]],
        scratch=[pltpu.VMEM((d, 2 * wide), BF16), pltpu.VMEM((d, wide), BF16), pltpu.VMEM((n // blocks, d), BF16)],
        flops=4 * m * d * wide + 8 * n * d * wide,
    )


def self_back_kernel(g_ref, own, came, middle, gain, upstream, qkv, mixed, logs, *refs):
    halves = (refs[0:4], refs[4:8])
    middle_grad, middle_low, sums, dqkv, head_sums, part = refs[8:14]
    w_in, w_out, mixed_grad = refs[14:]
    g, wide = g_ref[0], mixed.shape[1]
    fill(g, halves, w_in, [(0, 0), (1, wide), (2, 2 * wide)])
    fill(g, halves, w_out, [(3, 0)])
    norm_back_rows(own, came, middle, gain, upstream, middle_grad, middle_low, sums)
    mixed_grad[...] = dot(middle_low[...], w_out[...]).astype(BF16)
    cut = [slice(i * wide, (i + 1) * wide) for i in range(3)]
    attend_back(
        *(qkv.at[:, c] for c in cut), mixed_grad, mixed, logs, *(dqkv.at[:, c] for c in cut), head_sums, True, 1,
        middle.shape[0],
    )
    part[...] = dot(dqkv[...], w_in[...], NT).astype(BF16)


def self_back(g, own, came, middle, gain, upstream, qkv, mixed, logs, weights):
    m, d = middle.shape
    wide = mixed.shape[1]
    return call(
        self_back_kernel, "self_back",
        [((m, d), F32), ((m, d), BF16), ((8, d), F32), ((m, 3 * wide), BF16), ((8, wide), F32), ((m, d), BF16)],
        [g, own, came, middle, gain, upstream, qkv, mixed, logs, *weights[0], *weights[1]],
        scratch=[pltpu.VMEM((d, 3 * wide), BF16), pltpu.VMEM((d, wide), BF16), pltpu.VMEM((m, wide), BF16)],
        flops=8 * m * d * wide + 10 * m * m * wide * 2,
    )


def self_grads_kernel(g_ref, middle_low, mixed, normed, dqkv, *refs):
    grads, result = (refs[0:4], refs[4:8]), refs[8]
    g, wide = g_ref[0], mixed.shape[1]
    result[...] = dot(middle_low[...], mixed[...], TN).astype(BF16)
    unfill(g, grads, result, [(3, 0)])
    for which in range(3):
        result[...] = dot(normed[...], dqkv[:, which * wide : (which + 1) * wide], TN).astype(BF16)
        unfill(g, grads, result, [(which, 0)])


def self_grads(g, middle_low, mixed, normed, dqkv):
    m, d = middle_low.shape
    wide = mixed.shape[1]
    return call(
        self_grads_kernel, "self_grads", [((2, d // GROUPS, 4 * PAIR), BF16)] * (2 * GROUPS),
        [g, middle_low, mixed, normed, dqkv], scratch=[pltpu.VMEM((d, wide), BF16)], flops=8 * m * d * wide,
    )


def start_back_kernel(g_ref, own, came, start, gain, upstream, grad, sums):
    norm_back_rows(own, came, start, gain, upstream, grad, None, sums)


def flip(x, bit, size):
    return lax.ppermute(x, "fsdp", [(i, i ^ (1 << bit)) for i in range(size)])


def turn(x, step, size):
    return lax.ppermute(x, "tensor", [(i, (i + step) % size) for i in range(size)])


def half(x, index, axis):
    size = x.shape[axis] // 2
    return lax.dynamic_slice_in_dim(x, index * size, size, axis=axis)


def after(x, *waits):
    return lax.optimization_barrier((x, *waits))[0]


def after_all(xs, waits):
    return lax.optimization_barrier((*xs, *waits))[: len(xs)]


def add(a, b):
    return (a.astype(F32) + b.astype(F32)).astype(BF16)


def on_device(
    n_f, n_t,
    tokens, encoder, cotangent, self_weights, self_biases, self_output, cross_query, cross_memory,
    cross_biases, cross_output, hidden_weight, hidden_bias, reduce_weight, norm_gains, norm_shifts, branch_biases,
):
    bits = n_f.bit_length() - 1
    x_bit, y_bit = bits - 2, bits - 1
    f = lax.axis_index("fsdp")
    z = lax.axis_index("tensor")
    core = f % 2
    group = f >> x_bit
    g = jnp.stack([group, core]).astype(jnp.int32)
    length, d = tokens.shape[1], tokens.shape[2]
    frames = encoder.shape[1]
    own_clips = tokens.shape[0]
    assert own_clips * 2 == n_t == 4 and bits >= 3
    per = d // n_f
    units_here = hidden_bias.shape[1]
    units = units_here * n_f
    heads_here = self_biases.shape[2]
    inner = n_f // GROUPS

    def begin(weights, extra=None, waits=()):
        keep = jnp.concatenate([half(w, core, 1) for w in weights], axis=1)
        send = jnp.concatenate([half(w, 1 - core, 1) for w in weights], axis=1)
        width = keep.shape[1]
        now, more = keep, extra
        for bit in range(bits - 2):
            rows = now.shape[0]
            out = send if bit == 0 else now
            if more is not None:
                out = jnp.concatenate([out, more.reshape(-1, width)])
            if waits:
                out = after(out, *waits)
            came = flip(out, bit, n_f)
            low = (f >> bit) % 2 == 0
            a, b = now, came[:rows]
            now = jnp.where(low, jnp.concatenate([a, b]), jnp.concatenate([b, a]))
            if more is not None:
                b = came[rows:]
                more = jnp.where(low, jnp.concatenate([more, b]), jnp.concatenate([b, more]))
        return now if more is None else jnp.concatenate([now, more])

    def around(now):
        return [now] + [turn(now, s, n_t) for s in range(1, n_t)]

    def gather_xy(a, b):
        a1, b2 = flip(a, x_bit, n_f), flip(b, y_bit, n_f)
        b1, a2 = flip(b, x_bit, n_f), flip(a, y_bit, n_f)
        a3, b3 = flip(a1, y_bit, n_f), flip(b2, x_bit, n_f)
        return (a, a1, a2, a3), (b, b1, b2, b3)

    small = jnp.concatenate(
        [v.reshape(-1) for v in (norm_gains, norm_shifts, branch_biases, hidden_bias, self_biases, cross_biases)]
    )
    lanes = 4 * PAIR
    small_rows = -(-small.shape[0] // (16 * lanes)) * 16
    small = jnp.pad(small, (0, small_rows * lanes - small.shape[0])).reshape(small_rows, lanes)

    first = around(begin([self_weights[0], self_weights[1], self_weights[2], self_output.T], small))
    w_self = gather_xy(jnp.stack(first[:2]), jnp.stack(first[2:]))
    second = begin([cross_query, cross_memory[0], cross_memory[1], cross_output.T], waits=first[:1])
    second = around(after(second, *first[1:]))
    w_cross = gather_xy(
        *after_all([jnp.stack(second[:2]), jnp.stack(second[2:])], w_self[0][1:3] + w_self[1][1:3])
    )
    third = begin([hidden_weight, reduce_weight.T], waits=first[:1])
    third = around(after(third, *second[1:]))
    wide_half = units // 2
    w_hidden, w_reduce = gather_xy(
        *after_all(
            [jnp.stack([t[:, :wide_half] for t in third]), jnp.stack([t[:, wide_half:] for t in third])],
            w_cross[0][1:3] + w_cross[1][1:3],
        )
    )

    rows = d // GROUPS
    table = jnp.stack(
        [
            jnp.concatenate([w_self[0][j][:, rows:], w_self[1][j][:, rows:]]).reshape(n_t, inner, -1)
            for j in range(GROUPS)
        ]
    )
    table = jnp.concatenate(
        [lax.dynamic_index_in_dim(table, group ^ j, axis=0, keepdims=False) for j in range(GROUPS)], axis=1
    ).astype(F32)
    features = table[0, :, : 9 * per].reshape(n_f, 9, per).transpose(1, 0, 2).reshape(9, d)
    at = 9 * per
    hidden_slots = half(table[:, :, at : at + units_here].reshape(n_t, 1, units), core, 2)
    at += units_here

    def head_slots(at):
        v = table[:, :, at : at + 2 * heads_here].reshape(n_t, n_f, 2, heads_here).transpose(2, 0, 1, 3)
        return half(v.reshape(2, n_t, n_f * heads_here), core, 2).reshape(2, 1, -1)

    self_bias = head_slots(at)
    cross_bias = head_slots(at + 2 * heads_here)
    zero = jnp.zeros_like(self_bias[0])
    qkv_bias = jnp.concatenate([self_bias[0], zero, self_bias[1]], axis=1)
    kv_bias = jnp.concatenate([zero, cross_bias[1]], axis=1)
    gain, shift, branch = ([features[3 * i + j : 3 * i + j + 1] for j in range(3)] for i in range(3))

    mine = core == z // own_clips

    def take_clip(x):
        x = lax.dynamic_index_in_dim(x, z % own_clips, axis=0, keepdims=False)
        return jnp.where(mine, x, flip(x, 0, n_f))

    part_frames = frames // n_t
    part_pad = -(-part_frames // 128) * 128
    start = take_clip(after(tokens, first[0]))
    upstream = take_clip(after(cotangent, w_self[0][1]))
    memory = jnp.pad(
        take_clip(after(encoder, first[1])).reshape(n_t, part_frames, d), ((0, 0), (0, part_pad - part_frames), (0, 0))
    ).reshape(n_t * part_pad, d)

    def scatter_one(pieces, y_first):
        bit = y_bit if y_first else x_bit
        zero, one, two, three = pieces
        out = (two, three) if y_first else (one, three)
        return [flip(p, bit, n_f) for p in out]

    def scatter_two(pieces, came, y_first):
        zero, one, two, three = pieces
        rest = (zero, one) if y_first else (zero, two)
        stay, go = add(rest[0], came[0]), add(rest[1], came[1])
        return stay, flip(go, x_bit if y_first else y_bit, n_f)

    def scatter_z(slots):
        return slots[0], [turn(slots[s], -s, n_t) for s in range(1, n_t)]

    def scatter_end(own, came):
        now = own.astype(F32)
        for other in came:
            now = now + other.astype(F32)
        for bit in range(bits - 3, 0, -1):
            up = (f >> bit) % 2
            now = half(now, up, 0) + flip(half(now, 1 - up, 0).astype(BF16), bit, n_f).astype(F32)
        return half(now, core, 0), flip(half(now, 1 - core, 0), 0, n_f)

    def unpack(shares, widths):
        keep, came = shares
        result, at = [], 0
        for width in widths:
            a, b = keep[:, at : at + width], came[:, at : at + width]
            result.append(jnp.where(core == 0, jnp.concatenate([a, b], 1), jnp.concatenate([b, a], 1)))
            at += width
        return result

    normed_one, qkv, mixed_one, log_one, part = self_forward(g, start, gain[0], shift[0], qkv_bias, w_self)
    part_came = flip(part, 0, n_f)
    kv = cross_kv(g, memory, kv_bias, w_cross, n_t)
    middle, normed_two, cross_q, mixed_two, log_two, part = cross_forward(
        g, start, part, part_came, branch[0], gain[1], shift[1], cross_bias[0], kv, w_cross, n_t, part_frames
    )
    later, out_part, part, hidden_sums, *g_feed = feed(
        g, middle, part, flip(part, 0, n_f), branch[1], gain[2], shift[2], upstream, hidden_slots, w_hidden, w_reduce
    )
    g_hidden, g_reduce = g_feed[:GROUPS], g_feed[GROUPS:]

    part_came = flip(part, 0, n_f)
    hidden_came, reduce_came = scatter_one(g_hidden, True), scatter_one(g_reduce, False)
    (output,) = call(
        output_kernel, "output", [((length, d), BF16)], [g, later, out_part, flip(out_part, 0, n_f), branch[2]]
    )
    output_half = half(output, core, 0)
    later_grad, later_low, sums_three, dq, dkv, cross_sums, part = cross_back(
        g, part, part_came, after(later, output_half), gain[2], upstream, cross_q, kv, mixed_two, log_two, w_cross,
        n_t, part_frames,
    )
    part_came = flip(part, 0, n_f)
    *g_cross, memory_keep, memory_send = cross_grads(
        g, later_low, mixed_two, normed_two, dq, memory, dkv, w_cross, n_t
    )
    g_cross = (g_cross[:GROUPS], g_cross[GROUPS:])
    memory_came = flip(memory_send, 0, n_f)
    hidden_came, reduce_came = after_all(hidden_came, [memory_keep]), after_all(reduce_came, [memory_keep])
    hidden_two = scatter_two(g_hidden, hidden_came, True)
    reduce_two = scatter_two(g_reduce, reduce_came, False)
    cross_one = (scatter_one(g_cross[0], True), scatter_one(g_cross[1], False))
    memory_sum = add(memory_keep, memory_came)
    middle_grad, middle_low, sums_two, dqkv, self_sums, part = self_back(
        g, part, part_came, after(middle, hidden_two[0], reduce_two[0], memory_sum), gain[1], later_grad, qkv,
        mixed_one, log_one, w_self,
    )
    part_came = flip(part, 0, n_f)
    hidden_last, reduce_last = after_all([hidden_two[1], reduce_two[1]], [middle_low])
    feed_slots = [
        jnp.concatenate([add(hidden_two[0][s], hidden_last[s]), add(reduce_two[0][s], reduce_last[s])], axis=1)
        for s in range(n_t)
    ]
    g_self = self_grads(g, after(middle_low, *feed_slots), mixed_one, normed_one, dqkv)
    g_self = (g_self[:GROUPS], g_self[GROUPS:])
    feed_own, feed_came = scatter_z(feed_slots)
    self_one = (scatter_one(g_self[0], True), scatter_one(g_self[1], False))
    start_grad, sums_one = call(
        start_back_kernel, "start_back", [((length, d), BF16), ((8, d), F32)],
        [g, part, part_came, after(start, g_self[0][0]), gain[0], middle_grad],
    )
    start_half = half(start_grad, core, 0)

    def attention_slots(grads, came, waits):
        came = (after_all(came[0], waits), after_all(came[1], waits))
        two = (scatter_two(grads[0], came[0], True), scatter_two(grads[1], came[1], False))
        return [add(t[0][i], t[1][i]) for t in two for i in range(2)]

    cross_own, cross_came = scatter_z(attention_slots(g_cross, cross_one, [start_half]))
    self_own, self_came = scatter_z(attention_slots(g_self, self_one, [start_half]))
    feed_came = after_all(feed_came, [start_half])
    hidden_share, reduce_t = unpack(scatter_end(feed_own, feed_came), [wide_half, wide_half])
    cq_share, ck_share, cv_share, cross_out_t = unpack(scatter_end(cross_own, cross_came), [PAIR] * 4)
    q_share, k_share, v_share, self_out_t = unpack(scatter_end(self_own, self_came), [PAIR] * 4)

    lead = jnp.where(core == 0, 1.0, 0.0).astype(F32)
    feature_sums = jnp.stack(
        [sums_one[0], sums_two[0], sums_three[0], sums_one[1], sums_two[1], sums_three[1],
         sums_two[2], sums_three[2], sums_three[3]]
    ) * lead

    def from_slots(v):
        natural = jnp.stack(
            [lax.dynamic_index_in_dim(v, (z - at) % n_t, axis=0, keepdims=False) for at in range(n_t)], axis=1
        )
        wide = jnp.zeros((*natural.shape[:2], 2 * natural.shape[2]), F32)
        return lax.dynamic_update_slice(wide, natural, (0, 0, core * natural.shape[2]))

    def by_slot(v):
        return v[:2].reshape(2, n_t, -1).transpose(1, 0, 2)

    unit_sums = [from_slots(hidden_sums[:, :1]), from_slots(by_slot(self_sums)), from_slots(by_slot(cross_sums))]
    packed = jnp.concatenate([feature_sums.reshape(-1)] + [u.reshape(-1) for u in unit_sums]).reshape(-1, 1024)
    for bit in range(bits):
        packed = packed + flip(packed, bit, n_f)
    for step in (1, 2):
        packed = packed + lax.ppermute(packed, "tensor", [(i, i ^ step) for i in range(n_t)])
    packed = packed.reshape(-1)
    feature_share = lax.dynamic_slice(packed[: 9 * d].reshape(9, d), (0, f * per), (9, per))

    def unit_share(at, count, total):
        block = packed[at : at + count * n_t * total].reshape(count, n_t, total)
        return lax.dynamic_slice(block, (0, z, f * (total // n_f)), (count, 1, total // n_f))

    at = 9 * d
    hidden_bias_share = unit_share(at, 1, units)[0]
    at += n_t * units
    self_bias_share = unit_share(at, 2, heads_here * n_f)
    at += 2 * n_t * heads_here * n_f
    cross_bias_share = unit_share(at, 2, heads_here * n_f)

    def own_of(slots, c):
        stacked = jnp.stack(slots)
        return jnp.stack(
            [
                lax.dynamic_index_in_dim(stacked, (z - c * own_clips - i) % n_t, axis=0, keepdims=False)
                for i in range(own_clips)
            ]
        )

    def join(slots, axis):
        keep, came = own_of(slots, core), flip(own_of(slots, 1 - core), 0, n_f)
        return jnp.where(core == 0, jnp.concatenate([keep, came], axis), jnp.concatenate([came, keep], axis))

    def spread_clip(x):
        return join(around(x), 1)

    summed = memory_sum.reshape(n_t, part_pad, d // 2)
    slots = []
    for s in range(n_t):
        block = lax.dynamic_index_in_dim(summed, (z + s) % n_t, axis=0, keepdims=False)
        slots.append(turn(block, s, n_t) if s else block)
    memory_share = join(slots, 2)

    return (
        spread_clip(output_half),
        spread_clip(start_half),
        memory_share[:, :part_frames],
        jnp.stack([q_share, k_share, v_share]),
        self_bias_share,
        self_out_t.T,
        cq_share,
        jnp.stack([ck_share, cv_share]),
        cross_bias_share,
        cross_out_t.T,
        hidden_share,
        hidden_bias_share,
        reduce_t.T,
        feature_share[0:3],
        feature_share[3:6],
        feature_share[6:9],
    )


def solution(mesh):
    n_f, n_t = mesh.shape["fsdp"], mesh.shape["tensor"]
    clips = P("fsdp", None, None)
    stacked = P(None, "fsdp", "tensor")
    biases = P(None, "tensor", "fsdp")
    up, down, rows = P("fsdp", "tensor"), P("tensor", "fsdp"), P(None, "fsdp")
    return jax.shard_map(
        functools.partial(on_device, n_f, n_t),
        mesh=mesh,
        in_specs=(
            clips, clips, clips, stacked, biases, down, up, stacked, biases, down, up, down, down, rows, rows, rows,
        ),
        out_specs=(
            clips, clips, P("fsdp", "tensor", None), stacked, biases, down, up, stacked, biases, down, up, down,
            down, rows, rows, rows,
        ),
        check_vma=False,
    )
```

```python
import functools
import math

import jax
import jax.numpy as jnp
from jax import lax
from jax.experimental import pallas as pl
from jax.experimental.pallas import tpu as pltpu
from jax.sharding import PartitionSpec as P

HEAD_DIM = 64
PAIR = 2 * HEAD_DIM
GROUPS = 4
EPSILON = 1e-05
MASKED = -1e9
SCALE = HEAD_DIM**-0.5
F32 = jnp.float32
BF16 = jnp.bfloat16
VMEM_LIMIT = 63 * 1024 * 1024
MESH = pl.DeviceIdType.MESH
NT = (((1,), (1,)), ((), ()))
TN = (((0,), (0,)), ((), ()))


def call(kernel, name, outs, args, scratch=(), flops=0, grid=None, specs=None, out_specs=None, remote=None, anywhere=(0, 0)):
    out_shape = [jax.ShapeDtypeStruct(shape, dtype) for shape, dtype in outs]
    moved = sum(a.size * a.dtype.itemsize for a in args) + sum(
        math.prod(o.shape) * jnp.dtype(o.dtype).itemsize for o in out_shape
    )
    extra = {}
    if grid is None:
        here, there = pl.BlockSpec(memory_space=pltpu.VMEM), pl.BlockSpec(memory_space=pl.ANY)
        extra["in_specs"] = [there if i < anywhere[0] else here for i in range(len(args))]
        extra["out_specs"] = [there if i < anywhere[1] else here for i in range(len(outs))]
    else:
        extra["grid"] = grid
        extra["in_specs"], extra["out_specs"] = specs(block_whole), out_specs(block_whole)
    if remote is None:
        params = pltpu.CompilerParams(vmem_limit_bytes=VMEM_LIMIT)
    else:
        params = pltpu.CompilerParams(vmem_limit_bytes=VMEM_LIMIT, collective_id=remote, has_side_effects=True)
    return pl.pallas_call(
        kernel,
        name=name,
        out_shape=out_shape,
        scratch_shapes=list(scratch),
        compiler_params=params,
        cost_estimate=pl.CostEstimate(flops=int(flops), bytes_accessed=int(moved), transcendentals=0),
        **extra,
    )(*args)


def block_whole(shape):
    return pl.BlockSpec(shape, lambda *_: (0,) * len(shape))


def dot(a, b, dims=None):
    if dims is None:
        return jnp.dot(a, b, preferred_element_type=F32)
    return lax.dot_general(a, b, dims, preferred_element_type=F32)


def fill(weights, buffer, columns):
    rows, held = buffer.shape[0] // GROUPS, weights.shape[1] // GROUPS
    for s in range(weights.shape[0]):
        for g in range(GROUPS):
            for which, at in columns:
                buffer[g * rows : (g + 1) * rows, at + s * PAIR : at + (s + 1) * PAIR] = weights[
                    s, g * held : g * held + rows, which * PAIR : (which + 1) * PAIR
                ]


def unfill(grads, which, value):
    for s in range(grads.shape[0]):
        grads[s, :, which * PAIR : (which + 1) * PAIR] = value[:, s * PAIR : (s + 1) * PAIR]


class Place:
    def __init__(self, sizes):
        n_f, self.n_t = sizes
        self.x_size, self.y_size = n_f // 4, n_f // 2
        self.f, self.z = lax.axis_index("fsdp"), lax.axis_index("tensor")
        self.core = self.f % 2
        self.group = self.f // self.x_size
        x, y = self.group % 2, self.group // 2
        self.to_x = self.f + (1 - 2 * x) * self.x_size
        self.to_y = self.f + (1 - 2 * y) * self.y_size
        self.to_core = self.f + 1 - 2 * self.core
        self.group_x = self.group + 1 - 2 * x
        self.group_y = self.group + 2 - 4 * y
        self.group_xy = 3 - self.group

    def device(self, f, z):
        return {"fsdp": f, "tensor": z}

    def x(self):
        return self.device(self.to_x, self.z)

    def y(self):
        return self.device(self.to_y, self.z)

    def barrier(self):
        sem = pltpu.get_barrier_semaphore()
        for f in (self.to_x, self.to_y, self.to_core):
            pl.semaphore_signal(sem, inc=1, device_id=self.device(f, self.z), device_id_type=MESH)
        for step in (-1, 1):

            @pl.when(self.has(self.z + step))
            def _():
                pl.semaphore_signal(sem, inc=1, device_id=self.device(self.f, self.z + step), device_id_type=MESH)

        pl.semaphore_wait(sem, 3 + jnp.where(self.z > 0, 1, 0) + jnp.where(self.z < self.n_t - 1, 1, 0))

    def has(self, z):
        return jnp.logical_and(z >= 0, z < self.n_t)


def remote(src, dst, sems, at, device):
    return pltpu.make_async_remote_copy(
        src_ref=src, dst_ref=dst, send_sem=sems[0].at[at], recv_sem=sems[1].at[at], device_id=device, device_id_type=MESH
    )


def sem_pair(*shape):
    return [pltpu.SemaphoreType.DMA(shape), pltpu.SemaphoreType.DMA(shape)]


class Gather:
    steps = 6

    @staticmethod
    def scratch(n_t):
        return [
            pltpu.SemaphoreType.DMA((2, n_t)), pltpu.SemaphoreType.DMA((n_t,)),
            *sem_pair(n_t, 6), pltpu.SemaphoreType.DMA,
        ]

    def __init__(self, place, own, whole, scratch):
        self.place, self.own, self.whole = place, own, whole
        self.z_send, self.z_recv, s, r, self.local = scratch
        self.xy = (s, r)

    def rows(self, slot, group, half=None):
        size = self.own.shape[0]
        if half is None:
            return self.whole.at[slot, pl.ds(pl.multiple_of(group * size, 16), size)]
        return self.whole.at[slot, pl.ds(pl.multiple_of(group * size + half * (size // 2), 16), size // 2)]

    def along_z(self, slot, step, mine=False):
        p = self.place
        to = self.rows(slot, p.group)
        return pltpu.make_async_remote_copy(
            src_ref=self.own if mine else to, dst_ref=to, send_sem=self.z_send.at[(step + 1) // 2, slot],
            recv_sem=self.z_recv.at[slot], device_id=p.device(p.f, p.z + step), device_id_type=MESH,
        )

    def copy(self, slot, at, mine=False):
        p, size = self.place, self.own.shape[0]
        if at < 4:
            half = (0, 1, 1, 0)[at]
            to = self.rows(slot, p.group, half)
            src = self.own.at[pl.ds(half * (size // 2), size // 2)] if mine else to
        else:
            src = to = self.rows(slot, p.group_y, 1) if at == 4 else self.rows(slot, p.group_x, 0)
        return remote(src, to, self.xy, (slot, at), p.x() if at in (0, 1, 4) else p.y())

    def send_xy(self, slot, mine=False):
        for at in (0, 2, 1, 3):
            self.copy(slot, at, mine).start()

    def forward_xy(self, slot):
        self.copy(slot, 0).wait_recv()
        self.copy(slot, 5).start()
        self.copy(slot, 2).wait_recv()
        self.copy(slot, 4).start()

    def arrived(self, r, act):
        p = self.place
        for step in (-1, 1):
            slot = p.z + step * r
            pl.when(p.has(slot))(functools.partial(act, slot, step))

    def run(self, k):
        p = self.place
        if k == 0:
            for step in (-1, 1):
                pl.when(p.has(p.z + step))(lambda step=step: self.along_z(p.z, step, True).start())
            self.send_xy(p.z, True)
            pltpu.make_async_copy(self.own, self.rows(p.z, p.group), self.local).start()
            return
        if k <= 3:

            def passed(slot, step):
                copy = self.along_z(slot, -step)
                copy.wait_recv()
                pl.when(p.has(p.z - step))(copy.start)
                self.send_xy(slot)

            self.arrived(k, passed)
        if k == 1:
            self.forward_xy(p.z)
        elif k <= 4:
            self.arrived(k - 1, lambda slot, step: self.forward_xy(slot))
        else:
            for slot in range(p.n_t):
                for at in (1, 3, 4, 5):
                    self.copy(slot, at).wait_recv()
                for at in range(6):
                    self.copy(slot, at).wait_send()
                for step in (-1, 1):
                    sent = jnp.logical_and(p.has(p.z + step), (p.z - slot) * step >= 0)
                    pl.when(sent)(self.along_z(slot, step).wait_send)
            pltpu.make_async_copy(self.own, self.rows(p.z, p.group), self.local).wait()


class Scatter:
    steps = 7

    @staticmethod
    def scratch(n_t, size, wide):
        half = size // 2
        return [
            pltpu.VMEM((n_t, 2, half, wide), BF16), pltpu.VMEM((n_t, 2, half, wide), BF16),
            pltpu.VMEM((n_t, half, wide), BF16), pltpu.VMEM((n_t, half, wide), BF16),
            pltpu.VMEM((n_t, size, wide), BF16), pltpu.VMEM((2, n_t, size, wide), BF16),
            *sem_pair(n_t, 6), *sem_pair(2, n_t),
        ]

    def __init__(self, place, grads, own, scratch):
        self.place, self.grads, self.own = place, grads, own
        self.came_y, self.came_x, self.last_x, self.last_y, self.sums, self.came_z, a, b, c, d = scratch
        self.xy, self.zs = (a, b), (c, d)
        self.half = own.shape[0] // 2

    def slot(self, k):
        z = self.place.z
        last = self.place.n_t - 1
        low = z * 2 <= last
        far, near = jnp.where(low, last, 0), jnp.where(low, 0, last)
        edge = jnp.logical_or(z == 0, z == last)
        inward = jnp.where(low, 1, -1)
        if k == 0:
            return far
        if k == last:
            return z
        if k == last - 1:
            return z + inward
        return jnp.where(edge, z + 2 * inward, near)

    def at(self, group, half):
        return pl.ds(pl.multiple_of((2 * group + half) * self.half, 16), self.half)

    def copy(self, slot, at):
        p, g = self.place, self.grads
        by_y = at in (0, 2, 5)
        if at < 4:
            half = 0 if by_y else 1
            group = p.group_xy if at < 2 else (p.group_y if by_y else p.group_x)
            came = self.came_y if by_y else self.came_x
            src, to = g.at[slot, self.at(group, half)], came.at[slot, 1 if at < 2 else 0]
        else:
            src = self.came_x.at[slot, 1] if by_y else self.came_y.at[slot, 1]
            to = self.last_y.at[slot] if by_y else self.last_x.at[slot]
        return remote(src, to, self.xy, (slot, at), p.y() if by_y else p.x())

    def along_z(self, slot, way):
        p = self.place
        return remote(
            self.sums.at[slot], self.came_z.at[way, slot], self.zs, (way, slot), p.device(p.f, p.z + 2 * way - 1)
        )

    def over(self, rows, body):
        step = 32

        def one(i, carry):
            body(pl.multiple_of(i * step, step), step)
            return carry

        lax.fori_loop(0, rows // step, one, 0)

    def first(self, slot):
        for at in range(4):
            self.copy(slot, at).start()

    def second(self, slot):
        p = self.place
        self.copy(slot, 0).wait_recv()
        self.copy(slot, 1).wait_recv()

        def body(at, step):
            to = pl.ds(at, step)
            for came, group, half in ((self.came_y, p.group_x, 0), (self.came_x, p.group_y, 1)):
                own = self.grads[slot, pl.ds(pl.multiple_of((2 * group + half) * self.half + at, step), step)]
                came[slot, 1, to] = add(came[slot, 1, to], own)

        self.over(self.half, body)
        self.copy(slot, 4).start()
        self.copy(slot, 5).start()

    def third(self, slot):
        p = self.place
        for at in (2, 3, 4, 5):
            self.copy(slot, at).wait_recv()

        def body(at, step):
            to = pl.ds(at, step)
            for came, last, half in ((self.came_y, self.last_x, 0), (self.came_x, self.last_y, 1)):
                own = self.grads[slot, pl.ds(pl.multiple_of((2 * p.group + half) * self.half + at, step), step)]
                total = own.astype(F32) + came[slot, 0, to].astype(F32) + last[slot, to].astype(F32)
                self.sums[slot, pl.ds(pl.multiple_of(half * self.half + at, step), step)] = total.astype(BF16)

        self.over(self.half, body)
        for way in range(2):
            step = 2 * way - 1

            @pl.when((slot - p.z) * step > 0)
            def _():
                @pl.when(p.has(p.z - step))
                def _():
                    self.along_z(slot, way).wait_recv()

                    def body(at, step):
                        to = pl.ds(at, step)
                        self.sums[slot, to] = add(self.sums[slot, to], self.came_z[way, slot, to])

                    self.over(2 * self.half, body)

                self.along_z(slot, way).start()

    def run(self, k):
        p = self.place
        n = p.n_t
        if k == 0:
            self.first(self.slot(0))
            self.first(self.slot(1))
            return
        if k <= n:
            self.second(self.slot(k - 1))
        if k + 1 < n:
            self.first(self.slot(k + 1))
        if 2 <= k <= n + 1:
            self.third(self.slot(k - 2))
        if k == n + 2:
            z = p.z

            def begin(at, step):
                to = pl.ds(at, step)
                self.own[to] = self.sums[z, to].astype(F32)

            self.over(2 * self.half, begin)
            for way in range(2):
                step = 2 * way - 1

                @pl.when(p.has(z - step))
                def _():
                    self.along_z(z, way).wait_recv()

                    def body(at, step):
                        to = pl.ds(at, step)
                        self.own[to] += self.came_z[way, z, to].astype(F32)

                    self.over(2 * self.half, body)

            for slot in range(n):
                for at in range(6):
                    self.copy(slot, at).wait_send()
                for way in range(2):
                    pl.when((slot - z) * (2 * way - 1) > 0)(self.along_z(slot, way).wait_send)


def hook_of(job, first):
    def hook(p, pairs):
        for k in range(pairs):
            pl.when(p == k)(functools.partial(job.run, first + k))

    return hook


def swap(place, part, came, sems):
    return pltpu.make_async_remote_copy(
        src_ref=part, dst_ref=came, send_sem=sems.at[0], recv_sem=sems.at[1],
        device_id=place.device(place.to_core, place.z), device_id_type=MESH,
    )


def row_step(m):
    return m // 4 if m % 64 == 0 else m


def over_rows(m, body):
    step = row_step(m)

    def run(i, carry):
        return body(pl.ds(pl.multiple_of(i * step, step), step), carry)

    return lambda carry: lax.fori_loop(0, m // step, run, carry)


def normal(values):
    centre = values - jnp.mean(values, axis=-1, keepdims=True)
    inverse = lax.rsqrt(jnp.mean(centre * centre, axis=-1, keepdims=True) + EPSILON)
    return centre * inverse, inverse


def norm_rows(value_at, gain, shift, normed, kept=None):
    gain_row, shift_row = gain[...], shift[...]

    def body(at, carry):
        value = value_at(at)
        if kept is not None:
            kept[at, :] = value
        normed[at, :] = (normal(value)[0] * gain_row + shift_row).astype(BF16)
        return carry

    over_rows(normed.shape[0], body)(0)


def norm_back_rows(own, came, values, gain, upstream, grad_ref, low_ref, sums):
    gain_row = gain[...]
    wide = values.shape[1]

    def body(at, carry):
        q = own[at, :].astype(F32) + came[at, :].astype(F32)
        n, inverse = normal(values[at, :].astype(F32))
        up = upstream[at, :].astype(F32)
        v = q * gain_row
        back = inverse * (v - jnp.mean(v, axis=-1, keepdims=True) - n * jnp.mean(v * n, axis=-1, keepdims=True))
        grad = up + back
        grad_ref[at, :] = grad.astype(grad_ref.dtype)
        if low_ref is not None:
            low_ref[at, :] = grad.astype(BF16)
        terms = (q * n, q, grad, up)
        return tuple(c + jnp.sum(t, axis=0, keepdims=True) for c, t in zip(carry, terms))

    totals = over_rows(values.shape[0], body)(tuple(jnp.zeros((1, wide), F32) for _ in range(4)))
    row = lax.broadcasted_iota(jnp.int32, sums.shape, 0)
    value = jnp.zeros(sums.shape, F32)
    for at, total in enumerate(totals):
        value = jnp.where(row == at, total, value)
    sums[...] = value


def lane_mask(shape, h):
    return (lax.broadcasted_iota(jnp.int32, shape, 1) // HEAD_DIM) == h


def mask_scores(scores, causal, valid):
    size = scores.shape[0]
    if causal:
        key_at = lax.broadcasted_iota(jnp.int32, scores.shape, 0)
        query_at = lax.broadcasted_iota(jnp.int32, scores.shape, 1)
        return jnp.where(key_at <= query_at, scores, MASKED)
    if valid < size:
        edge = valid // 8 * 8
        tail = scores[edge:, :]
        key_at = lax.broadcasted_iota(jnp.int32, tail.shape, 0) + edge
        return jnp.concatenate([scores[:edge, :], jnp.where(key_at < valid, tail, -jnp.inf)], axis=0)
    return scores


def attend(q_ref, k_ref, v_ref, mixed_ref, log_ref, score_buf, causal, blocks, valid, hook):
    size = k_ref.shape[0] // blocks
    pairs = q_ref.shape[1] // PAIR

    def one_pair(p, carry):
        at = pl.ds(pl.multiple_of(p * PAIR, PAIR), PAIR)
        q_all = q_ref[:, at].astype(F32) * SCALE
        result = None
        for h in range(2):
            queries = jnp.where(lane_mask(q_all.shape, h), q_all, 0.0).astype(BF16)
            top = None
            for i in range(blocks):
                rows = slice(i * size, (i + 1) * size)
                scores = mask_scores(dot(k_ref[rows, at], queries, NT), causal, valid)
                score_buf[rows, :] = scores
                now = jnp.max(scores, axis=0, keepdims=True)
                top = now if top is None else jnp.maximum(top, now)
            total, mixed = None, None
            for i in range(blocks):
                rows = slice(i * size, (i + 1) * size)
                raised = jnp.exp(score_buf[rows, :] - top)
                now = jnp.sum(raised, axis=0, keepdims=True)
                total = now if total is None else total + now
                now = dot(v_ref[rows, at], raised.astype(BF16), TN)
                mixed = now if mixed is None else mixed + now
            log_ref[2 * p + h] = jnp.broadcast_to(top + jnp.log(total), log_ref.shape[1:])
            mixed = mixed / total
            if result is None:
                result = mixed
            else:
                row = lax.broadcasted_iota(jnp.int32, mixed.shape, 0)
                result = jnp.where(row < HEAD_DIM, result, mixed)
        mixed_ref[:, at] = jnp.transpose(result).astype(BF16)
        hook(p, pairs)
        return carry

    lax.fori_loop(0, pairs, one_pair, 0)


def attend_back(q_ref, k_ref, v_ref, up_ref, mixed_ref, log_ref, dq_ref, dk_ref, dv_ref, sums, causal, blocks, valid, hook):
    size = k_ref.shape[0] // blocks
    pairs = q_ref.shape[1] // PAIR

    def one_pair(p, carry):
        at = pl.ds(pl.multiple_of(p * PAIR, PAIR), PAIR)
        q_all = q_ref[:, at].astype(F32) * SCALE
        up_all = up_ref[:, at].astype(F32)
        product = up_all * mixed_ref[:, at].astype(F32)
        queries, upstream, inner, logs = [], [], [], []
        for h in range(2):
            chosen = lane_mask(q_all.shape, h)
            queries.append(jnp.where(chosen, q_all, 0.0).astype(BF16))
            upstream.append(jnp.where(chosen, up_all, 0.0).astype(BF16))
            ones = jnp.where(lane_mask((8, PAIR), h), 1.0, 0.0)
            inner.append(
                lax.dot_general(ones, product, NT, precision=lax.Precision.HIGHEST, preferred_element_type=F32)[0:1, :]
            )
            logs.append(log_ref[2 * p + h][0:1, :])
        query_grads = [None, None]
        value_sum = None
        for i in range(blocks):
            rows = slice(i * size, (i + 1) * size)
            keys, values = k_ref[rows, at], v_ref[rows, at]
            key_grad, value_grad = None, None
            for h in range(2):
                chance = jnp.exp(mask_scores(dot(keys, queries[h], NT), causal, valid) - logs[h])
                now = dot(chance.astype(BF16), upstream[h])
                value_grad = now if value_grad is None else value_grad + now
                grad = dot(values, upstream[h], NT)
                score_grad = (chance * (grad - inner[h])).astype(BF16)
                now = dot(score_grad, queries[h])
                key_grad = now if key_grad is None else key_grad + now
                now = dot(keys, score_grad, TN)
                query_grads[h] = now if query_grads[h] is None else query_grads[h] + now
            dk_ref[rows, at] = key_grad.astype(BF16)
            dv_ref[rows, at] = value_grad.astype(BF16)
            now = jnp.sum(value_grad, axis=0, keepdims=True)
            value_sum = now if value_sum is None else value_sum + now
        row = lax.broadcasted_iota(jnp.int32, query_grads[0].shape, 0)
        query_grad = jnp.transpose(jnp.where(row < HEAD_DIM, query_grads[0], query_grads[1])) * SCALE
        dq_ref[:, at] = query_grad.astype(BF16)
        query_sum = jnp.sum(query_grad, axis=0, keepdims=True)
        row = lax.broadcasted_iota(jnp.int32, (8, PAIR), 0)
        sums[:, at] = jnp.where(row == 0, query_sum, jnp.where(row == 1, value_sum, 0.0))
        hook(p, pairs)
        return carry

    lax.fori_loop(0, pairs, one_pair, 0)


def gather_kernel(sizes, own, whole, *scratch):
    place = Place(sizes)
    job = Gather(place, own, whole, scratch)
    place.barrier()
    for k in range(Gather.steps):
        job.run(k)


def gather(sizes, own):
    n_t = sizes[1]
    return call(
        functools.partial(gather_kernel, sizes), "gather", [((n_t, GROUPS * own.shape[0], own.shape[1]), BF16)], [own],
        scratch=Gather.scratch(n_t), remote=0, anywhere=(1, 1),
    )[0]


def self_forward_kernel(
    sizes, own, start, gain, shift, bias, weights, whole, normed, qkv, mixed, logs, part, came, w_in, w_out, score_buf,
    sems, *scratch,
):
    place = Place(sizes)
    job = Gather(place, own, whole, scratch)
    place.barrier()
    job.run(0)
    wide = mixed.shape[1]
    norm_rows(lambda at: start[at, :].astype(F32), gain, shift, normed)
    fill(weights, w_in, [(0, 0), (1, wide), (2, 2 * wide)])
    fill(weights, w_out, [(3, 0)])
    qkv[...] = (dot(normed[...], w_in[...]) + bias[...]).astype(BF16)
    q, k, v = (qkv.at[:, i * wide : (i + 1) * wide] for i in range(3))
    attend(q, k, v, mixed, logs, score_buf, True, 1, start.shape[0], hook_of(job, 1))
    part[...] = dot(mixed[...], w_out[...], NT).astype(BF16)
    job.run(5)
    exchange = swap(place, part, came, sems)
    exchange.start()
    exchange.wait()


def self_forward(sizes, own, start, gain, shift, bias, weights):
    m, d = start.shape
    n_t = sizes[1]
    wide = bias.shape[1] // 3
    heads = wide // HEAD_DIM
    return call(
        functools.partial(self_forward_kernel, sizes), "self_forward",
        [((n_t, GROUPS * own.shape[0], own.shape[1]), BF16), ((m, d), BF16), ((m, 3 * wide), BF16), ((m, wide), BF16),
         ((heads, 8, m), F32), ((m, d), BF16), ((m, d), BF16)],
        [own, start, gain, shift, bias, weights],
        scratch=[
            pltpu.VMEM((d, 3 * wide), BF16), pltpu.VMEM((d, wide), BF16), pltpu.VMEM((m, m), F32),
            pltpu.SemaphoreType.DMA((2,)), *Gather.scratch(n_t),
        ],
        flops=2 * m * d * 4 * wide + 4 * m * m * wide * 2, remote=1, anywhere=(1, 1),
    )


def cross_forward_kernel(
    sizes, blocks, valid, own_weights, start, own, came, branch, gain, shift, bias, bias_kv, memory, weights,
    whole, middle, normed, q, kv, mixed, logs, part, part_came, w_in, w_kv, w_out, score_buf, sems, *scratch,
):
    place = Place(sizes)
    job = Gather(place, own_weights, whole, scratch)
    place.barrier()
    job.run(0)
    wide = mixed.shape[1]
    fill(weights, w_kv, [(1, 0), (2, wide)])
    size = memory.shape[0] // blocks

    def one_block(i, carry):
        at = pl.ds(pl.multiple_of(i * size, size), size)
        kv[at, :] = (dot(memory[at, :], w_kv[...]) + bias_kv[...]).astype(BF16)
        return carry

    lax.fori_loop(0, blocks, one_block, 0)
    job.run(1)
    branch_row = branch[...]
    norm_rows(
        lambda at: start[at, :].astype(F32) + (own[at, :].astype(F32) + came[at, :].astype(F32)) + branch_row,
        gain, shift, normed, middle,
    )
    fill(weights, w_in, [(0, 0)])
    fill(weights, w_out, [(3, 0)])
    q[...] = (dot(normed[...], w_in[...]) + bias[...]).astype(BF16)

    def hook(p, pairs):
        for k in range(3):
            pl.when(p == k)(functools.partial(job.run, 2 + k))

    attend(q, kv.at[:, :wide], kv.at[:, wide:], mixed, logs, score_buf, False, blocks, valid, hook)
    part[...] = dot(mixed[...], w_out[...], NT).astype(BF16)
    job.run(5)
    exchange = swap(place, part, part_came, sems)
    exchange.start()
    exchange.wait()


def cross_forward(sizes, own_weights, start, own, came, branch, gain, shift, bias, bias_kv, memory, weights, blocks, valid):
    m, d = start.shape
    n_t = sizes[1]
    n, wide = memory.shape[0], bias.shape[1]
    heads = wide // HEAD_DIM
    return call(
        functools.partial(cross_forward_kernel, sizes, blocks, valid), "cross_forward",
        [((n_t, GROUPS * own_weights.shape[0], own_weights.shape[1]), BF16), ((m, d), F32), ((m, d), BF16),
         ((m, wide), BF16), ((n, 2 * wide), BF16), ((m, wide), BF16), ((heads, 8, m), F32), ((m, d), BF16),
         ((m, d), BF16)],
        [own_weights, start, own, came, branch, gain, shift, bias, bias_kv, memory, weights],
        scratch=[
            pltpu.VMEM((d, wide), BF16), pltpu.VMEM((d, 2 * wide), BF16), pltpu.VMEM((d, wide), BF16),
            pltpu.VMEM((n, m), F32), pltpu.SemaphoreType.DMA((2,)), *Gather.scratch(n_t),
        ],
        flops=2 * m * d * 2 * wide + 4 * n * d * wide + 4 * m * n * wide * 2, remote=2, anywhere=(1, 1),
    )


def feed_kernel(
    slots, middle, own, came, branch, gain, shift, upstream, bias, weights,
    later, out_part, grad_part, sums, grads, normed, out_acc, grad_acc,
):
    s = pl.program_id(0)
    width = bias.shape[1]
    w_hidden, w_reduce = weights.at[:, :width], weights.at[:, width:]

    @pl.when(s == 0)
    def _():
        branch_row = branch[...]
        norm_rows(
            lambda at: middle[at, :] + (own[at, :].astype(F32) + came[at, :].astype(F32)) + branch_row,
            gain, shift, normed, later,
        )

    expanded = dot(normed[...], w_hidden[...]) + bias[...]
    phi = 0.5 * (1.0 + lax.erf(expanded * (0.5**0.5)))
    activated = (expanded * phi).astype(BF16)
    density = jnp.exp(expanded * expanded * -0.5) * ((2.0 * math.pi) ** -0.5)
    slope = phi + expanded * density
    expanded_grad = dot(upstream[...], w_reduce[...]) * slope
    expanded_low = expanded_grad.astype(BF16)
    sums[...] = jnp.broadcast_to(jnp.sum(expanded_grad, axis=0, keepdims=True), sums.shape)
    out_now = dot(activated, w_reduce[...], NT)
    grad_now = dot(expanded_low, w_hidden[...], NT)

    @pl.when(s == 0)
    def _():
        out_acc[...] = out_now
        grad_acc[...] = grad_now

    @pl.when(jnp.logical_and(s > 0, s < slots - 1))
    def _():
        out_acc[...] += out_now
        grad_acc[...] += grad_now

    @pl.when(s == slots - 1)
    def _():
        out_part[...] = (out_acc[...] + out_now).astype(BF16)
        grad_part[...] = (grad_acc[...] + grad_now).astype(BF16)

    grads[:, :width] = dot(normed[...], expanded_low, TN).astype(BF16)
    grads[:, width:] = dot(upstream[...], activated, TN).astype(BF16)


def feed(middle, own, came, branch, gain, shift, upstream, bias, weights):
    m, d = middle.shape
    slots, _, width = bias.shape
    piece = pl.BlockSpec((None, d, 2 * width), lambda s: (s, 0, 0))
    args = [middle, own, came, branch, gain, shift, upstream]
    return call(
        functools.partial(feed_kernel, slots), "feed_forward_and_back",
        [((m, d), F32), ((m, d), BF16), ((m, d), BF16), ((slots, 8, width), F32), ((slots, d, 2 * width), BF16)],
        [*args, bias, weights],
        scratch=[pltpu.VMEM((m, d), BF16), pltpu.VMEM((m, d), F32), pltpu.VMEM((m, d), F32)],
        flops=12 * m * d * slots * width, grid=(slots,),
        specs=lambda whole: [whole(a.shape) for a in args]
        + [pl.BlockSpec((None, 1, width), lambda s: (s, 0, 0)), piece],
        out_specs=lambda whole: [whole((m, d))] * 3 + [pl.BlockSpec((None, 8, width), lambda s: (s, 0, 0)), piece],
    )


def output_kernel(later, own, came, branch, out):
    branch_row = branch[...]

    def body(at, carry):
        out[at, :] = (later[at, :] + (own[at, :].astype(F32) + came[at, :].astype(F32)) + branch_row).astype(BF16)
        return carry

    over_rows(out.shape[0], body)(0)


def cross_back_kernel(
    sizes, blocks, valid, own, came, later, gain, upstream, q, kv, mixed, logs, weights, normed, memory, feed_grads,
    later_grad, sums, head_sums, part, part_came, grads, keep, send, feed_own,
    later_low, dq, dkv, w_one, w_two, w_kv, mixed_grad, piece, sems, *scratch,
):
    place = Place(sizes)
    job = Scatter(place, feed_grads, feed_own, scratch)
    place.barrier()
    job.run(0)
    wide = q.shape[1]
    n, d = memory.shape
    fill(weights, w_one, [(3, 0)])
    fill(weights, w_two, [(0, 0)])
    norm_back_rows(own, came, later, gain, upstream, later_grad, later_low, sums)
    mixed_grad[...] = dot(later_low[...], w_one[...]).astype(BF16)
    attend_back(
        q, kv.at[:, :wide], kv.at[:, wide:], mixed_grad, mixed, logs, dq, dkv.at[:, :wide], dkv.at[:, wide:],
        head_sums, False, blocks, valid, hook_of(job, 1),
    )
    part[...] = dot(dq[...], w_two[...], NT).astype(BF16)
    fill(weights, w_kv, [(1, 0), (2, wide)])
    unfill(grads, 3, dot(later_low[...], mixed[...], TN).astype(BF16))
    exchange = swap(place, part, part_came, sems)
    exchange.start()
    unfill(grads, 0, dot(normed[...], dq[...], TN).astype(BF16))
    job.run(5)
    size = n // blocks
    own_half = pl.ds(pl.multiple_of(place.core * (d // 2), d // 2), d // 2)
    other_half = pl.ds(pl.multiple_of((1 - place.core) * (d // 2), d // 2), d // 2)

    def one_block(i, carry):
        rows = pl.ds(pl.multiple_of(i * size, size), size)
        piece[...] = dot(dkv[rows, :], w_kv[...], NT).astype(BF16)
        keep[rows, :] = piece[:, own_half]
        send[rows, :] = piece[:, other_half]
        return carry

    lax.fori_loop(0, blocks, one_block, 0)
    unfill(grads, 1, dot(memory[...], dkv[:, :wide], TN).astype(BF16))
    unfill(grads, 2, dot(memory[...], dkv[:, wide:], TN).astype(BF16))
    job.run(6)
    exchange.wait()


def cross_back(
    sizes, own, came, later, gain, upstream, q, kv, mixed, logs, weights, normed, memory, feed_grads, blocks, valid
):
    m, d = later.shape
    n_t = sizes[1]
    n, wide = memory.shape[0], q.shape[1]
    size, feed_wide = d // GROUPS, feed_grads.shape[2]
    return call(
        functools.partial(cross_back_kernel, sizes, blocks, valid), "cross_back",
        [((m, d), F32), ((8, d), F32), ((8, wide), F32), ((m, d), BF16), ((m, d), BF16), ((n_t, d, 4 * PAIR), BF16),
         ((n, d // 2), BF16), ((n, d // 2), BF16), ((size, feed_wide), F32)],
        [own, came, later, gain, upstream, q, kv, mixed, logs, weights, normed, memory, feed_grads],
        scratch=[
            pltpu.VMEM((m, d), BF16), pltpu.VMEM((m, wide), BF16), pltpu.VMEM((n, 2 * wide), BF16),
            pltpu.VMEM((d, wide), BF16), pltpu.VMEM((d, wide), BF16), pltpu.VMEM((d, 2 * wide), BF16),
            pltpu.VMEM((m, wide), BF16), pltpu.VMEM((n // blocks, d), BF16), pltpu.SemaphoreType.DMA((2,)),
            *Scatter.scratch(n_t, size, feed_wide),
        ],
        flops=8 * m * d * wide + 10 * m * n * wide * 2 + 8 * n * d * wide, remote=3,
    )


def self_back_kernel(
    sizes, own, came, middle, gain, upstream, qkv, mixed, logs, weights, normed, cross_grads,
    middle_grad, sums, head_sums, part, part_came, grads, cross_own,
    middle_low, dqkv, w_in, w_out, mixed_grad, sems, *scratch,
):
    place = Place(sizes)
    job = Scatter(place, cross_grads, cross_own, scratch)
    place.barrier()
    job.run(0)
    wide = mixed.shape[1]
    fill(weights, w_in, [(0, 0), (1, wide), (2, 2 * wide)])
    fill(weights, w_out, [(3, 0)])
    norm_back_rows(own, came, middle, gain, upstream, middle_grad, middle_low, sums)
    mixed_grad[...] = dot(middle_low[...], w_out[...]).astype(BF16)
    cut = [slice(i * wide, (i + 1) * wide) for i in range(3)]
    attend_back(
        *(qkv.at[:, c] for c in cut), mixed_grad, mixed, logs, *(dqkv.at[:, c] for c in cut), head_sums, True, 1,
        middle.shape[0], hook_of(job, 1),
    )
    part[...] = dot(dqkv[...], w_in[...], NT).astype(BF16)
    unfill(grads, 3, dot(middle_low[...], mixed[...], TN).astype(BF16))
    exchange = swap(place, part, part_came, sems)
    exchange.start()
    for which in range(3):
        unfill(grads, which, dot(normed[...], dqkv[:, cut[which]], TN).astype(BF16))
    job.run(5)
    job.run(6)
    exchange.wait()


def self_back(sizes, own, came, middle, gain, upstream, qkv, mixed, logs, weights, normed, cross_grads):
    m, d = middle.shape
    n_t = sizes[1]
    wide = mixed.shape[1]
    size, cross_wide = d // GROUPS, cross_grads.shape[2]
    return call(
        functools.partial(self_back_kernel, sizes), "self_back",
        [((m, d), F32), ((8, d), F32), ((8, wide), F32), ((m, d), BF16), ((m, d), BF16), ((n_t, d, 4 * PAIR), BF16),
         ((size, cross_wide), F32)],
        [own, came, middle, gain, upstream, qkv, mixed, logs, weights, normed, cross_grads],
        scratch=[
            pltpu.VMEM((m, d), BF16), pltpu.VMEM((m, 3 * wide), BF16), pltpu.VMEM((d, 3 * wide), BF16),
            pltpu.VMEM((d, wide), BF16), pltpu.VMEM((m, wide), BF16), pltpu.SemaphoreType.DMA((2,)),
            *Scatter.scratch(n_t, size, cross_wide),
        ],
        flops=16 * m * d * wide + 10 * m * m * wide * 2, remote=4,
    )


def start_back_kernel(sizes, own, came, start, gain, upstream, self_grads, grad, sums, self_own, *scratch):
    place = Place(sizes)
    job = Scatter(place, self_grads, self_own, scratch)
    place.barrier()
    job.run(0)
    norm_back_rows(own, came, start, gain, upstream, grad, None, sums)
    for k in range(1, Scatter.steps):
        job.run(k)


def flip(x, bit, size):
    return lax.ppermute(x, "fsdp", [(i, i ^ (1 << bit)) for i in range(size)])


def turn(x, step, size):
    return lax.ppermute(x, "tensor", [(i, (i + step) % size) for i in range(size)])


def half(x, index, axis):
    size = x.shape[axis] // 2
    return lax.dynamic_slice_in_dim(x, index * size, size, axis=axis)


def after(x, *waits):
    return lax.optimization_barrier((x, *waits))[0]


def after_all(xs, waits):
    return lax.optimization_barrier((*xs, *waits))[: len(xs)]


def add(a, b):
    return (a.astype(F32) + b.astype(F32)).astype(BF16)


def on_device(
    n_f, n_t,
    tokens, encoder, cotangent, self_weights, self_biases, self_output, cross_query, cross_memory,
    cross_biases, cross_output, hidden_weight, hidden_bias, reduce_weight, norm_gains, norm_shifts, branch_biases,
):
    bits = n_f.bit_length() - 1
    x_bit, y_bit = bits - 2, bits - 1
    f = lax.axis_index("fsdp")
    z = lax.axis_index("tensor")
    core = f % 2
    sizes = (n_f, n_t)
    length, d = tokens.shape[1], tokens.shape[2]
    frames = encoder.shape[1]
    own_clips = tokens.shape[0]
    assert own_clips * 2 == n_t == 4 and bits >= 3
    per = d // n_f
    units_here = hidden_bias.shape[1]
    units = units_here * n_f
    heads_here = self_biases.shape[2]
    inner = n_f // GROUPS

    def begin(weights, extra=None, waits=()):
        keep = jnp.concatenate([half(w, core, 1) for w in weights], axis=1)
        send = jnp.concatenate([half(w, 1 - core, 1) for w in weights], axis=1)
        width = keep.shape[1]
        now, more = keep, extra
        for bit in range(bits - 2):
            rows = now.shape[0]
            out = send if bit == 0 else now
            if more is not None:
                out = jnp.concatenate([out, more.reshape(-1, width)])
            if waits:
                out = after(out, *waits)
            came = flip(out, bit, n_f)
            low = (f >> bit) % 2 == 0
            a, b = now, came[:rows]
            now = jnp.where(low, jnp.concatenate([a, b]), jnp.concatenate([b, a]))
            if more is not None:
                b = came[rows:]
                more = jnp.where(low, jnp.concatenate([more, b]), jnp.concatenate([b, more]))
        return now if more is None else jnp.concatenate([now, more])

    def around(now):
        return [now] + [turn(now, s, n_t) for s in range(1, n_t)]

    small = jnp.concatenate(
        [v.reshape(-1) for v in (norm_gains, norm_shifts, branch_biases, hidden_bias, self_biases, cross_biases)]
    )
    lanes = 4 * PAIR
    small_rows = -(-small.shape[0] // (16 * lanes)) * 16
    small = jnp.pad(small, (0, small_rows * lanes - small.shape[0])).reshape(small_rows, lanes)

    first = begin([self_weights[0], self_weights[1], self_weights[2], self_output.T], small)
    second = begin([cross_query, cross_memory[0], cross_memory[1], cross_output.T])
    third = begin([hidden_weight, reduce_weight.T])
    wide_half = units // 2
    w_self = gather(sizes, first)

    rows = d // GROUPS
    table = w_self.reshape(n_t, GROUPS, -1, lanes)[:, :, rows:].reshape(n_t, n_f, -1).astype(F32)
    features = table[0, :, : 9 * per].reshape(n_f, 9, per).transpose(1, 0, 2).reshape(9, d)
    at = 9 * per
    hidden_slots = half(table[:, :, at : at + units_here].reshape(n_t, 1, units), core, 2)
    at += units_here

    def head_slots(at):
        v = table[:, :, at : at + 2 * heads_here].reshape(n_t, n_f, 2, heads_here).transpose(2, 0, 1, 3)
        return half(v.reshape(2, n_t, n_f * heads_here), core, 2).reshape(2, 1, -1)

    self_bias = head_slots(at)
    cross_bias = head_slots(at + 2 * heads_here)
    zero = jnp.zeros_like(self_bias[0])
    qkv_bias = jnp.concatenate([self_bias[0], zero, self_bias[1]], axis=1)
    kv_bias = jnp.concatenate([zero, cross_bias[1]], axis=1)
    gain, shift, branch = ([features[3 * i + j : 3 * i + j + 1] for j in range(3)] for i in range(3))

    mine = core == z // own_clips

    def take_clip(x):
        x = lax.dynamic_index_in_dim(x, z % own_clips, axis=0, keepdims=False)
        return jnp.where(mine, x, flip(x, 0, n_f))

    part_frames = frames // n_t
    part_pad = -(-part_frames // 128) * 128
    start = take_clip(tokens)
    upstream = take_clip(cotangent)
    memory = jnp.pad(
        take_clip(encoder).reshape(n_t, part_frames, d), ((0, 0), (0, part_pad - part_frames), (0, 0))
    ).reshape(n_t * part_pad, d)

    def scatter_end(now):
        for bit in range(bits - 3, 0, -1):
            up = (f >> bit) % 2
            now = half(now, up, 0) + flip(half(now, 1 - up, 0).astype(BF16), bit, n_f).astype(F32)
        return half(now, core, 0), flip(half(now, 1 - core, 0), 0, n_f)

    def unpack(shares, widths):
        keep, came = shares
        result, at = [], 0
        for width in widths:
            a, b = keep[:, at : at + width], came[:, at : at + width]
            result.append(jnp.where(core == 0, jnp.concatenate([a, b], 1), jnp.concatenate([b, a], 1)))
            at += width
        return result

    w_cross, normed_one, qkv, mixed_one, log_one, part, came = self_forward(
        sizes, second, start, gain[0], shift[0], qkv_bias, w_self
    )
    w_feed, middle, normed_two, cross_q, kv, mixed_two, log_two, part, came = cross_forward(
        sizes, third, start, part, came, branch[0], gain[1], shift[1], cross_bias[0], kv_bias, memory, w_cross, n_t,
        part_frames,
    )
    later, out_part, part, hidden_sums, g_feed = feed(
        middle, part, came, branch[1], gain[2], shift[2], upstream, hidden_slots, w_feed
    )

    came = flip(part, 0, n_f)
    (output,) = call(output_kernel, "output", [((length, d), BF16)], [later, out_part, flip(out_part, 0, n_f), branch[2]])
    output_half = half(output, core, 0)
    later_grad, sums_three, cross_sums, part, part_came, g_cross, memory_keep, memory_send, feed_own = cross_back(
        sizes, part, came, later, gain[2], upstream, cross_q, kv, mixed_two, log_two, w_cross, normed_two, memory,
        g_feed, n_t, part_frames,
    )
    memory_sum = add(memory_keep, flip(memory_send, 0, n_f))
    middle_grad, sums_two, self_sums, part, part_came, g_self, cross_own = self_back(
        sizes, part, part_came, middle, gain[1], later_grad, qkv, mixed_one, log_one, w_self, normed_one, g_cross
    )
    size = d // GROUPS
    start_grad, sums_one, self_own = call(
        functools.partial(start_back_kernel, sizes), "start_back",
        [((length, d), BF16), ((8, d), F32), ((size, 4 * PAIR), F32)],
        [part, part_came, start, gain[0], middle_grad, g_self], scratch=Scatter.scratch(n_t, size, 4 * PAIR), remote=5,
    )
    start_half = half(start_grad, core, 0)

    hidden_share, reduce_t = unpack(scatter_end(feed_own), [wide_half, wide_half])
    cq_share, ck_share, cv_share, cross_out_t = unpack(scatter_end(cross_own), [PAIR] * 4)
    q_share, k_share, v_share, self_out_t = unpack(scatter_end(self_own), [PAIR] * 4)

    lead = jnp.where(core == 0, 1.0, 0.0).astype(F32)
    feature_sums = jnp.stack(
        [sums_one[0], sums_two[0], sums_three[0], sums_one[1], sums_two[1], sums_three[1],
         sums_two[2], sums_three[2], sums_three[3]]
    ) * lead

    def from_slots(v):
        natural = jnp.swapaxes(v, 0, 1)
        wide = jnp.zeros((*natural.shape[:2], 2 * natural.shape[2]), F32)
        return lax.dynamic_update_slice(wide, natural, (0, 0, core * natural.shape[2]))

    def by_slot(v):
        return v[:2].reshape(2, n_t, -1).transpose(1, 0, 2)

    unit_sums = [from_slots(hidden_sums[:, :1]), from_slots(by_slot(self_sums)), from_slots(by_slot(cross_sums))]
    packed = jnp.concatenate([feature_sums.reshape(-1)] + [u.reshape(-1) for u in unit_sums]).reshape(-1, 1024)
    for bit in range(bits):
        packed = packed + flip(packed, bit, n_f)
    for step in (1, 2):
        packed = packed + lax.ppermute(packed, "tensor", [(i, i ^ step) for i in range(n_t)])
    packed = packed.reshape(-1)
    feature_share = lax.dynamic_slice(packed[: 9 * d].reshape(9, d), (0, f * per), (9, per))

    def unit_share(at, count, total):
        block = packed[at : at + count * n_t * total].reshape(count, n_t, total)
        return lax.dynamic_slice(block, (0, z, f * (total // n_f)), (count, 1, total // n_f))

    at = 9 * d
    hidden_bias_share = unit_share(at, 1, units)[0]
    at += n_t * units
    self_bias_share = unit_share(at, 2, heads_here * n_f)
    at += 2 * n_t * heads_here * n_f
    cross_bias_share = unit_share(at, 2, heads_here * n_f)

    def own_of(slots, c):
        stacked = jnp.stack(slots)
        return jnp.stack(
            [
                lax.dynamic_index_in_dim(stacked, (z - c * own_clips - i) % n_t, axis=0, keepdims=False)
                for i in range(own_clips)
            ]
        )

    def join(slots, axis):
        keep, came = own_of(slots, core), flip(own_of(slots, 1 - core), 0, n_f)
        return jnp.where(core == 0, jnp.concatenate([keep, came], axis), jnp.concatenate([came, keep], axis))

    def spread_clip(x):
        return join(around(x), 1)

    summed = memory_sum.reshape(n_t, part_pad, d // 2)
    slots = []
    for s in range(n_t):
        block = lax.dynamic_index_in_dim(summed, (z + s) % n_t, axis=0, keepdims=False)
        slots.append(turn(block, s, n_t) if s else block)
    memory_share = join(slots, 2)

    return (
        spread_clip(output_half),
        spread_clip(start_half),
        memory_share[:, :part_frames],
        jnp.stack([q_share, k_share, v_share]),
        self_bias_share,
        self_out_t.T,
        cq_share,
        jnp.stack([ck_share, cv_share]),
        cross_bias_share,
        cross_out_t.T,
        hidden_share,
        hidden_bias_share,
        reduce_t.T,
        feature_share[0:3],
        feature_share[3:6],
        feature_share[6:9],
    )


def solution(mesh):
    n_f, n_t = mesh.shape["fsdp"], mesh.shape["tensor"]
    clips = P("fsdp", None, None)
    stacked = P(None, "fsdp", "tensor")
    biases = P(None, "tensor", "fsdp")
    up, down, rows = P("fsdp", "tensor"), P("tensor", "fsdp"), P(None, "fsdp")
    return jax.shard_map(
        functools.partial(on_device, n_f, n_t),
        mesh=mesh,
        in_specs=(
            clips, clips, clips, stacked, biases, down, up, stacked, biases, down, up, down, down, rows, rows, rows,
        ),
        out_specs=(
            clips, clips, P("fsdp", "tensor", None), stacked, biases, down, up, stacked, biases, down, up, down,
            down, rows, rows, rows,
        ),
        check_vma=False,
    )
```

```python
import functools
import math

import jax
import jax.numpy as jnp
from jax import lax
from jax.experimental import pallas as pl
from jax.experimental.pallas import tpu as pltpu
from jax.sharding import PartitionSpec as P

HEAD_DIM = 64
PAIR = 2 * HEAD_DIM
GROUPS = 4
EPSILON = 1e-05
MASKED = -1e9
SCALE = HEAD_DIM**-0.5
F32 = jnp.float32
BF16 = jnp.bfloat16
VMEM_LIMIT = 63 * 1024 * 1024
MESH = pl.DeviceIdType.MESH
NT = (((1,), (1,)), ((), ()))
TN = (((0,), (0,)), ((), ()))


def call(kernel, name, outs, args, scratch=(), flops=0, grid=None, specs=None, out_specs=None, remote=None, anywhere=((), ())):
    out_shape = [jax.ShapeDtypeStruct(shape, dtype) for shape, dtype in outs]
    moved = sum(a.size * a.dtype.itemsize for a in args) + sum(
        math.prod(o.shape) * jnp.dtype(o.dtype).itemsize for o in out_shape
    )
    extra = {}
    if grid is None:
        here, there = pl.BlockSpec(memory_space=pltpu.VMEM), pl.BlockSpec(memory_space=pl.ANY)
        extra["in_specs"] = [there if i in anywhere[0] else here for i in range(len(args))]
        extra["out_specs"] = [there if i in anywhere[1] else here for i in range(len(outs))]
    else:
        extra["grid"] = grid
        extra["in_specs"], extra["out_specs"] = specs(block_whole), out_specs(block_whole)
    if remote is None:
        params = pltpu.CompilerParams(vmem_limit_bytes=VMEM_LIMIT)
    else:
        params = pltpu.CompilerParams(vmem_limit_bytes=VMEM_LIMIT, collective_id=remote, has_side_effects=True)
    return pl.pallas_call(
        kernel,
        name=name,
        out_shape=out_shape,
        scratch_shapes=list(scratch),
        compiler_params=params,
        cost_estimate=pl.CostEstimate(flops=int(flops), bytes_accessed=int(moved), transcendentals=0),
        **extra,
    )(*args)


def block_whole(shape):
    return pl.BlockSpec(shape, lambda *_: (0,) * len(shape))


def dot(a, b, dims=None):
    if dims is None:
        return jnp.dot(a, b, preferred_element_type=F32)
    return lax.dot_general(a, b, dims, preferred_element_type=F32)


def fetch(weights, buffer, columns, sem):
    rows, held = buffer.shape[0] // GROUPS, weights.shape[1] // GROUPS
    parts = [(0, 0, buffer.shape[0])] if rows == held else [(g * held, g * rows, rows) for g in range(GROUPS)]
    for s in range(weights.shape[0]):
        for src, to, size in parts:
            for which, at in columns:
                pltpu.make_async_copy(
                    weights.at[s, src : src + size, which * PAIR : (which + 1) * PAIR],
                    buffer.at[to : to + size, at + s * PAIR : at + (s + 1) * PAIR], sem,
                ).start()


def fetched(buffer, sem):
    pltpu.make_async_copy(buffer, buffer, sem).wait()


def unfill(grads, which, value):
    for s in range(grads.shape[0]):
        grads[s, :, which * PAIR : (which + 1) * PAIR] = value[:, s * PAIR : (s + 1) * PAIR]


class Place:
    def __init__(self, sizes):
        n_f, self.n_t = sizes
        self.x_size, self.y_size = n_f // 4, n_f // 2
        self.f, self.z = lax.axis_index("fsdp"), lax.axis_index("tensor")
        self.core = self.f % 2
        self.group = self.f // self.x_size
        x, y = self.group % 2, self.group // 2
        self.to_x = self.f + (1 - 2 * x) * self.x_size
        self.to_y = self.f + (1 - 2 * y) * self.y_size
        self.to_core = self.f + 1 - 2 * self.core
        self.group_x = self.group + 1 - 2 * x
        self.group_y = self.group + 2 - 4 * y
        self.group_xy = 3 - self.group

    def device(self, f, z):
        return {"fsdp": f, "tensor": z}

    def x(self):
        return self.device(self.to_x, self.z)

    def y(self):
        return self.device(self.to_y, self.z)

    def box(self, at):
        core, x, y, step = at % 2, at // 2 % 2, at // 4 % 2, at // 8
        f, place = self.f, 2 * self.group + self.core
        if core:
            f, place = f + 1 - 2 * self.core, place + 1 - 2 * self.core
        if x:
            f, place = f + self.to_x - self.f, place + 2 * (self.group_x - self.group)
        if y:
            f, place = f + self.to_y - self.f, place + 2 * (self.group_y - self.group)
        z = (self.z, self.z + 1 - 2 * lax.rem(self.z, 2), self.z + 2 - 4 * (self.z // 2), 3 - self.z)[step]
        return f, z, place * self.n_t + z

    def barrier(self, all_of_box=False):
        sem = pltpu.get_barrier_semaphore()
        if all_of_box:
            peers = [self.box(at)[:2] for at in range(1, 8 * self.n_t)]
        else:
            peers = [(self.to_x, self.z), (self.to_y, self.z), (self.to_core, self.z)]
            for step in range(1, self.n_t):
                z = lax.rem(self.z + step, self.n_t)
                peers += [(self.f, z), (self.to_core, z)]
        for f, z in peers:
            pl.semaphore_signal(sem, inc=1, device_id=self.device(f, z), device_id_type=MESH)
        pl.semaphore_wait(sem, len(peers))

    def has(self, z):
        return jnp.logical_and(z >= 0, z < self.n_t)


def remote(src, dst, sems, at, device):
    return pltpu.make_async_remote_copy(
        src_ref=src, dst_ref=dst, send_sem=sems[0].at[at], recv_sem=sems[1].at[at], device_id=device, device_id_type=MESH
    )


def sem_pair(*shape):
    return [pltpu.SemaphoreType.DMA(shape), pltpu.SemaphoreType.DMA(shape)]


class Gather:
    steps = 6

    @staticmethod
    def scratch(n_t):
        return [
            pltpu.SemaphoreType.DMA((2, n_t)), pltpu.SemaphoreType.DMA((n_t,)),
            *sem_pair(n_t, 6), pltpu.SemaphoreType.DMA,
        ]

    def __init__(self, place, own, whole, scratch):
        self.place, self.own, self.whole = place, own, whole
        self.z_send, self.z_recv, s, r, self.local = scratch
        self.xy = (s, r)

    def rows(self, slot, group, half=None):
        size = self.own.shape[0]
        if half is None:
            return self.whole.at[slot, pl.ds(pl.multiple_of(group * size, 16), size)]
        return self.whole.at[slot, pl.ds(pl.multiple_of(group * size + half * (size // 2), 16), size // 2)]

    def along_z(self, slot, step, mine=False):
        p = self.place
        to = self.rows(slot, p.group)
        return pltpu.make_async_remote_copy(
            src_ref=self.own if mine else to, dst_ref=to, send_sem=self.z_send.at[(step + 1) // 2, slot],
            recv_sem=self.z_recv.at[slot], device_id=p.device(p.f, p.z + step), device_id_type=MESH,
        )

    def copy(self, slot, at, mine=False):
        p, size = self.place, self.own.shape[0]
        if at < 4:
            half = (0, 1, 1, 0)[at]
            to = self.rows(slot, p.group, half)
            src = self.own.at[pl.ds(half * (size // 2), size // 2)] if mine else to
        else:
            src = to = self.rows(slot, p.group_y, 1) if at == 4 else self.rows(slot, p.group_x, 0)
        return remote(src, to, self.xy, (slot, at), p.x() if at in (0, 1, 4) else p.y())

    def send_xy(self, slot, mine=False):
        for at in (0, 2, 1, 3):
            self.copy(slot, at, mine).start()

    def forward_xy(self, slot):
        self.copy(slot, 0).wait_recv()
        self.copy(slot, 5).start()
        self.copy(slot, 2).wait_recv()
        self.copy(slot, 4).start()

    def arrived(self, r, act):
        p = self.place
        for step in (-1, 1):
            slot = p.z + step * r
            pl.when(p.has(slot))(functools.partial(act, slot, step))

    def run(self, k):
        p = self.place
        if k == 0:
            for step in (-1, 1):
                pl.when(p.has(p.z + step))(lambda step=step: self.along_z(p.z, step, True).start())
            self.send_xy(p.z, True)
            pltpu.make_async_copy(self.own, self.rows(p.z, p.group), self.local).start()
            return
        if k <= 3:

            def passed(slot, step):
                copy = self.along_z(slot, -step)
                copy.wait_recv()
                pl.when(p.has(p.z - step))(copy.start)
                self.send_xy(slot)

            self.arrived(k, passed)
        if k == 1:
            self.forward_xy(p.z)
        elif k <= 4:
            self.arrived(k - 1, lambda slot, step: self.forward_xy(slot))
        else:
            for slot in range(p.n_t):
                for at in (1, 3, 4, 5):
                    self.copy(slot, at).wait_recv()
                for at in range(6):
                    self.copy(slot, at).wait_send()
                for step in (-1, 1):
                    sent = jnp.logical_and(p.has(p.z + step), (p.z - slot) * step >= 0)
                    pl.when(sent)(self.along_z(slot, step).wait_send)
            pltpu.make_async_copy(self.own, self.rows(p.z, p.group), self.local).wait()


class Clips:
    @staticmethod
    def scratch(count):
        return [*sem_pair(count), pltpu.SemaphoreType.DMA((count,))]

    def __init__(self, place, stored, here, scratch):
        self.place, self.pairs, self.sems, self.local = place, list(zip(stored, here)), scratch[:2], scratch[2]

    def copies(self, i, local):
        p, (stored, here) = self.place, self.pairs[i]
        src = stored.at[lax.rem(p.z, stored.shape[0])]
        if local:
            return pltpu.make_async_copy(src, here, self.local.at[i])
        return remote(src, here, self.sems, i, p.device(p.to_core, p.z))

    def owner(self):
        p = self.place
        return p.z // self.pairs[0][0].shape[0] == p.core

    def start(self):
        @pl.when(self.owner())
        def _():
            for i in range(len(self.pairs)):
                self.copies(i, True).start()
                self.copies(i, False).start()

    def finish(self):
        @pl.when(self.owner())
        def _():
            for i in range(len(self.pairs)):
                self.copies(i, True).wait()
                self.copies(i, False).wait_send()

        @pl.when(jnp.logical_not(self.owner()))
        def _():
            for i in range(len(self.pairs)):
                self.copies(i, False).wait_recv()


class Spread:
    steps = 6

    @staticmethod
    def scratch(clips):
        return [pltpu.SemaphoreType.DMA, *sem_pair(1), pltpu.SemaphoreType.DMA((2, clips)), pltpu.SemaphoreType.DMA((clips,))]

    def __init__(self, place, half, whole, scratch):
        self.place, self.half, self.whole = place, half, whole
        self.local, a, b, self.z_send, self.z_recv = scratch
        self.halves = (a, b)
        self.clips = whole.shape[0]
        self.mine = place.z // self.clips == place.core

    def columns(self, core):
        wide = self.half.shape[1]
        return self.whole.at[lax.rem(self.place.z, self.clips), :, pl.ds(pl.multiple_of(core * wide, 128), wide)]

    def to_owner(self, core):
        p = self.place
        return remote(self.half, self.columns(core), self.halves, 0, p.device(p.to_core, p.z))

    def along_z(self, z, step):
        p = self.place
        clip = lax.rem(z, self.clips)
        return pltpu.make_async_remote_copy(
            src_ref=self.whole.at[clip], dst_ref=self.whole.at[clip], send_sem=self.z_send.at[(step + 1) // 2, clip],
            recv_sem=self.z_recv.at[clip], device_id=p.device(p.f, p.z + step), device_id_type=MESH,
        )

    def run(self, k):
        p = self.place
        if k == 0:
            keep = pltpu.make_async_copy(self.half, self.columns(p.core), self.local)
            pl.when(self.mine)(keep.start)
            pl.when(jnp.logical_not(self.mine))(lambda: self.to_owner(p.core).start())
        elif k == 1:

            @pl.when(self.mine)
            def _():
                pltpu.make_async_copy(self.half, self.columns(p.core), self.local).wait()
                self.to_owner(1 - p.core).wait_recv()
                for step in (-1, 1):
                    pl.when(p.has(p.z + step))(lambda step=step: self.along_z(p.z, step).start())

        elif k <= 4:
            for step in (-1, 1):
                z = p.z + step * (k - 1)

                @pl.when(jnp.logical_and(p.has(z), z // self.clips == p.core))
                def _():
                    self.along_z(z, -step).wait_recv()
                    pl.when(p.has(p.z - step))(lambda: self.along_z(z, -step).start())

        else:
            pl.when(jnp.logical_not(self.mine))(lambda: self.to_owner(p.core).wait_send())
            for i in range(self.clips):
                z = p.core * self.clips + i
                for step in (-1, 1):
                    sent = jnp.logical_and(p.has(p.z + step), (p.z - z) * step >= 0)
                    pl.when(sent)(lambda: self.along_z(z, step).wait_send())


class Frames:
    @staticmethod
    def scratch(n_t, clips):
        return [pltpu.SemaphoreType.DMA, pltpu.SemaphoreType.DMA((n_t,)), pltpu.SemaphoreType.DMA((clips, 2))]

    def __init__(self, place, half, whole, part, scratch):
        self.place, self.half, self.whole, self.part = place, half, whole, part
        self.local, self.send, self.recv = scratch
        self.clips = whole.shape[0]
        self.mine = place.z // self.clips == place.core

    def to(self, clip, core):
        wide = self.half.shape[1]
        return self.whole.at[clip, :, pl.ds(pl.multiple_of(core * wide, 128), wide)]

    def rows(self, z):
        return self.half.at[pl.ds(pl.multiple_of(self.part * z // 16 * 16, 16), self.whole.shape[1])]

    def keep(self):
        p = self.place
        return pltpu.make_async_copy(self.rows(p.z), self.to(lax.rem(p.z, self.clips), p.core), self.local)

    def copy(self, step):
        p = self.place
        clip, z = lax.rem(p.z, self.clips), lax.rem(p.z + step, p.n_t)
        f = p.to_core if step == 0 else p.f - p.core + p.z // self.clips
        return pltpu.make_async_remote_copy(
            src_ref=self.rows(z), dst_ref=self.to(clip, p.core), send_sem=self.send.at[step],
            recv_sem=self.recv.at[clip, p.core], device_id=p.device(f, z), device_id_type=MESH,
        )

    def arriving(self, clip, core):
        p = self.place
        return pltpu.make_async_remote_copy(
            src_ref=self.rows(p.z), dst_ref=self.to(clip, core), send_sem=self.send.at[0],
            recv_sem=self.recv.at[clip, core], device_id=p.device(p.to_core, p.z), device_id_type=MESH,
        )

    def start(self, step):
        if step:
            self.copy(step).start()
        else:
            pl.when(self.mine)(lambda: self.keep().start())
            pl.when(jnp.logical_not(self.mine))(lambda: self.copy(0).start())

    def finish(self):
        p = self.place
        for step in range(1, p.n_t):
            self.copy(step).wait_send()
        pl.when(self.mine)(lambda: self.keep().wait())
        pl.when(jnp.logical_not(self.mine))(lambda: self.copy(0).wait_send())
        for clip in range(self.clips):
            for core in range(2):
                own = jnp.logical_and(p.core * self.clips + clip == p.z, p.core == core)
                pl.when(jnp.logical_not(own))(lambda: self.arriving(clip, core).wait_recv())


class Total:
    @staticmethod
    def scratch(shape):
        return [pltpu.VMEM(shape, F32), *sem_pair(shape[0]), *sem_pair(shape[0])]

    def __init__(self, place, packed, total, scratch):
        self.place, self.packed, self.total, self.came = place, packed, total, scratch[0]
        self.to_sum, self.to_all = scratch[1:3], scratch[3:5]
        self.me = place.box(0)[2]
        self.peers = [place.box(at) for at in range(1, packed.shape[0])]

    def out(self, peer):
        f, z, at = peer
        return pltpu.make_async_remote_copy(
            src_ref=self.packed.at[at], dst_ref=self.came.at[self.me], send_sem=self.to_sum[0].at[at],
            recv_sem=self.to_sum[1].at[self.me], device_id=self.place.device(f, z), device_id_type=MESH,
        )

    def back(self, peer):
        f, z, at = peer
        return pltpu.make_async_remote_copy(
            src_ref=self.total.at[self.me], dst_ref=self.total.at[self.me], send_sem=self.to_all[0].at[at],
            recv_sem=self.to_all[1].at[self.me], device_id=self.place.device(f, z), device_id_type=MESH,
        )

    def arrived(self, sems, buffer, peer):
        f, z, at = peer
        pltpu.make_async_remote_copy(
            src_ref=buffer.at[at], dst_ref=buffer.at[at], send_sem=sems[0].at[at], recv_sem=sems[1].at[at],
            device_id=self.place.device(f, z), device_id_type=MESH,
        ).wait_recv()

    def run(self, k):
        if k == 0:
            for peer in self.peers:
                self.out(peer).start()
            self.came[self.me] = self.packed[self.me]
        elif k == 1:
            for peer in self.peers:
                self.arrived(self.to_sum, self.came, peer)
            self.total[self.me] = jnp.sum(self.came[...], axis=0)
        elif k == 2:
            for peer in self.peers:
                self.back(peer).start()
        else:
            for peer in self.peers:
                self.arrived(self.to_all, self.total, peer)
                self.out(peer).wait_send()
                self.back(peer).wait_send()


class Scatter:
    steps = 7

    @staticmethod
    def scratch(n_t, size, wide):
        half = size // 2
        return [
            pltpu.VMEM((n_t, 2, half, wide), BF16), pltpu.VMEM((n_t, 2, half, wide), BF16),
            pltpu.VMEM((n_t, half, wide), BF16), pltpu.VMEM((n_t, half, wide), BF16),
            pltpu.VMEM((n_t, size, wide), BF16), pltpu.VMEM((2, n_t, size, wide), BF16),
            pltpu.VMEM((n_t, 4, half, wide), BF16), pltpu.SemaphoreType.DMA((n_t, 4)),
            *sem_pair(n_t, 6), *sem_pair(2, n_t),
        ]

    def __init__(self, place, grads, own, scratch):
        self.place, self.grads, self.own = place, grads, own
        self.came_y, self.came_x, self.last_x, self.last_y, self.sums, self.came_z, self.held, self.load, a, b, c, d = scratch
        self.xy, self.zs = (a, b), (c, d)
        self.half = own.shape[0] // 2

    def slot(self, k):
        z = self.place.z
        last = self.place.n_t - 1
        low = z * 2 <= last
        far, near = jnp.where(low, last, 0), jnp.where(low, 0, last)
        edge = jnp.logical_or(z == 0, z == last)
        inward = jnp.where(low, 1, -1)
        if k == 0:
            return far
        if k == last:
            return z
        if k == last - 1:
            return z + inward
        return jnp.where(edge, z + 2 * inward, near)

    def at(self, group, half):
        return pl.ds(pl.multiple_of((2 * group + half) * self.half, 16), self.half)

    def copy(self, slot, at):
        p, g = self.place, self.grads
        by_y = at in (0, 2, 5)
        if at < 4:
            half = 0 if by_y else 1
            group = p.group_xy if at < 2 else (p.group_y if by_y else p.group_x)
            came = self.came_y if by_y else self.came_x
            src, to = g.at[slot, self.at(group, half)], came.at[slot, 1 if at < 2 else 0]
        else:
            src = self.came_x.at[slot, 1] if by_y else self.came_y.at[slot, 1]
            to = self.last_y.at[slot] if by_y else self.last_x.at[slot]
        return remote(src, to, self.xy, (slot, at), p.y() if by_y else p.x())

    def along_z(self, slot, way):
        p = self.place
        return remote(
            self.sums.at[slot], self.came_z.at[way, slot], self.zs, (way, slot), p.device(p.f, p.z + 2 * way - 1)
        )

    def over(self, rows, body):
        step = 32

        def one(i, carry):
            body(pl.multiple_of(i * step, step), step)
            return carry

        lax.fori_loop(0, rows // step, one, 0)

    def hold(self, slot, at):
        p = self.place
        rows = self.at((p.group_x, p.group_y, p.group, p.group)[at], (0, 1, 0, 1)[at])
        return pltpu.make_async_copy(self.grads.at[slot, rows], self.held.at[slot, at], self.load.at[slot, at])

    def first(self, slot):
        for at in range(4):
            self.copy(slot, at).start()
        for at in range(4):
            self.hold(slot, at).start()

    def second(self, slot):
        for at in range(2):
            self.hold(slot, at).wait()
            self.copy(slot, at).wait_recv()

        def body(at, step):
            to = pl.ds(at, step)
            for i, came in enumerate((self.came_y, self.came_x)):
                came[slot, 1, to] = add(came[slot, 1, to], self.held[slot, i, to])

        self.over(self.half, body)
        self.copy(slot, 4).start()
        self.copy(slot, 5).start()

    def third(self, slot):
        p = self.place
        for at in (2, 3, 4, 5):
            self.copy(slot, at).wait_recv()
        for at in (2, 3):
            self.hold(slot, at).wait()

        def body(at, step):
            to = pl.ds(at, step)
            for came, last, half in ((self.came_y, self.last_x, 0), (self.came_x, self.last_y, 1)):
                total = self.held[slot, 2 + half, to].astype(F32) + came[slot, 0, to].astype(F32) + last[slot, to].astype(F32)
                self.sums[slot, pl.ds(pl.multiple_of(half * self.half + at, step), step)] = total.astype(BF16)

        self.over(self.half, body)
        for way in range(2):
            step = 2 * way - 1

            @pl.when((slot - p.z) * step > 0)
            def _():
                @pl.when(p.has(p.z - step))
                def _():
                    self.along_z(slot, way).wait_recv()

                    def body(at, step):
                        to = pl.ds(at, step)
                        self.sums[slot, to] = add(self.sums[slot, to], self.came_z[way, slot, to])

                    self.over(2 * self.half, body)

                self.along_z(slot, way).start()

    def run(self, k):
        p = self.place
        n = p.n_t
        if k == 0:
            self.first(self.slot(0))
            self.first(self.slot(1))
            return
        if k <= n:
            self.second(self.slot(k - 1))
        if k + 1 < n:
            self.first(self.slot(k + 1))
        if 2 <= k <= n + 1:
            self.third(self.slot(k - 2))
        if k == n + 2:
            z = p.z

            def begin(at, step):
                to = pl.ds(at, step)
                self.own[to] = self.sums[z, to].astype(F32)

            self.over(2 * self.half, begin)
            for way in range(2):
                step = 2 * way - 1

                @pl.when(p.has(z - step))
                def _():
                    self.along_z(z, way).wait_recv()

                    def body(at, step):
                        to = pl.ds(at, step)
                        self.own[to] += self.came_z[way, z, to].astype(F32)

                    self.over(2 * self.half, body)

            for slot in range(n):
                for at in range(6):
                    self.copy(slot, at).wait_send()
                for way in range(2):
                    pl.when((slot - z) * (2 * way - 1) > 0)(self.along_z(slot, way).wait_send)


def hook_of(steps):
    def hook(p, pairs):
        for k, functions in steps.items():

            @pl.when(p == k)
            def _():
                for function in functions:
                    function()

    return hook


def step(job, k):
    return functools.partial(job.run, k)


def swap(place, part, came, sems):
    return pltpu.make_async_remote_copy(
        src_ref=part, dst_ref=came, send_sem=sems.at[0], recv_sem=sems.at[1],
        device_id=place.device(place.to_core, place.z), device_id_type=MESH,
    )


def row_step(m):
    return m // 4 if m % 64 == 0 else m


def over_rows(m, body):
    step = row_step(m)

    def run(i, carry):
        return body(pl.ds(pl.multiple_of(i * step, step), step), carry)

    return lambda carry: lax.fori_loop(0, m // step, run, carry)


def normal(values):
    centre = values - jnp.mean(values, axis=-1, keepdims=True)
    inverse = lax.rsqrt(jnp.mean(centre * centre, axis=-1, keepdims=True) + EPSILON)
    return centre * inverse, inverse


def norm_rows(value_at, gain, shift, normed, kept=None):
    gain_row, shift_row = gain[...], shift[...]

    def body(at, carry):
        value = value_at(at)
        if kept is not None:
            kept[at, :] = value
        normed[at, :] = (normal(value)[0] * gain_row + shift_row).astype(BF16)
        return carry

    over_rows(normed.shape[0], body)(0)


def norm_back_rows(own, came, values, gain, upstream, grad_ref, low_ref, sums):
    gain_row = gain[...]
    wide = values.shape[1]

    def body(at, carry):
        q = own[at, :].astype(F32) + came[at, :].astype(F32)
        n, inverse = normal(values[at, :].astype(F32))
        up = upstream[at, :].astype(F32)
        v = q * gain_row
        back = inverse * (v - jnp.mean(v, axis=-1, keepdims=True) - n * jnp.mean(v * n, axis=-1, keepdims=True))
        grad = up + back
        grad_ref[at, :] = grad.astype(grad_ref.dtype)
        if low_ref is not None:
            low_ref[at, :] = grad.astype(BF16)
        terms = (q * n, q, grad, up)
        return tuple(c + jnp.sum(t, axis=0, keepdims=True) for c, t in zip(carry, terms))

    totals = over_rows(values.shape[0], body)(tuple(jnp.zeros((1, wide), F32) for _ in range(4)))
    row = lax.broadcasted_iota(jnp.int32, sums.shape, 0)
    value = jnp.zeros(sums.shape, F32)
    for at, total in enumerate(totals):
        value = jnp.where(row == at, total, value)
    sums[...] = value


def lane_mask(shape, h):
    return (lax.broadcasted_iota(jnp.int32, shape, 1) // HEAD_DIM) == h


def mask_scores(scores, causal, valid):
    size = scores.shape[0]
    if causal:
        key_at = lax.broadcasted_iota(jnp.int32, scores.shape, 0)
        query_at = lax.broadcasted_iota(jnp.int32, scores.shape, 1)
        return jnp.where(key_at <= query_at, scores, MASKED)
    if valid < size:
        edge = valid // 8 * 8
        tail = scores[edge:, :]
        key_at = lax.broadcasted_iota(jnp.int32, tail.shape, 0) + edge
        return jnp.concatenate([scores[:edge, :], jnp.where(key_at < valid, tail, -jnp.inf)], axis=0)
    return scores


def attend(q_ref, k_ref, v_ref, mixed_ref, log_ref, score_buf, causal, blocks, valid, hook):
    size = k_ref.shape[0] // blocks
    pairs = q_ref.shape[1] // PAIR

    def one_pair(p, carry):
        at = pl.ds(pl.multiple_of(p * PAIR, PAIR), PAIR)
        q_all = q_ref[:, at].astype(F32) * SCALE
        result = None
        for h in range(2):
            queries = jnp.where(lane_mask(q_all.shape, h), q_all, 0.0).astype(BF16)
            top = None
            for i in range(blocks):
                rows = slice(i * size, (i + 1) * size)
                scores = mask_scores(dot(k_ref[rows, at], queries, NT), causal, valid - i * size)
                score_buf[rows, :] = scores
                now = jnp.max(scores, axis=0, keepdims=True)
                top = now if top is None else jnp.maximum(top, now)
            total, mixed = None, None
            for i in range(blocks):
                rows = slice(i * size, (i + 1) * size)
                raised = jnp.exp(score_buf[rows, :] - top)
                now = jnp.sum(raised, axis=0, keepdims=True)
                total = now if total is None else total + now
                now = dot(v_ref[rows, at], raised.astype(BF16), TN)
                mixed = now if mixed is None else mixed + now
            log_ref[2 * p + h] = jnp.broadcast_to(top + jnp.log(total), log_ref.shape[1:])
            mixed = mixed / total
            if result is None:
                result = mixed
            else:
                row = lax.broadcasted_iota(jnp.int32, mixed.shape, 0)
                result = jnp.where(row < HEAD_DIM, result, mixed)
        mixed_ref[:, at] = jnp.transpose(result).astype(BF16)
        hook(p, pairs)
        return carry

    lax.fori_loop(0, pairs, one_pair, 0)


def attend_back(q_ref, k_ref, v_ref, up_ref, mixed_ref, log_ref, dq_ref, dk_ref, dv_ref, sums, causal, blocks, valid, hook):
    size = k_ref.shape[0] // blocks
    pairs = q_ref.shape[1] // PAIR

    def one_pair(p, carry):
        at = pl.ds(pl.multiple_of(p * PAIR, PAIR), PAIR)
        q_all = q_ref[:, at].astype(F32) * SCALE
        up_all = up_ref[:, at].astype(F32)
        product = up_all * mixed_ref[:, at].astype(F32)
        queries, upstream, inner, logs = [], [], [], []
        for h in range(2):
            chosen = lane_mask(q_all.shape, h)
            queries.append(jnp.where(chosen, q_all, 0.0).astype(BF16))
            upstream.append(jnp.where(chosen, up_all, 0.0).astype(BF16))
            ones = jnp.where(lane_mask((8, PAIR), h), 1.0, 0.0)
            inner.append(
                lax.dot_general(ones, product, NT, precision=lax.Precision.HIGHEST, preferred_element_type=F32)[0:1, :]
            )
            logs.append(log_ref[2 * p + h][0:1, :])
        query_grads = [None, None]
        value_sum = None
        for i in range(blocks):
            rows = slice(i * size, (i + 1) * size)
            keys, values = k_ref[rows, at], v_ref[rows, at]
            key_grad, value_grad = None, None
            for h in range(2):
                chance = jnp.exp(mask_scores(dot(keys, queries[h], NT), causal, valid - i * size) - logs[h])
                now = dot(chance.astype(BF16), upstream[h])
                value_grad = now if value_grad is None else value_grad + now
                grad = dot(values, upstream[h], NT)
                score_grad = (chance * (grad - inner[h])).astype(BF16)
                now = dot(score_grad, queries[h])
                key_grad = now if key_grad is None else key_grad + now
                now = dot(keys, score_grad, TN)
                query_grads[h] = now if query_grads[h] is None else query_grads[h] + now
            dk_ref[rows, at] = key_grad.astype(BF16)
            dv_ref[rows, at] = value_grad.astype(BF16)
            now = jnp.sum(value_grad, axis=0, keepdims=True)
            value_sum = now if value_sum is None else value_sum + now
        row = lax.broadcasted_iota(jnp.int32, query_grads[0].shape, 0)
        query_grad = jnp.transpose(jnp.where(row < HEAD_DIM, query_grads[0], query_grads[1])) * SCALE
        dq_ref[:, at] = query_grad.astype(BF16)
        query_sum = jnp.sum(query_grad, axis=0, keepdims=True)
        row = lax.broadcasted_iota(jnp.int32, (8, PAIR), 0)
        sums[:, at] = jnp.where(row == 0, query_sum, jnp.where(row == 1, value_sum, 0.0))
        hook(p, pairs)
        return carry

    lax.fori_loop(0, pairs, one_pair, 0)


def gather_kernel(sizes, own, *refs):
    stored, whole, here, scratch = refs[:3], refs[3], refs[4:7], refs[7:]
    place = Place(sizes)
    clips = Clips(place, stored, here, scratch[:3])
    job = Gather(place, own, whole, scratch[3:])
    place.barrier()
    job.run(0)
    clips.start()
    for k in range(1, Gather.steps):
        job.run(k)
    clips.finish()


def gather(sizes, own, stored):
    n_t = sizes[1]
    return call(
        functools.partial(gather_kernel, sizes), "gather",
        [((n_t, GROUPS * own.shape[0], own.shape[1]), BF16)] + [(v.shape[1:], v.dtype) for v in stored], [own, *stored],
        scratch=Clips.scratch(len(stored)) + Gather.scratch(n_t), remote=0, anywhere=((0, 1, 2, 3), (0,)),
    )


def self_forward_kernel(
    sizes, own, start, gain, shift, bias, weights, whole, normed, qkv, mixed, logs, part, came, w_in, w_out, score_buf,
    sems, loads, *scratch,
):
    place = Place(sizes)
    job = Gather(place, own, whole, scratch)
    wide = mixed.shape[1]
    fetch(weights, w_in, [(0, 0), (1, wide), (2, 2 * wide)], loads.at[0])
    fetch(weights, w_out, [(3, 0)], loads.at[1])
    place.barrier()
    job.run(0)
    norm_rows(lambda at: start[at, :].astype(F32), gain, shift, normed)
    fetched(w_in, loads.at[0])
    fetched(w_out, loads.at[1])
    qkv[...] = (dot(normed[...], w_in[...]) + bias[...]).astype(BF16)
    job.run(1)
    q, k, v = (qkv.at[:, i * wide : (i + 1) * wide] for i in range(3))
    attend(q, k, v, mixed, logs, score_buf, True, 1, start.shape[0], hook_of({2: [step(job, 2)]}))
    part[...] = dot(mixed[...], w_out[...], NT).astype(BF16)
    job.run(3)
    exchange = swap(place, part, came, sems)
    exchange.start()
    job.run(4)
    job.run(5)
    exchange.wait()


def self_forward(sizes, own, start, gain, shift, bias, weights):
    m, d = start.shape
    n_t = sizes[1]
    wide = bias.shape[1] // 3
    heads = wide // HEAD_DIM
    return call(
        functools.partial(self_forward_kernel, sizes), "self_forward",
        [((n_t, GROUPS * own.shape[0], own.shape[1]), BF16), ((m, d), BF16), ((m, 3 * wide), BF16), ((m, wide), BF16),
         ((heads, 8, m), F32), ((m, d), BF16), ((m, d), BF16)],
        [own, start, gain, shift, bias, weights],
        scratch=[
            pltpu.VMEM((d, 3 * wide), BF16), pltpu.VMEM((d, wide), BF16), pltpu.VMEM((m, m), F32),
            pltpu.SemaphoreType.DMA((2,)), pltpu.SemaphoreType.DMA((2,)), *Gather.scratch(n_t),
        ],
        flops=2 * m * d * 4 * wide + 4 * m * m * wide * 2, remote=1, anywhere=((0, 5), (0,)),
    )


def cross_forward_kernel(
    sizes, blocks, valid, own_weights, start, own, came, branch, gain, shift, bias, bias_kv, memory, weights,
    whole, middle, normed, q, kv, mixed, logs, part, part_came, w_in, w_kv, w_out, score_buf, sems, loads, *scratch,
):
    place = Place(sizes)
    job = Gather(place, own_weights, whole, scratch)
    wide = mixed.shape[1]
    fetch(weights, w_kv, [(1, 0), (2, wide)], loads.at[0])
    fetch(weights, w_in, [(0, 0)], loads.at[1])
    fetch(weights, w_out, [(3, 0)], loads.at[2])
    place.barrier()
    job.run(0)
    fetched(w_kv, loads.at[0])
    size = memory.shape[0] // blocks

    def one_block(i, carry):
        at = pl.ds(pl.multiple_of(i * size, size), size)
        kv[at, :] = (dot(memory[at, :], w_kv[...]) + bias_kv[...]).astype(BF16)
        return carry

    lax.fori_loop(0, blocks, one_block, 0)
    job.run(1)
    branch_row = branch[...]
    norm_rows(
        lambda at: start[at, :].astype(F32) + (own[at, :].astype(F32) + came[at, :].astype(F32)) + branch_row,
        gain, shift, normed, middle,
    )
    fetched(w_in, loads.at[1])
    fetched(w_out, loads.at[2])
    q[...] = (dot(normed[...], w_in[...]) + bias[...]).astype(BF16)

    attend(
        q, kv.at[:, :wide], kv.at[:, wide:], mixed, logs, score_buf, False, blocks, valid, hook_of({1: [step(job, 2)]})
    )
    part[...] = dot(mixed[...], w_out[...], NT).astype(BF16)
    job.run(3)
    exchange = swap(place, part, part_came, sems)
    exchange.start()
    job.run(4)
    job.run(5)
    exchange.wait()


def cross_forward(sizes, own_weights, start, own, came, branch, gain, shift, bias, bias_kv, memory, weights, blocks, valid):
    m, d = start.shape
    n_t = sizes[1]
    n, wide = memory.shape[0], bias.shape[1]
    heads = wide // HEAD_DIM
    return call(
        functools.partial(cross_forward_kernel, sizes, blocks, valid), "cross_forward",
        [((n_t, GROUPS * own_weights.shape[0], own_weights.shape[1]), BF16), ((m, d), F32), ((m, d), BF16),
         ((m, wide), BF16), ((n, 2 * wide), BF16), ((m, wide), BF16), ((heads, 8, m), F32), ((m, d), BF16),
         ((m, d), BF16)],
        [own_weights, start, own, came, branch, gain, shift, bias, bias_kv, memory, weights],
        scratch=[
            pltpu.VMEM((d, wide), BF16), pltpu.VMEM((d, 2 * wide), BF16), pltpu.VMEM((d, wide), BF16),
            pltpu.VMEM((n, m), F32), pltpu.SemaphoreType.DMA((2,)), pltpu.SemaphoreType.DMA((3,)), *Gather.scratch(n_t),
        ],
        flops=2 * m * d * 2 * wide + 4 * n * d * wide + 4 * m * n * wide * 2, remote=2, anywhere=((0, 10), (0,)),
    )


def feed_kernel(
    slots, middle, own, came, branch, gain, shift, upstream, bias, weights,
    later, out_part, grad_part, sums, grads, normed, out_acc, grad_acc,
):
    s = pl.program_id(0)
    width = bias.shape[1]
    w_hidden, w_reduce = weights.at[:, :width], weights.at[:, width:]

    @pl.when(s == 0)
    def _():
        branch_row = branch[...]
        norm_rows(
            lambda at: middle[at, :] + (own[at, :].astype(F32) + came[at, :].astype(F32)) + branch_row,
            gain, shift, normed, later,
        )

    expanded = dot(normed[...], w_hidden[...]) + bias[...]
    phi = 0.5 * (1.0 + lax.erf(expanded * (0.5**0.5)))
    activated = (expanded * phi).astype(BF16)
    density = jnp.exp(expanded * expanded * -0.5) * ((2.0 * math.pi) ** -0.5)
    slope = phi + expanded * density
    expanded_grad = dot(upstream[...], w_reduce[...]) * slope
    expanded_low = expanded_grad.astype(BF16)
    sums[...] = jnp.broadcast_to(jnp.sum(expanded_grad, axis=0, keepdims=True), sums.shape)
    out_now = dot(activated, w_reduce[...], NT)
    grad_now = dot(expanded_low, w_hidden[...], NT)

    @pl.when(s == 0)
    def _():
        out_acc[...] = out_now
        grad_acc[...] = grad_now

    @pl.when(jnp.logical_and(s > 0, s < slots - 1))
    def _():
        out_acc[...] += out_now
        grad_acc[...] += grad_now

    @pl.when(s == slots - 1)
    def _():
        out_part[...] = (out_acc[...] + out_now).astype(BF16)
        grad_part[...] = (grad_acc[...] + grad_now).astype(BF16)

    grads[:, :width] = dot(normed[...], expanded_low, TN).astype(BF16)
    grads[:, width:] = dot(upstream[...], activated, TN).astype(BF16)


def feed(middle, own, came, branch, gain, shift, upstream, bias, weights):
    m, d = middle.shape
    slots, _, width = bias.shape
    piece = pl.BlockSpec((None, d, 2 * width), lambda s: (s, 0, 0))
    args = [middle, own, came, branch, gain, shift, upstream]
    return call(
        functools.partial(feed_kernel, slots), "feed_forward_and_back",
        [((m, d), F32), ((m, d), BF16), ((m, d), BF16), ((slots, 8, width), F32), ((slots, d, 2 * width), BF16)],
        [*args, bias, weights],
        scratch=[pltpu.VMEM((m, d), BF16), pltpu.VMEM((m, d), F32), pltpu.VMEM((m, d), F32)],
        flops=12 * m * d * slots * width, grid=(slots,),
        specs=lambda whole: [whole(a.shape) for a in args]
        + [pl.BlockSpec((None, 1, width), lambda s: (s, 0, 0)), piece],
        out_specs=lambda whole: [whole((m, d))] * 3 + [pl.BlockSpec((None, 8, width), lambda s: (s, 0, 0)), piece],
    )


def cross_back_kernel(
    sizes, blocks, valid, own, came, later, gain, upstream, q, kv, mixed, logs, weights, normed, memory, feed_grads,
    out_part, out_came, branch,
    output, memory_came, later_grad, sums, head_sums, part, part_came, grads, keep, feed_own,
    later_low, dq, dkv, w_one, w_two, w_kv, mixed_grad, piece, out_half, send, sems, memory_sems, loads, *scratch,
):
    place = Place(sizes)
    spread = Spread(place, out_half, output, scratch[:5])
    job = Scatter(place, feed_grads, feed_own, scratch[5:])
    wide = q.shape[1]
    n, d = memory.shape
    fetch(weights, w_one, [(3, 0)], loads.at[0])
    fetch(weights, w_two, [(0, 0)], loads.at[1])
    fetch(weights, w_kv, [(1, 0), (2, wide)], loads.at[2])
    place.barrier()
    job.run(0)
    out_wide = out_half.shape[1]
    out_at = pl.ds(pl.multiple_of(place.core * out_wide, out_wide), out_wide)
    branch_half = branch[:, out_at]

    def one_row(at, carry):
        total = later[at, out_at] + (out_part[at, out_at].astype(F32) + out_came[at, out_at].astype(F32)) + branch_half
        out_half[at, :] = total.astype(BF16)
        return carry

    over_rows(out_half.shape[0], one_row)(0)
    norm_back_rows(own, came, later, gain, upstream, later_grad, later_low, sums)
    spread.run(0)
    for at, buffer in enumerate((w_one, w_two, w_kv)):
        fetched(buffer, loads.at[at])
    mixed_grad[...] = dot(later_low[...], w_one[...]).astype(BF16)
    attend_back(
        q, kv.at[:, :wide], kv.at[:, wide:], mixed_grad, mixed, logs, dq, dkv.at[:, :wide], dkv.at[:, wide:],
        head_sums, False, blocks, valid, hook_of({0: [step(job, 1), step(spread, 1)], 2: [step(job, 2), step(spread, 2)]}),
    )
    part[...] = dot(dq[...], w_two[...], NT).astype(BF16)
    unfill(grads, 3, dot(later_low[...], mixed[...], TN).astype(BF16))
    exchange = swap(place, part, part_came, sems)
    exchange.start()
    unfill(grads, 0, dot(normed[...], dq[...], TN).astype(BF16))
    job.run(3)
    spread.run(3)
    size = n // blocks
    own_half = pl.ds(pl.multiple_of(place.core * (d // 2), d // 2), d // 2)
    other_half = pl.ds(pl.multiple_of((1 - place.core) * (d // 2), d // 2), d // 2)

    def one_block(i, carry):
        rows = pl.ds(pl.multiple_of(i * size, size), size)
        piece[...] = dot(dkv[rows, :], w_kv[...], NT).astype(BF16)
        keep[rows, :] = piece[:, own_half]
        send[rows, :] = piece[:, other_half]
        return carry

    lax.fori_loop(0, blocks, one_block, 0)
    spread.run(4)
    memory_exchange = swap(place, send, memory_came, memory_sems)
    memory_exchange.start()
    unfill(grads, 1, dot(memory[...], dkv[:, :wide], TN).astype(BF16))
    unfill(grads, 2, dot(memory[...], dkv[:, wide:], TN).astype(BF16))
    for k in (4, 5, 6):
        job.run(k)
    spread.run(5)
    exchange.wait()
    memory_exchange.wait()


def cross_back(
    sizes, own, came, later, gain, upstream, q, kv, mixed, logs, weights, normed, memory, feed_grads, out_part, out_came,
    branch, clips, blocks, valid,
):
    m, d = later.shape
    n_t = sizes[1]
    n, wide = memory.shape[0], q.shape[1]
    size, feed_wide = d // GROUPS, feed_grads.shape[2]
    return call(
        functools.partial(cross_back_kernel, sizes, blocks, valid), "cross_back",
        [((clips, m, d), BF16), ((n, d // 2), BF16), ((m, d), F32), ((8, d), F32), ((8, wide), F32), ((m, d), BF16),
         ((m, d), BF16), ((n_t, d, 4 * PAIR), BF16), ((n, d // 2), BF16), ((size, feed_wide), F32)],
        [own, came, later, gain, upstream, q, kv, mixed, logs, weights, normed, memory, feed_grads, out_part, out_came,
         branch],
        scratch=[
            pltpu.VMEM((m, d), BF16), pltpu.VMEM((m, wide), BF16), pltpu.VMEM((n, 2 * wide), BF16),
            pltpu.VMEM((d, wide), BF16), pltpu.VMEM((d, wide), BF16), pltpu.VMEM((d, 2 * wide), BF16),
            pltpu.VMEM((m, wide), BF16), pltpu.VMEM((n // blocks, d), BF16), pltpu.VMEM((m, d // 2), BF16),
            pltpu.VMEM((n, d // 2), BF16), pltpu.SemaphoreType.DMA((2,)), pltpu.SemaphoreType.DMA((2,)),
            pltpu.SemaphoreType.DMA((3,)), *Spread.scratch(clips), *Scatter.scratch(n_t, size, feed_wide),
        ],
        flops=8 * m * d * wide + 10 * m * n * wide * 2 + 8 * n * d * wide, remote=3, anywhere=((9, 12), (0, 1)),
    )


def self_back_kernel(
    sizes, frames, own, came, middle, gain, upstream, qkv, mixed, logs, weights, normed, cross_grads, keep, keep_came,
    start, start_gain,
    whole, half_grad, start_sums, sums, head_sums, grads, cross_own,
    middle_grad, grad, part, part_came, middle_low, dqkv, w_in, w_out, mixed_grad, memory_sum, sems, loads, *scratch,
):
    place = Place(sizes)
    memory_job = Frames(place, memory_sum, whole, frames, scratch[:3])
    job = Scatter(place, cross_grads, cross_own, scratch[3:])
    wide = mixed.shape[1]
    fetch(weights, w_in, [(0, 0), (1, wide), (2, 2 * wide)], loads.at[0])
    fetch(weights, w_out, [(3, 0)], loads.at[1])
    place.barrier()
    job.run(0)

    def one_row(at, carry):
        memory_sum[at, :] = add(keep[at, :], keep_came[at, :])
        return carry

    over_rows(memory_sum.shape[0], one_row)(0)
    fetched(w_in, loads.at[0])
    fetched(w_out, loads.at[1])
    for at in (1, 3, 0):
        memory_job.start(at)
    norm_back_rows(own, came, middle, gain, upstream, middle_grad, middle_low, sums)
    job.run(1)
    mixed_grad[...] = dot(middle_low[...], w_out[...]).astype(BF16)
    cut = [slice(i * wide, (i + 1) * wide) for i in range(3)]
    attend_back(
        *(qkv.at[:, c] for c in cut), mixed_grad, mixed, logs, *(dqkv.at[:, c] for c in cut), head_sums, True, 1,
        middle.shape[0], hook_of({0: [step(job, 2)], 2: [step(job, 3)]}),
    )
    part[...] = dot(dqkv[...], w_in[...], NT).astype(BF16)
    job.run(4)
    exchange = swap(place, part, part_came, sems)
    exchange.start()
    unfill(grads, 3, dot(middle_low[...], mixed[...], TN).astype(BF16))
    unfill(grads, 0, dot(normed[...], dqkv[:, cut[0]], TN).astype(BF16))
    job.run(5)
    memory_job.start(2)
    exchange.wait()
    norm_back_rows(part, part_came, start, start_gain, middle_grad, grad, None, start_sums)
    half = half_grad.shape[1]
    half_grad[...] = grad[:, pl.ds(pl.multiple_of(place.core * half, half), half)]
    for which in (1, 2):
        unfill(grads, which, dot(normed[...], dqkv[:, cut[which]], TN).astype(BF16))
    job.run(6)
    memory_job.finish()


def self_back(
    sizes, own, came, middle, gain, upstream, qkv, mixed, logs, weights, normed, cross_grads, keep, keep_came, start, start_gain,
    clips, frames,
):
    m, d = middle.shape
    n_t = sizes[1]
    wide = mixed.shape[1]
    size, cross_wide = d // GROUPS, cross_grads.shape[2]
    return call(
        functools.partial(self_back_kernel, sizes, frames), "self_back",
        [((clips, (frames + 30) // 16 * 16, d), BF16), ((m, d // 2), BF16), ((8, d), F32), ((8, d), F32), ((8, wide), F32),
         ((n_t, d, 4 * PAIR), BF16), ((size, cross_wide), F32)],
        [own, came, middle, gain, upstream, qkv, mixed, logs, weights, normed, cross_grads, keep, keep_came,
         start, start_gain],
        scratch=[
            pltpu.VMEM((m, d), F32), *[pltpu.VMEM((m, d), BF16)] * 4,
            pltpu.VMEM((m, 3 * wide), BF16), pltpu.VMEM((d, 3 * wide), BF16),
            pltpu.VMEM((d, wide), BF16), pltpu.VMEM((m, wide), BF16), pltpu.VMEM(keep.shape, BF16),
            pltpu.SemaphoreType.DMA((2,)), pltpu.SemaphoreType.DMA((2,)), *Frames.scratch(n_t, clips), *Scatter.scratch(n_t, size, cross_wide),
        ],
        flops=16 * m * d * wide + 10 * m * m * wide * 2, remote=4, anywhere=((8, 10), (0,)),
    )


def finish_kernel(sizes, self_grads, half_grad, packed, whole, total, self_own, *scratch):
    place = Place(sizes)
    spread = Spread(place, half_grad, whole, scratch[:5])
    all_sum = Total(place, packed, total, scratch[5:10])
    job = Scatter(place, self_grads, self_own, scratch[10:])
    place.barrier(True)
    all_sum.run(0)
    spread.run(0)
    job.run(0)
    spread.run(1)
    job.run(1)
    all_sum.run(1)
    spread.run(2)
    job.run(2)
    all_sum.run(2)
    spread.run(3)
    job.run(3)
    spread.run(4)
    for k in (4, 5, 6):
        job.run(k)
    spread.run(5)
    all_sum.run(3)


def finish(sizes, half_grad, self_grads, packed, clips):
    m, half = half_grad.shape
    n_t, d, wide = self_grads.shape
    size = d // GROUPS
    return call(
        functools.partial(finish_kernel, sizes), "finish",
        [((clips, m, 2 * half), BF16), (packed.shape, F32), ((size, wide), F32)], [self_grads, half_grad, packed],
        scratch=[*Spread.scratch(clips), *Total.scratch(packed.shape), *Scatter.scratch(n_t, size, wide)],
        remote=5, anywhere=((0,), (0,)),
    )


def flip(x, bit, size):
    return lax.ppermute(x, "fsdp", [(i, i ^ (1 << bit)) for i in range(size)])


def half(x, index, axis):
    size = x.shape[axis] // 2
    return lax.dynamic_slice_in_dim(x, index * size, size, axis=axis)


def add(a, b):
    return (a.astype(F32) + b.astype(F32)).astype(BF16)


def on_device(
    n_f, n_t,
    tokens, encoder, cotangent, self_weights, self_biases, self_output, cross_query, cross_memory,
    cross_biases, cross_output, hidden_weight, hidden_bias, reduce_weight, norm_gains, norm_shifts, branch_biases,
):
    bits = n_f.bit_length() - 1
    x_bit, y_bit = bits - 2, bits - 1
    f = lax.axis_index("fsdp")
    z = lax.axis_index("tensor")
    core = f % 2
    sizes = (n_f, n_t)
    length, d = tokens.shape[1], tokens.shape[2]
    frames = encoder.shape[1]
    own_clips = tokens.shape[0]
    assert own_clips * 2 == n_t == 4 and bits >= 3
    per = d // n_f
    units_here = hidden_bias.shape[1]
    units = units_here * n_f
    heads_here = self_biases.shape[2]
    inner = n_f // GROUPS

    def begin(weights, extra=None, waits=()):
        keep = jnp.concatenate([half(w, core, 1) for w in weights], axis=1)
        send = jnp.concatenate([half(w, 1 - core, 1) for w in weights], axis=1)
        width = keep.shape[1]
        now, more = keep, extra
        for bit in range(bits - 2):
            rows = now.shape[0]
            out = send if bit == 0 else now
            if more is not None:
                out = jnp.concatenate([out, more.reshape(-1, width)])
            if waits:
                out = after(out, *waits)
            came = flip(out, bit, n_f)
            low = (f >> bit) % 2 == 0
            a, b = now, came[:rows]
            now = jnp.where(low, jnp.concatenate([a, b]), jnp.concatenate([b, a]))
            if more is not None:
                b = came[rows:]
                more = jnp.where(low, jnp.concatenate([more, b]), jnp.concatenate([b, more]))
        return now if more is None else jnp.concatenate([now, more])

    small = jnp.concatenate(
        [v.reshape(-1) for v in (norm_gains, norm_shifts, branch_biases, hidden_bias, self_biases, cross_biases)]
    )
    lanes = 4 * PAIR
    small_rows = -(-small.shape[0] // (16 * lanes)) * 16
    small = jnp.pad(small, (0, small_rows * lanes - small.shape[0])).reshape(small_rows, lanes)

    first = begin([self_weights[0], self_weights[1], self_weights[2], self_output.T], small)
    second = begin([cross_query, cross_memory[0], cross_memory[1], cross_output.T])
    third = begin([hidden_weight, reduce_weight.T])
    wide_half = units // 2
    pad = -(-frames // 512) * 512 - frames
    w_self, start, upstream, memory = gather(
        sizes, first, [tokens, cotangent, jnp.pad(encoder, ((0, 0), (0, pad), (0, 0)))]
    )

    rows = d // GROUPS
    table = w_self.reshape(n_t, GROUPS, -1, lanes)[:, :, rows:].reshape(n_t, n_f, -1).astype(F32)
    features = table[0, :, : 9 * per].reshape(n_f, 9, per).transpose(1, 0, 2).reshape(9, d)
    at = 9 * per
    hidden_slots = half(table[:, :, at : at + units_here].reshape(n_t, 1, units), core, 2)
    at += units_here

    def head_slots(at):
        v = table[:, :, at : at + 2 * heads_here].reshape(n_t, n_f, 2, heads_here).transpose(2, 0, 1, 3)
        return half(v.reshape(2, n_t, n_f * heads_here), core, 2).reshape(2, 1, -1)

    self_bias = head_slots(at)
    cross_bias = head_slots(at + 2 * heads_here)
    zero = jnp.zeros_like(self_bias[0])
    qkv_bias = jnp.concatenate([self_bias[0], zero, self_bias[1]], axis=1)
    kv_bias = jnp.concatenate([zero, cross_bias[1]], axis=1)
    gain, shift, branch = ([features[3 * i + j : 3 * i + j + 1] for j in range(3)] for i in range(3))

    part_frames = frames // n_t

    def scatter_end(now):
        for bit in range(bits - 3, 0, -1):
            up = (f >> bit) % 2
            now = half(now, up, 0) + flip(half(now, 1 - up, 0).astype(BF16), bit, n_f).astype(F32)
        return half(now, core, 0), flip(half(now, 1 - core, 0), 0, n_f)

    def unpack(shares, widths):
        keep, came = shares
        result, at = [], 0
        for width in widths:
            a, b = keep[:, at : at + width], came[:, at : at + width]
            result.append(jnp.where(core == 0, jnp.concatenate([a, b], 1), jnp.concatenate([b, a], 1)))
            at += width
        return result

    w_cross, normed_one, qkv, mixed_one, log_one, part, came = self_forward(
        sizes, second, start, gain[0], shift[0], qkv_bias, w_self
    )
    w_feed, middle, normed_two, cross_q, kv, mixed_two, log_two, part, came = cross_forward(
        sizes, third, start, part, came, branch[0], gain[1], shift[1], cross_bias[0], kv_bias, memory, w_cross, n_t,
        frames,
    )
    later, out_part, part, hidden_sums, g_feed = feed(
        middle, part, came, branch[1], gain[2], shift[2], upstream, hidden_slots, w_feed
    )

    came, out_came = flip(part, 0, n_f), flip(out_part, 0, n_f)
    output, memory_came, later_grad, sums_three, cross_sums, part, part_came, g_cross, memory_keep, feed_own = cross_back(
        sizes, part, came, later, gain[2], upstream, cross_q, kv, mixed_two, log_two, w_cross, normed_two, memory,
        g_feed, out_part, out_came, branch[2], own_clips, n_t, frames,
    )
    memory_share, half_grad, sums_one, sums_two, self_sums, g_self, cross_own = self_back(
        sizes, part, part_came, middle, gain[1], later_grad, qkv, mixed_one, log_one, w_self, normed_one, g_cross,
        memory_keep, memory_came, start, gain[0], own_clips, part_frames,
    )

    lead = jnp.where(core == 0, 1.0, 0.0).astype(F32)
    feature_sums = jnp.stack(
        [sums_one[0], sums_two[0], sums_three[0], sums_one[1], sums_two[1], sums_three[1],
         sums_two[2], sums_three[2], sums_three[3]]
    ) * lead

    def from_slots(v):
        natural = jnp.swapaxes(v, 0, 1)
        wide = jnp.zeros((*natural.shape[:2], 2 * natural.shape[2]), F32)
        return lax.dynamic_update_slice(wide, natural, (0, 0, core * natural.shape[2]))

    def by_slot(v):
        return v[:2].reshape(2, n_t, -1).transpose(1, 0, 2)

    unit_sums = [from_slots(hidden_sums[:, :1]), from_slots(by_slot(self_sums)), from_slots(by_slot(cross_sums))]
    packed = jnp.concatenate([feature_sums.reshape(-1)] + [u.reshape(-1) for u in unit_sums])
    boxes = -(-packed.size // (32 * 1024))
    packed = jnp.pad(packed.reshape(-1), (0, boxes * 32 * 1024 - packed.size)).reshape(32, 8 * boxes, 128)
    tokens_grad, packed, self_own = finish(sizes, half_grad, g_self, packed, own_clips)
    for bit in range(1, bits - 2):
        packed = packed + flip(packed, bit, n_f)
    packed = packed.reshape(-1)
    feature_share = lax.dynamic_slice(packed[: 9 * d].reshape(9, d), (0, f * per), (9, per))

    def unit_share(at, count, total):
        block = packed[at : at + count * n_t * total].reshape(count, n_t, total)
        return lax.dynamic_slice(block, (0, z, f * (total // n_f)), (count, 1, total // n_f))

    at = 9 * d
    hidden_bias_share = unit_share(at, 1, units)[0]
    at += n_t * units
    self_bias_share = unit_share(at, 2, heads_here * n_f)
    at += 2 * n_t * heads_here * n_f
    cross_bias_share = unit_share(at, 2, heads_here * n_f)

    hidden_share, reduce_t = unpack(scatter_end(feed_own), [wide_half, wide_half])
    cq_share, ck_share, cv_share, cross_out_t = unpack(scatter_end(cross_own), [PAIR] * 4)
    q_share, k_share, v_share, self_out_t = unpack(scatter_end(self_own), [PAIR] * 4)

    memory_share = lax.dynamic_slice_in_dim(memory_share, part_frames * z % 16, part_frames, axis=1)

    return (
        output,
        tokens_grad,
        memory_share,
        jnp.stack([q_share, k_share, v_share]),
        self_bias_share,
        self_out_t.T,
        cq_share,
        jnp.stack([ck_share, cv_share]),
        cross_bias_share,
        cross_out_t.T,
        hidden_share,
        hidden_bias_share,
        reduce_t.T,
        feature_share[0:3],
        feature_share[3:6],
        feature_share[6:9],
    )


def solution(mesh):
    n_f, n_t = mesh.shape["fsdp"], mesh.shape["tensor"]
    clips = P("fsdp", None, None)
    stacked = P(None, "fsdp", "tensor")
    biases = P(None, "tensor", "fsdp")
    up, down, rows = P("fsdp", "tensor"), P("tensor", "fsdp"), P(None, "fsdp")
    return jax.shard_map(
        functools.partial(on_device, n_f, n_t),
        mesh=mesh,
        in_specs=(
            clips, clips, clips, stacked, biases, down, up, stacked, biases, down, up, down, down, rows, rows, rows,
        ),
        out_specs=(
            clips, clips, P("fsdp", "tensor", None), stacked, biases, down, up, stacked, biases, down, up, down,
            down, rows, rows, rows,
        ),
        check_vma=False,
    )
```

```python
import functools
import math

import jax
import jax.numpy as jnp
from jax import lax
from jax.experimental import pallas as pl
from jax.experimental.pallas import tpu as pltpu
from jax.sharding import PartitionSpec as P

HEAD_DIM = 64
PAIR = 2 * HEAD_DIM
GROUPS = 4
EPSILON = 1e-05
MASKED = -1e9
SCALE = HEAD_DIM**-0.5
F32 = jnp.float32
BF16 = jnp.bfloat16
VMEM_LIMIT = 63 * 1024 * 1024
MESH = pl.DeviceIdType.MESH
NT = (((1,), (1,)), ((), ()))
TN = (((0,), (0,)), ((), ()))


def call(kernel, name, outs, args, scratch=(), flops=0, grid=None, specs=None, out_specs=None, remote=None, anywhere=((), ())):
    out_shape = [jax.ShapeDtypeStruct(shape, dtype) for shape, dtype in outs]
    moved = sum(a.size * a.dtype.itemsize for a in args) + sum(
        math.prod(o.shape) * jnp.dtype(o.dtype).itemsize for o in out_shape
    )
    extra = {}
    if grid is None:
        here, there = pl.BlockSpec(memory_space=pltpu.VMEM), pl.BlockSpec(memory_space=pl.ANY)
        extra["in_specs"] = [there if i in anywhere[0] else here for i in range(len(args))]
        extra["out_specs"] = [there if i in anywhere[1] else here for i in range(len(outs))]
    else:
        extra["grid"] = grid
        extra["in_specs"], extra["out_specs"] = specs(block_whole), out_specs(block_whole)
    if remote is None:
        params = pltpu.CompilerParams(vmem_limit_bytes=VMEM_LIMIT)
    else:
        params = pltpu.CompilerParams(vmem_limit_bytes=VMEM_LIMIT, collective_id=remote, has_side_effects=True)
    return pl.pallas_call(
        kernel,
        name=name,
        out_shape=out_shape,
        scratch_shapes=list(scratch),
        compiler_params=params,
        cost_estimate=pl.CostEstimate(flops=int(flops), bytes_accessed=int(moved), transcendentals=0),
        **extra,
    )(*args)


def block_whole(shape):
    return pl.BlockSpec(shape, lambda *_: (0,) * len(shape))


def dot(a, b, dims=None):
    if dims is None:
        return jnp.dot(a, b, preferred_element_type=F32)
    return lax.dot_general(a, b, dims, preferred_element_type=F32)


def fetch(weights, buffer, columns, sem):
    rows, held = buffer.shape[0] // GROUPS, weights.shape[1] // GROUPS
    parts = [(0, 0, buffer.shape[0])] if rows == held else [(g * held, g * rows, rows) for g in range(GROUPS)]
    for s in range(weights.shape[0]):
        for src, to, size in parts:
            for which, at in columns:
                pltpu.make_async_copy(
                    weights.at[s, src : src + size, which * PAIR : (which + 1) * PAIR],
                    buffer.at[to : to + size, at + s * PAIR : at + (s + 1) * PAIR], sem,
                ).start()


def fetched(buffer, sem):
    pltpu.make_async_copy(buffer, buffer, sem).wait()


def unfill(grads, which, value):
    for s in range(grads.shape[0]):
        grads[s, :, which * PAIR : (which + 1) * PAIR] = value[:, s * PAIR : (s + 1) * PAIR]


class Place:
    def __init__(self, sizes):
        n_f, self.n_t = sizes
        self.x_size, self.y_size = n_f // 4, n_f // 2
        self.f, self.z = lax.axis_index("fsdp"), lax.axis_index("tensor")
        self.core = self.f % 2
        self.group = self.f // self.x_size
        x, y = self.group % 2, self.group // 2
        self.to_x = self.f + (1 - 2 * x) * self.x_size
        self.to_y = self.f + (1 - 2 * y) * self.y_size
        self.to_core = self.f + 1 - 2 * self.core
        self.group_x = self.group + 1 - 2 * x
        self.group_y = self.group + 2 - 4 * y
        self.group_xy = 3 - self.group

    def device(self, f, z):
        return {"fsdp": f, "tensor": z}

    def x(self):
        return self.device(self.to_x, self.z)

    def y(self):
        return self.device(self.to_y, self.z)

    def box(self, at):
        core, x, y, step = at % 2, at // 2 % 2, at // 4 % 2, at // 8
        f, place = self.f, 2 * self.group + self.core
        if core:
            f, place = f + 1 - 2 * self.core, place + 1 - 2 * self.core
        if x:
            f, place = f + self.to_x - self.f, place + 2 * (self.group_x - self.group)
        if y:
            f, place = f + self.to_y - self.f, place + 2 * (self.group_y - self.group)
        z = (self.z, self.z + 1 - 2 * lax.rem(self.z, 2), self.z + 2 - 4 * (self.z // 2), 3 - self.z)[step]
        return f, z, place * self.n_t + z

    def barrier(self, all_of_box=False):
        sem = pltpu.get_barrier_semaphore()
        if all_of_box:
            peers = [self.box(at)[:2] for at in range(1, 8 * self.n_t)]
        else:
            peers = [(self.to_x, self.z), (self.to_y, self.z), (self.to_core, self.z)]
            for step in range(1, self.n_t):
                z = lax.rem(self.z + step, self.n_t)
                peers += [(self.f, z), (self.to_core, z)]
        for f, z in peers:
            pl.semaphore_signal(sem, inc=1, device_id=self.device(f, z), device_id_type=MESH)
        pl.semaphore_wait(sem, len(peers))

    def slot(self, k):
        z, last = self.z, self.n_t - 1
        low = z * 2 <= last
        far, near = jnp.where(low, last, 0), jnp.where(low, 0, last)
        inward = jnp.where(low, 1, -1)
        if k == 0:
            return far
        if k == last:
            return z
        if k == last - 1:
            return z + inward
        return jnp.where(jnp.logical_or(z == 0, z == last), z + 2 * inward, near)

    def has(self, z):
        return jnp.logical_and(z >= 0, z < self.n_t)


def remote(src, dst, sems, at, device):
    return pltpu.make_async_remote_copy(
        src_ref=src, dst_ref=dst, send_sem=sems[0].at[at], recv_sem=sems[1].at[at], device_id=device, device_id_type=MESH
    )


def sem_pair(*shape):
    return [pltpu.SemaphoreType.DMA(shape), pltpu.SemaphoreType.DMA(shape)]


class Gather:
    steps = 6

    @staticmethod
    def scratch(n_t):
        return [
            pltpu.SemaphoreType.DMA((2, n_t)), pltpu.SemaphoreType.DMA((n_t,)),
            *sem_pair(n_t, 6), pltpu.SemaphoreType.DMA,
        ]

    def __init__(self, place, own, whole, scratch):
        self.place, self.own, self.whole = place, own, whole
        self.z_send, self.z_recv, s, r, self.local = scratch
        self.xy = (s, r)

    def rows(self, slot, group, half=None):
        size = self.own.shape[0]
        if half is None:
            return self.whole.at[slot, pl.ds(pl.multiple_of(group * size, 16), size)]
        return self.whole.at[slot, pl.ds(pl.multiple_of(group * size + half * (size // 2), 16), size // 2)]

    def along_z(self, slot, step, mine=False):
        p = self.place
        to = self.rows(slot, p.group)
        return pltpu.make_async_remote_copy(
            src_ref=self.own if mine else to, dst_ref=to, send_sem=self.z_send.at[(step + 1) // 2, slot],
            recv_sem=self.z_recv.at[slot], device_id=p.device(p.f, p.z + step), device_id_type=MESH,
        )

    def copy(self, slot, at, mine=False):
        p, size = self.place, self.own.shape[0]
        if at < 4:
            half = (0, 1, 1, 0)[at]
            to = self.rows(slot, p.group, half)
            src = self.own.at[pl.ds(half * (size // 2), size // 2)] if mine else to
        else:
            src = to = self.rows(slot, p.group_y, 1) if at == 4 else self.rows(slot, p.group_x, 0)
        return remote(src, to, self.xy, (slot, at), p.x() if at in (0, 1, 4) else p.y())

    def send_xy(self, slot, mine=False):
        for at in (0, 2, 1, 3):
            self.copy(slot, at, mine).start()

    def forward_xy(self, slot):
        self.copy(slot, 0).wait_recv()
        self.copy(slot, 5).start()
        self.copy(slot, 2).wait_recv()
        self.copy(slot, 4).start()

    def arrived(self, r, act):
        p = self.place
        for step in (-1, 1):
            slot = p.z + step * r
            pl.when(p.has(slot))(functools.partial(act, slot, step))

    def complete(self, slot):
        for at in (1, 3, 4, 5):
            self.copy(slot, at).wait_recv()

    def run(self, k, arrivals=True):
        p = self.place
        if k == 0:
            for step in (-1, 1):
                pl.when(p.has(p.z + step))(lambda step=step: self.along_z(p.z, step, True).start())
            self.send_xy(p.z, True)
            pltpu.make_async_copy(self.own, self.rows(p.z, p.group), self.local).start()
            return
        if k <= 3:

            def passed(slot, step):
                copy = self.along_z(slot, -step)
                copy.wait_recv()
                pl.when(p.has(p.z - step))(copy.start)
                self.send_xy(slot)

            self.arrived(k, passed)
        if k == 1:
            self.forward_xy(p.z)
            pltpu.make_async_copy(self.own, self.rows(p.z, p.group), self.local).wait()
        elif k <= 4:
            self.arrived(k - 1, lambda slot, step: self.forward_xy(slot))
        else:
            for slot in range(p.n_t):
                if arrivals:
                    self.complete(slot)
                for at in range(6):
                    self.copy(slot, at).wait_send()
                for step in (-1, 1):
                    sent = jnp.logical_and(p.has(p.z + step), (p.z - slot) * step >= 0)
                    pl.when(sent)(self.along_z(slot, step).wait_send)


class Clips:
    @staticmethod
    def scratch(count):
        return [*sem_pair(count), pltpu.SemaphoreType.DMA((count,))]

    def __init__(self, place, stored, here, scratch):
        self.place, self.pairs, self.sems, self.local = place, list(zip(stored, here)), scratch[:2], scratch[2]

    def copies(self, i, local):
        p, (stored, here) = self.place, self.pairs[i]
        src = stored.at[lax.rem(p.z, stored.shape[0])]
        if local:
            return pltpu.make_async_copy(src, here, self.local.at[i])
        return remote(src, here, self.sems, i, p.device(p.to_core, p.z))

    def owner(self):
        p = self.place
        return p.z // self.pairs[0][0].shape[0] == p.core

    def start(self):
        @pl.when(self.owner())
        def _():
            for i in range(len(self.pairs)):
                self.copies(i, True).start()
                self.copies(i, False).start()

    def finish(self):
        @pl.when(self.owner())
        def _():
            for i in range(len(self.pairs)):
                self.copies(i, True).wait()
                self.copies(i, False).wait_send()

        @pl.when(jnp.logical_not(self.owner()))
        def _():
            for i in range(len(self.pairs)):
                self.copies(i, False).wait_recv()


class Spread:
    steps = 6

    @staticmethod
    def scratch(clips):
        return [pltpu.SemaphoreType.DMA, *sem_pair(1), pltpu.SemaphoreType.DMA((2, clips)), pltpu.SemaphoreType.DMA((clips,))]

    def __init__(self, place, half, whole, scratch):
        self.place, self.half, self.whole = place, half, whole
        self.local, a, b, self.z_send, self.z_recv = scratch
        self.halves = (a, b)
        self.clips = whole.shape[0]
        self.mine = place.z // self.clips == place.core

    def columns(self, core):
        wide = self.half.shape[1]
        return self.whole.at[lax.rem(self.place.z, self.clips), :, pl.ds(pl.multiple_of(core * wide, 128), wide)]

    def to_owner(self, core):
        p = self.place
        return remote(self.half, self.columns(core), self.halves, 0, p.device(p.to_core, p.z))

    def along_z(self, z, step):
        p = self.place
        clip = lax.rem(z, self.clips)
        return pltpu.make_async_remote_copy(
            src_ref=self.whole.at[clip], dst_ref=self.whole.at[clip], send_sem=self.z_send.at[(step + 1) // 2, clip],
            recv_sem=self.z_recv.at[clip], device_id=p.device(p.f, p.z + step), device_id_type=MESH,
        )

    def run(self, k):
        p = self.place
        if k == 0:
            keep = pltpu.make_async_copy(self.half, self.columns(p.core), self.local)
            pl.when(self.mine)(keep.start)
            pl.when(jnp.logical_not(self.mine))(lambda: self.to_owner(p.core).start())
        elif k == 1:

            @pl.when(self.mine)
            def _():
                pltpu.make_async_copy(self.half, self.columns(p.core), self.local).wait()
                self.to_owner(1 - p.core).wait_recv()
                for step in (-1, 1):
                    pl.when(p.has(p.z + step))(lambda step=step: self.along_z(p.z, step).start())

        elif k <= 4:
            for step in (-1, 1):
                z = p.z + step * (k - 1)

                @pl.when(jnp.logical_and(p.has(z), z // self.clips == p.core))
                def _():
                    self.along_z(z, -step).wait_recv()
                    pl.when(p.has(p.z - step))(lambda: self.along_z(z, -step).start())

        else:
            pl.when(jnp.logical_not(self.mine))(lambda: self.to_owner(p.core).wait_send())
            for i in range(self.clips):
                z = p.core * self.clips + i
                for step in (-1, 1):
                    sent = jnp.logical_and(p.has(p.z + step), (p.z - z) * step >= 0)
                    pl.when(sent)(lambda: self.along_z(z, step).wait_send())


class Frames:
    @staticmethod
    def scratch(n_t, clips):
        return [pltpu.SemaphoreType.DMA, pltpu.SemaphoreType.DMA((n_t,)), pltpu.SemaphoreType.DMA((clips, 2))]

    def __init__(self, place, half, whole, part, scratch):
        self.place, self.half, self.whole, self.part = place, half, whole, part
        self.local, self.send, self.recv = scratch
        self.clips = whole.shape[0]
        self.mine = place.z // self.clips == place.core

    def to(self, clip, core):
        wide = self.half.shape[1]
        return self.whole.at[clip, :, pl.ds(pl.multiple_of(core * wide, 128), wide)]

    def rows(self, z):
        return self.half.at[pl.ds(pl.multiple_of(self.part * z // 16 * 16, 16), self.whole.shape[1])]

    def keep(self):
        p = self.place
        return pltpu.make_async_copy(self.rows(p.z), self.to(lax.rem(p.z, self.clips), p.core), self.local)

    def copy(self, step):
        p = self.place
        clip, z = lax.rem(p.z, self.clips), lax.rem(p.z + step, p.n_t)
        f = p.to_core if step == 0 else p.f - p.core + p.z // self.clips
        return pltpu.make_async_remote_copy(
            src_ref=self.rows(z), dst_ref=self.to(clip, p.core), send_sem=self.send.at[step],
            recv_sem=self.recv.at[clip, p.core], device_id=p.device(f, z), device_id_type=MESH,
        )

    def arriving(self, clip, core):
        p = self.place
        return pltpu.make_async_remote_copy(
            src_ref=self.rows(p.z), dst_ref=self.to(clip, core), send_sem=self.send.at[0],
            recv_sem=self.recv.at[clip, core], device_id=p.device(p.to_core, p.z), device_id_type=MESH,
        )

    def start(self, step):
        if step:
            self.copy(step).start()
        else:
            pl.when(self.mine)(lambda: self.keep().start())
            pl.when(jnp.logical_not(self.mine))(lambda: self.copy(0).start())

    def finish(self):
        p = self.place
        for step in range(1, p.n_t):
            self.copy(step).wait_send()
        pl.when(self.mine)(lambda: self.keep().wait())
        pl.when(jnp.logical_not(self.mine))(lambda: self.copy(0).wait_send())
        for clip in range(self.clips):
            for core in range(2):
                own = jnp.logical_and(p.core * self.clips + clip == p.z, p.core == core)
                pl.when(jnp.logical_not(own))(lambda: self.arriving(clip, core).wait_recv())


class Total:
    @staticmethod
    def scratch(shape):
        return [pltpu.VMEM(shape, F32), *sem_pair(shape[0]), *sem_pair(shape[0])]

    def __init__(self, place, packed, total, scratch):
        self.place, self.packed, self.total, self.came = place, packed, total, scratch[0]
        self.to_sum, self.to_all = scratch[1:3], scratch[3:5]
        self.me = place.box(0)[2]
        self.peers = [place.box(at) for at in range(1, packed.shape[0])]

    def out(self, peer):
        f, z, at = peer
        return pltpu.make_async_remote_copy(
            src_ref=self.packed.at[at], dst_ref=self.came.at[self.me], send_sem=self.to_sum[0].at[at],
            recv_sem=self.to_sum[1].at[self.me], device_id=self.place.device(f, z), device_id_type=MESH,
        )

    def back(self, peer):
        f, z, at = peer
        return pltpu.make_async_remote_copy(
            src_ref=self.total.at[self.me], dst_ref=self.total.at[self.me], send_sem=self.to_all[0].at[at],
            recv_sem=self.to_all[1].at[self.me], device_id=self.place.device(f, z), device_id_type=MESH,
        )

    def arrived(self, sems, buffer, peer):
        f, z, at = peer
        pltpu.make_async_remote_copy(
            src_ref=buffer.at[at], dst_ref=buffer.at[at], send_sem=sems[0].at[at], recv_sem=sems[1].at[at],
            device_id=self.place.device(f, z), device_id_type=MESH,
        ).wait_recv()

    def run(self, k):
        if k == 0:
            for peer in self.peers:
                self.out(peer).start()
            self.came[self.me] = self.packed[self.me]
        elif k == 1:
            for peer in self.peers:
                self.arrived(self.to_sum, self.came, peer)
            self.total[self.me] = jnp.sum(self.came[...], axis=0)
        elif k == 2:
            for peer in self.peers:
                self.back(peer).start()
        else:
            for peer in self.peers:
                self.arrived(self.to_all, self.total, peer)
                self.out(peer).wait_send()
                self.back(peer).wait_send()


class Scatter:
    steps = 7

    @staticmethod
    def scratch(n_t, size, wide):
        half = size // 2
        return [
            pltpu.VMEM((n_t, 2, half, wide), BF16), pltpu.VMEM((n_t, 2, half, wide), BF16),
            pltpu.VMEM((n_t, half, wide), BF16), pltpu.VMEM((n_t, half, wide), BF16),
            pltpu.VMEM((n_t, size, wide), BF16), pltpu.VMEM((2, n_t, size, wide), BF16),
            pltpu.VMEM((n_t, 4, half, wide), BF16), pltpu.SemaphoreType.DMA((n_t, 4)),
            *sem_pair(n_t, 6), *sem_pair(2, n_t),
        ]

    def __init__(self, place, grads, own, scratch):
        self.place, self.grads, self.own = place, grads, own
        self.came_y, self.came_x, self.last_x, self.last_y, self.sums, self.came_z, self.held, self.load, a, b, c, d = scratch
        self.xy, self.zs = (a, b), (c, d)
        self.half = own.shape[0] // 2

    def at(self, group, half):
        return pl.ds(pl.multiple_of((2 * group + half) * self.half, 16), self.half)

    def copy(self, slot, at):
        p, g = self.place, self.grads
        by_y = at in (0, 2, 5)
        if at < 4:
            half = 0 if by_y else 1
            group = p.group_xy if at < 2 else (p.group_y if by_y else p.group_x)
            came = self.came_y if by_y else self.came_x
            src, to = g.at[slot, self.at(group, half)], came.at[slot, 1 if at < 2 else 0]
        else:
            src = self.came_x.at[slot, 1] if by_y else self.came_y.at[slot, 1]
            to = self.last_y.at[slot] if by_y else self.last_x.at[slot]
        return remote(src, to, self.xy, (slot, at), p.y() if by_y else p.x())

    def along_z(self, slot, way):
        p = self.place
        return remote(
            self.sums.at[slot], self.came_z.at[way, slot], self.zs, (way, slot), p.device(p.f, p.z + 2 * way - 1)
        )

    def over(self, rows, body):
        step = 32

        def one(i, carry):
            body(pl.multiple_of(i * step, step), step)
            return carry

        lax.fori_loop(0, rows // step, one, 0)

    def hold(self, slot, at):
        p = self.place
        rows = self.at((p.group_x, p.group_y, p.group, p.group)[at], (0, 1, 0, 1)[at])
        return pltpu.make_async_copy(self.grads.at[slot, rows], self.held.at[slot, at], self.load.at[slot, at])

    def first(self, slot):
        for at in range(4):
            self.copy(slot, at).start()
        for at in range(4):
            self.hold(slot, at).start()

    def second(self, slot):
        for at in range(2):
            self.hold(slot, at).wait()
            self.copy(slot, at).wait_recv()

        def body(at, step):
            to = pl.ds(at, step)
            for i, came in enumerate((self.came_y, self.came_x)):
                came[slot, 1, to] = add(came[slot, 1, to], self.held[slot, i, to])

        self.over(self.half, body)
        self.copy(slot, 4).start()
        self.copy(slot, 5).start()

    def third(self, slot):
        p = self.place
        for at in (2, 3, 4, 5):
            self.copy(slot, at).wait_recv()
        for at in (2, 3):
            self.hold(slot, at).wait()

        def body(at, step):
            to = pl.ds(at, step)
            for came, last, half in ((self.came_y, self.last_x, 0), (self.came_x, self.last_y, 1)):
                total = self.held[slot, 2 + half, to].astype(F32) + came[slot, 0, to].astype(F32) + last[slot, to].astype(F32)
                self.sums[slot, pl.ds(pl.multiple_of(half * self.half + at, step), step)] = total.astype(BF16)

        self.over(self.half, body)
        for way in range(2):
            step = 2 * way - 1

            @pl.when((slot - p.z) * step > 0)
            def _():
                @pl.when(p.has(p.z - step))
                def _():
                    self.along_z(slot, way).wait_recv()

                    def body(at, step):
                        to = pl.ds(at, step)
                        self.sums[slot, to] = add(self.sums[slot, to], self.came_z[way, slot, to])

                    self.over(2 * self.half, body)

                self.along_z(slot, way).start()

    def run(self, k):
        p = self.place
        n = p.n_t
        if k == 0:
            self.first(self.place.slot(0))
            self.first(self.place.slot(1))
            return
        if k <= n:
            self.second(self.place.slot(k - 1))
        if k + 1 < n:
            self.first(self.place.slot(k + 1))
        if 2 <= k <= n + 1:
            self.third(self.place.slot(k - 2))
        if k == n + 2:
            z = p.z

            def begin(at, step):
                to = pl.ds(at, step)
                self.own[to] = self.sums[z, to].astype(F32)

            self.over(2 * self.half, begin)
            for way in range(2):
                step = 2 * way - 1

                @pl.when(p.has(z - step))
                def _():
                    self.along_z(z, way).wait_recv()

                    def body(at, step):
                        to = pl.ds(at, step)
                        self.own[to] += self.came_z[way, z, to].astype(F32)

                    self.over(2 * self.half, body)

            for slot in range(n):
                for at in range(6):
                    self.copy(slot, at).wait_send()
                for way in range(2):
                    pl.when((slot - z) * (2 * way - 1) > 0)(self.along_z(slot, way).wait_send)


def hook_of(steps):
    def hook(p, pairs):
        for k, functions in steps.items():

            @pl.when(p == k)
            def _():
                for function in functions:
                    function()

    return hook


def step(job, k):
    return functools.partial(job.run, k)


def swap(place, part, came, sems):
    return pltpu.make_async_remote_copy(
        src_ref=part, dst_ref=came, send_sem=sems.at[0], recv_sem=sems.at[1],
        device_id=place.device(place.to_core, place.z), device_id_type=MESH,
    )


def row_step(m):
    return m // 4 if m % 64 == 0 else m


def over_rows(m, body):
    step = row_step(m)

    def run(i, carry):
        return body(pl.ds(pl.multiple_of(i * step, step), step), carry)

    return lambda carry: lax.fori_loop(0, m // step, run, carry)


def normal(values):
    centre = values - jnp.mean(values, axis=-1, keepdims=True)
    inverse = lax.rsqrt(jnp.mean(centre * centre, axis=-1, keepdims=True) + EPSILON)
    return centre * inverse, inverse


def norm_rows(value_at, gain, shift, normed, kept=None):
    gain_row, shift_row = gain[...], shift[...]

    def body(at, carry):
        value = value_at(at)
        if kept is not None:
            kept[at, :] = value
        normed[at, :] = (normal(value)[0] * gain_row + shift_row).astype(BF16)
        return carry

    over_rows(normed.shape[0], body)(0)


def norm_back_rows(own, came, values, gain, upstream, grad_ref, low_ref, sums):
    gain_row = gain[...]
    wide = values.shape[1]

    def body(at, carry):
        q = own[at, :].astype(F32) + came[at, :].astype(F32)
        n, inverse = normal(values[at, :].astype(F32))
        up = upstream[at, :].astype(F32)
        v = q * gain_row
        back = inverse * (v - jnp.mean(v, axis=-1, keepdims=True) - n * jnp.mean(v * n, axis=-1, keepdims=True))
        grad = up + back
        grad_ref[at, :] = grad.astype(grad_ref.dtype)
        if low_ref is not None:
            low_ref[at, :] = grad.astype(BF16)
        terms = (q * n, q, grad, up)
        return tuple(c + jnp.sum(t, axis=0, keepdims=True) for c, t in zip(carry, terms))

    totals = over_rows(values.shape[0], body)(tuple(jnp.zeros((1, wide), F32) for _ in range(4)))
    row = lax.broadcasted_iota(jnp.int32, sums.shape, 0)
    value = jnp.zeros(sums.shape, F32)
    for at, total in enumerate(totals):
        value = jnp.where(row == at, total, value)
    sums[...] = value


def lane_mask(shape, h):
    return (lax.broadcasted_iota(jnp.int32, shape, 1) // HEAD_DIM) == h


def mask_scores(scores, causal, valid):
    size = scores.shape[0]
    if causal:
        key_at = lax.broadcasted_iota(jnp.int32, scores.shape, 0)
        query_at = lax.broadcasted_iota(jnp.int32, scores.shape, 1)
        return jnp.where(key_at <= query_at, scores, MASKED)
    if valid < size:
        edge = valid // 8 * 8
        tail = scores[edge:, :]
        key_at = lax.broadcasted_iota(jnp.int32, tail.shape, 0) + edge
        return jnp.concatenate([scores[:edge, :], jnp.where(key_at < valid, tail, -jnp.inf)], axis=0)
    return scores


def attend(q_ref, k_ref, v_ref, mixed_ref, log_ref, score_buf, causal, blocks, valid, hook):
    size = k_ref.shape[0] // blocks
    pairs = q_ref.shape[1] // PAIR

    def one_pair(p, carry):
        at = pl.ds(pl.multiple_of(p * PAIR, PAIR), PAIR)
        q_all = q_ref[:, at].astype(F32) * SCALE
        result = None
        for h in range(2):
            queries = jnp.where(lane_mask(q_all.shape, h), q_all, 0.0).astype(BF16)
            top = None
            for i in range(blocks):
                rows = slice(i * size, (i + 1) * size)
                scores = mask_scores(dot(k_ref[rows, at], queries, NT), causal, valid - i * size)
                score_buf[rows, :] = scores
                now = jnp.max(scores, axis=0, keepdims=True)
                top = now if top is None else jnp.maximum(top, now)
            total, mixed = None, None
            for i in range(blocks):
                rows = slice(i * size, (i + 1) * size)
                raised = jnp.exp(score_buf[rows, :] - top)
                now = jnp.sum(raised, axis=0, keepdims=True)
                total = now if total is None else total + now
                now = dot(v_ref[rows, at], raised.astype(BF16), TN)
                mixed = now if mixed is None else mixed + now
            log_ref[2 * p + h] = jnp.broadcast_to(top + jnp.log(total), log_ref.shape[1:])
            mixed = mixed / total
            if result is None:
                result = mixed
            else:
                row = lax.broadcasted_iota(jnp.int32, mixed.shape, 0)
                result = jnp.where(row < HEAD_DIM, result, mixed)
        mixed_ref[:, at] = jnp.transpose(result).astype(BF16)
        hook(p, pairs)
        return carry

    lax.fori_loop(0, pairs, one_pair, 0)


def attend_back(q_ref, k_ref, v_ref, up_ref, mixed_ref, log_ref, dq_ref, dk_ref, dv_ref, sums, causal, blocks, valid, hook):
    size = k_ref.shape[0] // blocks
    pairs = q_ref.shape[1] // PAIR

    def one_pair(p, carry):
        at = pl.ds(pl.multiple_of(p * PAIR, PAIR), PAIR)
        q_all = q_ref[:, at].astype(F32) * SCALE
        up_all = up_ref[:, at].astype(F32)
        product = up_all * mixed_ref[:, at].astype(F32)
        queries, upstream, inner, logs = [], [], [], []
        for h in range(2):
            chosen = lane_mask(q_all.shape, h)
            queries.append(jnp.where(chosen, q_all, 0.0).astype(BF16))
            upstream.append(jnp.where(chosen, up_all, 0.0).astype(BF16))
            ones = jnp.where(lane_mask((8, PAIR), h), 1.0, 0.0)
            inner.append(
                lax.dot_general(ones, product, NT, precision=lax.Precision.HIGHEST, preferred_element_type=F32)[0:1, :]
            )
            logs.append(log_ref[2 * p + h][0:1, :])
        query_grads = [None, None]
        value_sum = None
        for i in range(blocks):
            rows = slice(i * size, (i + 1) * size)
            keys, values = k_ref[rows, at], v_ref[rows, at]
            key_grad, value_grad = None, None
            for h in range(2):
                chance = jnp.exp(mask_scores(dot(keys, queries[h], NT), causal, valid - i * size) - logs[h])
                now = dot(chance.astype(BF16), upstream[h])
                value_grad = now if value_grad is None else value_grad + now
                grad = dot(values, upstream[h], NT)
                score_grad = (chance * (grad - inner[h])).astype(BF16)
                now = dot(score_grad, queries[h])
                key_grad = now if key_grad is None else key_grad + now
                now = dot(keys, score_grad, TN)
                query_grads[h] = now if query_grads[h] is None else query_grads[h] + now
            dk_ref[rows, at] = key_grad.astype(BF16)
            dv_ref[rows, at] = value_grad.astype(BF16)
            now = jnp.sum(value_grad, axis=0, keepdims=True)
            value_sum = now if value_sum is None else value_sum + now
        row = lax.broadcasted_iota(jnp.int32, query_grads[0].shape, 0)
        query_grad = jnp.transpose(jnp.where(row < HEAD_DIM, query_grads[0], query_grads[1])) * SCALE
        dq_ref[:, at] = query_grad.astype(BF16)
        query_sum = jnp.sum(query_grad, axis=0, keepdims=True)
        row = lax.broadcasted_iota(jnp.int32, (8, PAIR), 0)
        sums[:, at] = jnp.where(row == 0, query_sum, jnp.where(row == 1, value_sum, 0.0))
        hook(p, pairs)
        return carry

    lax.fori_loop(0, pairs, one_pair, 0)


def gather_kernel(sizes, own, *refs):
    stored, whole, here, scratch = refs[:3], refs[3], refs[4:7], refs[7:]
    place = Place(sizes)
    clips = Clips(place, stored, here, scratch[:3])
    job = Gather(place, own, whole, scratch[3:])
    place.barrier()
    job.run(0)
    clips.start()
    for k in range(1, Gather.steps):
        job.run(k)
    clips.finish()


def gather(sizes, own, stored):
    n_t = sizes[1]
    return call(
        functools.partial(gather_kernel, sizes), "gather",
        [((n_t, GROUPS * own.shape[0], own.shape[1]), BF16)] + [(v.shape[1:], v.dtype) for v in stored], [own, *stored],
        scratch=Clips.scratch(len(stored)) + Gather.scratch(n_t), remote=0, anywhere=((0, 1, 2, 3), (0,)),
    )


def self_forward_kernel(
    sizes, own, start, gain, shift, bias, weights, whole, normed, qkv, mixed, logs, part, came, w_in, w_out, score_buf,
    sems, loads, *scratch,
):
    place = Place(sizes)
    job = Gather(place, own, whole, scratch)
    wide = mixed.shape[1]
    fetch(weights, w_in, [(0, 0), (1, wide), (2, 2 * wide)], loads.at[0])
    fetch(weights, w_out, [(3, 0)], loads.at[1])
    place.barrier()
    job.run(0)
    norm_rows(lambda at: start[at, :].astype(F32), gain, shift, normed)
    fetched(w_in, loads.at[0])
    fetched(w_out, loads.at[1])
    qkv[...] = (dot(normed[...], w_in[...]) + bias[...]).astype(BF16)
    job.run(1)
    q, k, v = (qkv.at[:, i * wide : (i + 1) * wide] for i in range(3))
    attend(q, k, v, mixed, logs, score_buf, True, 1, start.shape[0], hook_of({2: [step(job, 2)]}))
    part[...] = dot(mixed[...], w_out[...], NT).astype(BF16)
    job.run(3)
    exchange = swap(place, part, came, sems)
    exchange.start()
    job.run(4)
    job.run(5)
    exchange.wait()


def self_forward(sizes, own, start, gain, shift, bias, weights):
    m, d = start.shape
    n_t = sizes[1]
    wide = bias.shape[1] // 3
    heads = wide // HEAD_DIM
    return call(
        functools.partial(self_forward_kernel, sizes), "self_forward",
        [((n_t, GROUPS * own.shape[0], own.shape[1]), BF16), ((m, d), BF16), ((m, 3 * wide), BF16), ((m, wide), BF16),
         ((heads, 8, m), F32), ((m, d), BF16), ((m, d), BF16)],
        [own, start, gain, shift, bias, weights],
        scratch=[
            pltpu.VMEM((d, 3 * wide), BF16), pltpu.VMEM((d, wide), BF16), pltpu.VMEM((m, m), F32),
            pltpu.SemaphoreType.DMA((2,)), pltpu.SemaphoreType.DMA((2,)), *Gather.scratch(n_t),
        ],
        flops=2 * m * d * 4 * wide + 4 * m * m * wide * 2, remote=1, anywhere=((0, 5), (0,)),
    )


def cross_forward_kernel(
    sizes, blocks, valid, own_weights, start, own, came, branch, gain, shift, bias, bias_kv, memory, weights,
    branch_two, gain_two, shift_two, upstream, hidden_bias,
    grads, middle, normed, q, kv, mixed, logs, later, out_part, out_came, grad_part, grad_came, sums,
    whole, normed_three, out_acc, grad_acc, stage, part, part_came, w_in, w_kv, w_out, score_buf, sems, loads, stores,
    out_sems, grad_sems, *scratch,
):
    place = Place(sizes)
    job = Gather(place, own_weights, whole, scratch)
    wide = mixed.shape[1]
    fetch(weights, w_kv, [(1, 0), (2, wide)], loads.at[0])
    fetch(weights, w_in, [(0, 0)], loads.at[1])
    fetch(weights, w_out, [(3, 0)], loads.at[2])
    place.barrier()
    job.run(0)
    fetched(w_kv, loads.at[0])
    size = memory.shape[0] // blocks

    def one_block(i, carry):
        at = pl.ds(pl.multiple_of(i * size, size), size)
        kv[at, :] = (dot(memory[at, :], w_kv[...]) + bias_kv[...]).astype(BF16)
        return carry

    lax.fori_loop(0, blocks, one_block, 0)
    job.run(1)
    branch_row = branch[...]
    norm_rows(
        lambda at: start[at, :].astype(F32) + (own[at, :].astype(F32) + came[at, :].astype(F32)) + branch_row,
        gain, shift, normed, middle,
    )
    fetched(w_in, loads.at[1])
    fetched(w_out, loads.at[2])
    q[...] = (dot(normed[...], w_in[...]) + bias[...]).astype(BF16)

    attend(
        q, kv.at[:, :wide], kv.at[:, wide:], mixed, logs, score_buf, False, blocks, valid, hook_of({1: [step(job, 2)]})
    )
    part[...] = dot(mixed[...], w_out[...], NT).astype(BF16)
    exchange = swap(place, part, part_came, sems)
    job.run(3)
    exchange.start()
    out_acc[...] = jnp.zeros(out_acc.shape, F32)
    grad_acc[...] = jnp.zeros(grad_acc.shape, F32)
    exchange.wait()
    branch_two_row = branch_two[...]
    norm_rows(
        lambda at: middle[at, :] + (part[at, :].astype(F32) + part_came[at, :].astype(F32)) + branch_two_row,
        gain_two, shift_two, normed_three, later,
    )
    slots, width = place.n_t, hidden_bias.shape[2]
    order = [place.slot(slots - 1 - i) for i in range(slots)]

    def store(i, slot):
        return pltpu.make_async_copy(stage.at[lax.rem(i, 2)], grads.at[slot], stores.at[lax.rem(i, 2)])

    def one_slot(i, carry):
        slot = order[-1]
        for at in range(slots - 1):
            slot = jnp.where(i == at, order[at], slot)
        pl.when(i == slots - 1)(step(job, 4))
        job.complete(slot)
        pl.when(i >= 2)(lambda: store(i, slot).wait())
        expanded = dot(normed_three[...], whole[slot, :, :width]) + hidden_bias[slot]
        phi = 0.5 * (1.0 + lax.erf(expanded * (0.5**0.5)))
        activated = (expanded * phi).astype(BF16)
        density = jnp.exp(expanded * expanded * -0.5) * ((2.0 * math.pi) ** -0.5)
        slope = phi + expanded * density
        expanded_grad = dot(upstream[...], whole[slot, :, width:]) * slope
        expanded_low = expanded_grad.astype(BF16)
        sums[slot] = jnp.broadcast_to(jnp.sum(expanded_grad, axis=0, keepdims=True), sums.shape[1:])
        out_acc[...] += dot(activated, whole[slot, :, width:], NT)
        grad_acc[...] += dot(expanded_low, whole[slot, :, :width], NT)
        held = stage.at[lax.rem(i, 2)]
        held[:, :width] = dot(normed_three[...], expanded_low, TN).astype(BF16)
        held[:, width:] = dot(upstream[...], activated, TN).astype(BF16)
        store(i, slot).start()
        return carry

    lax.fori_loop(0, slots, one_slot, 0)
    grad_part[...] = grad_acc[...].astype(BF16)
    out_part[...] = out_acc[...].astype(BF16)
    job.run(5, False)
    grad_exchange = swap(place, grad_part, grad_came, grad_sems)
    out_exchange = swap(place, out_part, out_came, out_sems)
    grad_exchange.start()
    out_exchange.start()
    store(0, 0).wait()
    store(1, 0).wait()
    grad_exchange.wait()
    out_exchange.wait()


def cross_forward(
    sizes, own_weights, start, own, came, branch, gain, shift, bias, bias_kv, memory, weights, branch_two, gain_two,
    shift_two, upstream, hidden_bias, blocks, valid,
):
    m, d = start.shape
    n_t = sizes[1]
    n, wide = memory.shape[0], bias.shape[1]
    feed_wide = own_weights.shape[1]
    heads = wide // HEAD_DIM
    return call(
        functools.partial(cross_forward_kernel, sizes, blocks, valid), "cross_and_feed",
        [((n_t, d, feed_wide), BF16), ((m, d), F32), ((m, d), BF16),
         ((m, wide), BF16), ((n, 2 * wide), BF16), ((m, wide), BF16), ((heads, 8, m), F32), ((m, d), F32)]
        + [((m, d), BF16)] * 4 + [((n_t, 8, feed_wide // 2), F32)],
        [own_weights, start, own, came, branch, gain, shift, bias, bias_kv, memory, weights, branch_two, gain_two,
         shift_two, upstream, hidden_bias],
        scratch=[
            pltpu.VMEM((n_t, GROUPS * own_weights.shape[0], feed_wide), BF16), pltpu.VMEM((m, d), BF16),
            pltpu.VMEM((m, d), F32), pltpu.VMEM((m, d), F32), pltpu.VMEM((2, d, feed_wide), BF16),
            pltpu.VMEM((m, d), BF16), pltpu.VMEM((m, d), BF16),
            pltpu.VMEM((d, wide), BF16), pltpu.VMEM((d, 2 * wide), BF16), pltpu.VMEM((d, wide), BF16),
            pltpu.VMEM((n, m), F32), pltpu.SemaphoreType.DMA((2,)), pltpu.SemaphoreType.DMA((3,)),
            *[pltpu.SemaphoreType.DMA((2,))] * 3, *Gather.scratch(n_t),
        ],
        flops=6 * m * d * feed_wide * n_t + 2 * m * d * 2 * wide + 4 * n * d * wide + 4 * m * n * wide * 2, remote=2, anywhere=((0, 10), (0,)),
    )


def cross_back_kernel(
    sizes, blocks, valid, own, came, later, gain, upstream, q, kv, mixed, logs, weights, normed, memory, feed_grads,
    out_part, out_came, branch,
    output, memory_came, later_grad, sums, head_sums, part, part_came, grads, keep, feed_own,
    later_low, dq, dkv, w_one, w_two, w_kv, mixed_grad, piece, out_half, send, sems, memory_sems, loads, *scratch,
):
    place = Place(sizes)
    spread = Spread(place, out_half, output, scratch[:5])
    job = Scatter(place, feed_grads, feed_own, scratch[5:])
    wide = q.shape[1]
    n, d = memory.shape
    fetch(weights, w_one, [(3, 0)], loads.at[0])
    fetch(weights, w_two, [(0, 0)], loads.at[1])
    fetch(weights, w_kv, [(1, 0), (2, wide)], loads.at[2])
    place.barrier()
    job.run(0)
    out_wide = out_half.shape[1]
    out_at = pl.ds(pl.multiple_of(place.core * out_wide, out_wide), out_wide)
    branch_half = branch[:, out_at]

    def one_row(at, carry):
        total = later[at, out_at] + (out_part[at, out_at].astype(F32) + out_came[at, out_at].astype(F32)) + branch_half
        out_half[at, :] = total.astype(BF16)
        return carry

    over_rows(out_half.shape[0], one_row)(0)
    norm_back_rows(own, came, later, gain, upstream, later_grad, later_low, sums)
    spread.run(0)
    for at, buffer in enumerate((w_one, w_two, w_kv)):
        fetched(buffer, loads.at[at])
    mixed_grad[...] = dot(later_low[...], w_one[...]).astype(BF16)
    attend_back(
        q, kv.at[:, :wide], kv.at[:, wide:], mixed_grad, mixed, logs, dq, dkv.at[:, :wide], dkv.at[:, wide:],
        head_sums, False, blocks, valid, hook_of({0: [step(job, 1), step(spread, 1)], 2: [step(job, 2), step(spread, 2)]}),
    )
    part[...] = dot(dq[...], w_two[...], NT).astype(BF16)
    unfill(grads, 3, dot(later_low[...], mixed[...], TN).astype(BF16))
    exchange = swap(place, part, part_came, sems)
    exchange.start()
    unfill(grads, 0, dot(normed[...], dq[...], TN).astype(BF16))
    job.run(3)
    spread.run(3)
    size = n // blocks
    own_half = pl.ds(pl.multiple_of(place.core * (d // 2), d // 2), d // 2)
    other_half = pl.ds(pl.multiple_of((1 - place.core) * (d // 2), d // 2), d // 2)

    def one_block(i, carry):
        rows = pl.ds(pl.multiple_of(i * size, size), size)
        piece[...] = dot(dkv[rows, :], w_kv[...], NT).astype(BF16)
        keep[rows, :] = piece[:, own_half]
        send[rows, :] = piece[:, other_half]
        return carry

    lax.fori_loop(0, blocks, one_block, 0)
    spread.run(4)
    memory_exchange = swap(place, send, memory_came, memory_sems)
    memory_exchange.start()
    unfill(grads, 1, dot(memory[...], dkv[:, :wide], TN).astype(BF16))
    unfill(grads, 2, dot(memory[...], dkv[:, wide:], TN).astype(BF16))
    for k in (4, 5, 6):
        job.run(k)
    spread.run(5)
    exchange.wait()
    memory_exchange.wait()


def cross_back(
    sizes, own, came, later, gain, upstream, q, kv, mixed, logs, weights, normed, memory, feed_grads, out_part, out_came,
    branch, clips, blocks, valid,
):
    m, d = later.shape
    n_t = sizes[1]
    n, wide = memory.shape[0], q.shape[1]
    size, feed_wide = d // GROUPS, feed_grads.shape[2]
    return call(
        functools.partial(cross_back_kernel, sizes, blocks, valid), "cross_back",
        [((clips, m, d), BF16), ((n, d // 2), BF16), ((m, d), F32), ((8, d), F32), ((8, wide), F32), ((m, d), BF16),
         ((m, d), BF16), ((n_t, d, 4 * PAIR), BF16), ((n, d // 2), BF16), ((size, feed_wide), F32)],
        [own, came, later, gain, upstream, q, kv, mixed, logs, weights, normed, memory, feed_grads, out_part, out_came,
         branch],
        scratch=[
            pltpu.VMEM((m, d), BF16), pltpu.VMEM((m, wide), BF16), pltpu.VMEM((n, 2 * wide), BF16),
            pltpu.VMEM((d, wide), BF16), pltpu.VMEM((d, wide), BF16), pltpu.VMEM((d, 2 * wide), BF16),
            pltpu.VMEM((m, wide), BF16), pltpu.VMEM((n // blocks, d), BF16), pltpu.VMEM((m, d // 2), BF16),
            pltpu.VMEM((n, d // 2), BF16), pltpu.SemaphoreType.DMA((2,)), pltpu.SemaphoreType.DMA((2,)),
            pltpu.SemaphoreType.DMA((3,)), *Spread.scratch(clips), *Scatter.scratch(n_t, size, feed_wide),
        ],
        flops=8 * m * d * wide + 10 * m * n * wide * 2 + 8 * n * d * wide, remote=3, anywhere=((9, 12), (0, 1)),
    )


def self_back_kernel(
    sizes, frames, own, came, middle, gain, upstream, qkv, mixed, logs, weights, normed, cross_grads, keep, keep_came,
    start, start_gain,
    whole, half_grad, start_sums, sums, head_sums, grads, cross_own,
    middle_grad, grad, part, part_came, middle_low, dqkv, w_in, w_out, mixed_grad, memory_sum, sems, loads, *scratch,
):
    place = Place(sizes)
    memory_job = Frames(place, memory_sum, whole, frames, scratch[:3])
    job = Scatter(place, cross_grads, cross_own, scratch[3:])
    wide = mixed.shape[1]
    fetch(weights, w_in, [(0, 0), (1, wide), (2, 2 * wide)], loads.at[0])
    fetch(weights, w_out, [(3, 0)], loads.at[1])
    place.barrier()
    job.run(0)

    def one_row(at, carry):
        memory_sum[at, :] = add(keep[at, :], keep_came[at, :])
        return carry

    over_rows(memory_sum.shape[0], one_row)(0)
    fetched(w_in, loads.at[0])
    fetched(w_out, loads.at[1])
    for at in (1, 3, 0):
        memory_job.start(at)
    norm_back_rows(own, came, middle, gain, upstream, middle_grad, middle_low, sums)
    job.run(1)
    mixed_grad[...] = dot(middle_low[...], w_out[...]).astype(BF16)
    cut = [slice(i * wide, (i + 1) * wide) for i in range(3)]
    attend_back(
        *(qkv.at[:, c] for c in cut), mixed_grad, mixed, logs, *(dqkv.at[:, c] for c in cut), head_sums, True, 1,
        middle.shape[0], hook_of({0: [step(job, 2)], 2: [step(job, 3)]}),
    )
    part[...] = dot(dqkv[...], w_in[...], NT).astype(BF16)
    job.run(4)
    exchange = swap(place, part, part_came, sems)
    exchange.start()
    unfill(grads, 3, dot(middle_low[...], mixed[...], TN).astype(BF16))
    unfill(grads, 0, dot(normed[...], dqkv[:, cut[0]], TN).astype(BF16))
    job.run(5)
    memory_job.start(2)
    exchange.wait()
    norm_back_rows(part, part_came, start, start_gain, middle_grad, grad, None, start_sums)
    half = half_grad.shape[1]
    half_grad[...] = grad[:, pl.ds(pl.multiple_of(place.core * half, half), half)]
    for which in (1, 2):
        unfill(grads, which, dot(normed[...], dqkv[:, cut[which]], TN).astype(BF16))
    job.run(6)
    memory_job.finish()


def self_back(
    sizes, own, came, middle, gain, upstream, qkv, mixed, logs, weights, normed, cross_grads, keep, keep_came, start, start_gain,
    clips, frames,
):
    m, d = middle.shape
    n_t = sizes[1]
    wide = mixed.shape[1]
    size, cross_wide = d // GROUPS, cross_grads.shape[2]
    return call(
        functools.partial(self_back_kernel, sizes, frames), "self_back",
        [((clips, (frames + 30) // 16 * 16, d), BF16), ((m, d // 2), BF16), ((8, d), F32), ((8, d), F32), ((8, wide), F32),
         ((n_t, d, 4 * PAIR), BF16), ((size, cross_wide), F32)],
        [own, came, middle, gain, upstream, qkv, mixed, logs, weights, normed, cross_grads, keep, keep_came,
         start, start_gain],
        scratch=[
            pltpu.VMEM((m, d), F32), *[pltpu.VMEM((m, d), BF16)] * 4,
            pltpu.VMEM((m, 3 * wide), BF16), pltpu.VMEM((d, 3 * wide), BF16),
            pltpu.VMEM((d, wide), BF16), pltpu.VMEM((m, wide), BF16), pltpu.VMEM(keep.shape, BF16),
            pltpu.SemaphoreType.DMA((2,)), pltpu.SemaphoreType.DMA((2,)), *Frames.scratch(n_t, clips), *Scatter.scratch(n_t, size, cross_wide),
        ],
        flops=16 * m * d * wide + 10 * m * m * wide * 2, remote=4, anywhere=((8, 10), (0,)),
    )


def finish_kernel(sizes, self_grads, half_grad, packed, whole, total, self_own, *scratch):
    place = Place(sizes)
    spread = Spread(place, half_grad, whole, scratch[:5])
    all_sum = Total(place, packed, total, scratch[5:10])
    job = Scatter(place, self_grads, self_own, scratch[10:])
    place.barrier(True)
    all_sum.run(0)
    spread.run(0)
    job.run(0)
    spread.run(1)
    job.run(1)
    all_sum.run(1)
    spread.run(2)
    job.run(2)
    all_sum.run(2)
    spread.run(3)
    job.run(3)
    spread.run(4)
    for k in (4, 5, 6):
        job.run(k)
    spread.run(5)
    all_sum.run(3)


def finish(sizes, half_grad, self_grads, packed, clips):
    m, half = half_grad.shape
    n_t, d, wide = self_grads.shape
    size = d // GROUPS
    return call(
        functools.partial(finish_kernel, sizes), "finish",
        [((clips, m, 2 * half), BF16), (packed.shape, F32), ((size, wide), F32)], [self_grads, half_grad, packed],
        scratch=[*Spread.scratch(clips), *Total.scratch(packed.shape), *Scatter.scratch(n_t, size, wide)],
        remote=5, anywhere=((0,), (0,)),
    )


def flip(x, bit, size):
    return lax.ppermute(x, "fsdp", [(i, i ^ (1 << bit)) for i in range(size)])


def half(x, index, axis):
    size = x.shape[axis] // 2
    return lax.dynamic_slice_in_dim(x, index * size, size, axis=axis)


def add(a, b):
    return (a.astype(F32) + b.astype(F32)).astype(BF16)


def on_device(
    n_f, n_t,
    tokens, encoder, cotangent, self_weights, self_biases, self_output, cross_query, cross_memory,
    cross_biases, cross_output, hidden_weight, hidden_bias, reduce_weight, norm_gains, norm_shifts, branch_biases,
):
    bits = n_f.bit_length() - 1
    x_bit, y_bit = bits - 2, bits - 1
    f = lax.axis_index("fsdp")
    z = lax.axis_index("tensor")
    core = f % 2
    sizes = (n_f, n_t)
    length, d = tokens.shape[1], tokens.shape[2]
    frames = encoder.shape[1]
    own_clips = tokens.shape[0]
    assert own_clips * 2 == n_t == 4 and bits >= 3
    per = d // n_f
    units_here = hidden_bias.shape[1]
    units = units_here * n_f
    heads_here = self_biases.shape[2]
    inner = n_f // GROUPS

    def begin(weights, extra=None, waits=()):
        keep = jnp.concatenate([half(w, core, 1) for w in weights], axis=1)
        send = jnp.concatenate([half(w, 1 - core, 1) for w in weights], axis=1)
        width = keep.shape[1]
        now, more = keep, extra
        for bit in range(bits - 2):
            rows = now.shape[0]
            out = send if bit == 0 else now
            if more is not None:
                out = jnp.concatenate([out, more.reshape(-1, width)])
            if waits:
                out = after(out, *waits)
            came = flip(out, bit, n_f)
            low = (f >> bit) % 2 == 0
            a, b = now, came[:rows]
            now = jnp.where(low, jnp.concatenate([a, b]), jnp.concatenate([b, a]))
            if more is not None:
                b = came[rows:]
                more = jnp.where(low, jnp.concatenate([more, b]), jnp.concatenate([b, more]))
        return now if more is None else jnp.concatenate([now, more])

    small = jnp.concatenate(
        [v.reshape(-1) for v in (norm_gains, norm_shifts, branch_biases, hidden_bias, self_biases, cross_biases)]
    )
    lanes = 4 * PAIR
    small_rows = -(-small.shape[0] // (16 * lanes)) * 16
    small = jnp.pad(small, (0, small_rows * lanes - small.shape[0])).reshape(small_rows, lanes)

    first = begin([self_weights[0], self_weights[1], self_weights[2], self_output.T], small)
    second = begin([cross_query, cross_memory[0], cross_memory[1], cross_output.T])
    third = begin([hidden_weight, reduce_weight.T])
    wide_half = units // 2
    pad = -(-frames // 512) * 512 - frames
    w_self, start, upstream, memory = gather(
        sizes, first, [tokens, cotangent, jnp.pad(encoder, ((0, 0), (0, pad), (0, 0)))]
    )

    rows = d // GROUPS
    table = w_self.reshape(n_t, GROUPS, -1, lanes)[:, :, rows:].reshape(n_t, n_f, -1).astype(F32)
    features = table[0, :, : 9 * per].reshape(n_f, 9, per).transpose(1, 0, 2).reshape(9, d)
    at = 9 * per
    hidden_slots = half(table[:, :, at : at + units_here].reshape(n_t, 1, units), core, 2)
    at += units_here

    def head_slots(at):
        v = table[:, :, at : at + 2 * heads_here].reshape(n_t, n_f, 2, heads_here).transpose(2, 0, 1, 3)
        return half(v.reshape(2, n_t, n_f * heads_here), core, 2).reshape(2, 1, -1)

    self_bias = head_slots(at)
    cross_bias = head_slots(at + 2 * heads_here)
    zero = jnp.zeros_like(self_bias[0])
    qkv_bias = jnp.concatenate([self_bias[0], zero, self_bias[1]], axis=1)
    kv_bias = jnp.concatenate([zero, cross_bias[1]], axis=1)
    gain, shift, branch = ([features[3 * i + j : 3 * i + j + 1] for j in range(3)] for i in range(3))

    part_frames = frames // n_t

    def scatter_end(now):
        for bit in range(bits - 3, 0, -1):
            up = (f >> bit) % 2
            now = half(now, up, 0) + flip(half(now, 1 - up, 0).astype(BF16), bit, n_f).astype(F32)
        return half(now, core, 0), flip(half(now, 1 - core, 0), 0, n_f)

    def unpack(shares, widths):
        keep, came = shares
        result, at = [], 0
        for width in widths:
            a, b = keep[:, at : at + width], came[:, at : at + width]
            result.append(jnp.where(core == 0, jnp.concatenate([a, b], 1), jnp.concatenate([b, a], 1)))
            at += width
        return result

    w_cross, normed_one, qkv, mixed_one, log_one, part, came = self_forward(
        sizes, second, start, gain[0], shift[0], qkv_bias, w_self
    )
    (
        g_feed, middle, normed_two, cross_q, kv, mixed_two, log_two, later, out_part, out_came, part, came, hidden_sums,
    ) = cross_forward(
        sizes, third, start, part, came, branch[0], gain[1], shift[1], cross_bias[0], kv_bias, memory, w_cross, branch[1],
        gain[2], shift[2], upstream, hidden_slots, n_t, frames,
    )

    output, memory_came, later_grad, sums_three, cross_sums, part, part_came, g_cross, memory_keep, feed_own = cross_back(
        sizes, part, came, later, gain[2], upstream, cross_q, kv, mixed_two, log_two, w_cross, normed_two, memory,
        g_feed, out_part, out_came, branch[2], own_clips, n_t, frames,
    )
    memory_share, half_grad, sums_one, sums_two, self_sums, g_self, cross_own = self_back(
        sizes, part, part_came, middle, gain[1], later_grad, qkv, mixed_one, log_one, w_self, normed_one, g_cross,
        memory_keep, memory_came, start, gain[0], own_clips, part_frames,
    )

    lead = jnp.where(core == 0, 1.0, 0.0).astype(F32)
    feature_sums = jnp.stack(
        [sums_one[0], sums_two[0], sums_three[0], sums_one[1], sums_two[1], sums_three[1],
         sums_two[2], sums_three[2], sums_three[3]]
    ) * lead

    def from_slots(v):
        natural = jnp.swapaxes(v, 0, 1)
        wide = jnp.zeros((*natural.shape[:2], 2 * natural.shape[2]), F32)
        return lax.dynamic_update_slice(wide, natural, (0, 0, core * natural.shape[2]))

    def by_slot(v):
        return v[:2].reshape(2, n_t, -1).transpose(1, 0, 2)

    unit_sums = [from_slots(hidden_sums[:, :1]), from_slots(by_slot(self_sums)), from_slots(by_slot(cross_sums))]
    packed = jnp.concatenate([feature_sums.reshape(-1)] + [u.reshape(-1) for u in unit_sums])
    boxes = -(-packed.size // (32 * 1024))
    packed = jnp.pad(packed.reshape(-1), (0, boxes * 32 * 1024 - packed.size)).reshape(32, 8 * boxes, 128)
    tokens_grad, packed, self_own = finish(sizes, half_grad, g_self, packed, own_clips)
    for bit in range(1, bits - 2):
        packed = packed + flip(packed, bit, n_f)
    packed = packed.reshape(-1)
    feature_share = lax.dynamic_slice(packed[: 9 * d].reshape(9, d), (0, f * per), (9, per))

    def unit_share(at, count, total):
        block = packed[at : at + count * n_t * total].reshape(count, n_t, total)
        return lax.dynamic_slice(block, (0, z, f * (total // n_f)), (count, 1, total // n_f))

    at = 9 * d
    hidden_bias_share = unit_share(at, 1, units)[0]
    at += n_t * units
    self_bias_share = unit_share(at, 2, heads_here * n_f)
    at += 2 * n_t * heads_here * n_f
    cross_bias_share = unit_share(at, 2, heads_here * n_f)

    hidden_share, reduce_t = unpack(scatter_end(feed_own), [wide_half, wide_half])
    cq_share, ck_share, cv_share, cross_out_t = unpack(scatter_end(cross_own), [PAIR] * 4)
    q_share, k_share, v_share, self_out_t = unpack(scatter_end(self_own), [PAIR] * 4)

    memory_share = lax.dynamic_slice_in_dim(memory_share, part_frames * z % 16, part_frames, axis=1)

    return (
        output,
        tokens_grad,
        memory_share,
        jnp.stack([q_share, k_share, v_share]),
        self_bias_share,
        self_out_t.T,
        cq_share,
        jnp.stack([ck_share, cv_share]),
        cross_bias_share,
        cross_out_t.T,
        hidden_share,
        hidden_bias_share,
        reduce_t.T,
        feature_share[0:3],
        feature_share[3:6],
        feature_share[6:9],
    )


def solution(mesh):
    n_f, n_t = mesh.shape["fsdp"], mesh.shape["tensor"]
    clips = P("fsdp", None, None)
    stacked = P(None, "fsdp", "tensor")
    biases = P(None, "tensor", "fsdp")
    up, down, rows = P("fsdp", "tensor"), P("tensor", "fsdp"), P(None, "fsdp")
    return jax.shard_map(
        functools.partial(on_device, n_f, n_t),
        mesh=mesh,
        in_specs=(
            clips, clips, clips, stacked, biases, down, up, stacked, biases, down, up, down, down, rows, rows, rows,
        ),
        out_specs=(
            clips, clips, P("fsdp", "tensor", None), stacked, biases, down, up, stacked, biases, down, up, down,
            down, rows, rows, rows,
        ),
        check_vma=False,
    )
```

```python
import functools
import math

import jax
import jax.numpy as jnp
from jax import lax
from jax.experimental import pallas as pl
from jax.experimental.pallas import tpu as pltpu
from jax.sharding import PartitionSpec as P

HEAD_DIM = 64
PAIR = 2 * HEAD_DIM
GROUPS = 4
EPSILON = 1e-05
MASKED = -1e9
SCALE = HEAD_DIM**-0.5
F32 = jnp.float32
BF16 = jnp.bfloat16
VMEM_LIMIT = 63 * 1024 * 1024
MESH = pl.DeviceIdType.MESH
NT = (((1,), (1,)), ((), ()))
TN = (((0,), (0,)), ((), ()))


def call(kernel, name, outs, args, scratch=(), flops=0, grid=None, specs=None, out_specs=None, remote=None, anywhere=((), ())):
    out_shape = [jax.ShapeDtypeStruct(shape, dtype) for shape, dtype in outs]
    moved = sum(a.size * a.dtype.itemsize for a in args) + sum(
        math.prod(o.shape) * jnp.dtype(o.dtype).itemsize for o in out_shape
    )
    extra = {}
    if grid is None:
        here, there = pl.BlockSpec(memory_space=pltpu.VMEM), pl.BlockSpec(memory_space=pl.ANY)
        extra["in_specs"] = [there if i in anywhere[0] else here for i in range(len(args))]
        extra["out_specs"] = [there if i in anywhere[1] else here for i in range(len(outs))]
    else:
        extra["grid"] = grid
        extra["in_specs"], extra["out_specs"] = specs(block_whole), out_specs(block_whole)
    if remote is None:
        params = pltpu.CompilerParams(vmem_limit_bytes=VMEM_LIMIT)
    else:
        params = pltpu.CompilerParams(vmem_limit_bytes=VMEM_LIMIT, collective_id=remote, has_side_effects=True)
    return pl.pallas_call(
        kernel,
        name=name,
        out_shape=out_shape,
        scratch_shapes=list(scratch),
        compiler_params=params,
        cost_estimate=pl.CostEstimate(flops=int(flops), bytes_accessed=int(moved), transcendentals=0),
        **extra,
    )(*args)


def block_whole(shape):
    return pl.BlockSpec(shape, lambda *_: (0,) * len(shape))


def dot(a, b, dims=None):
    if dims is None:
        return jnp.dot(a, b, preferred_element_type=F32)
    return lax.dot_general(a, b, dims, preferred_element_type=F32)


def fetch(weights, buffer, columns, sem):
    rows, held = buffer.shape[0] // GROUPS, weights.shape[1] // GROUPS
    parts = [(0, 0, buffer.shape[0])] if rows == held else [(g * held, g * rows, rows) for g in range(GROUPS)]
    for s in range(weights.shape[0]):
        for src, to, size in parts:
            for which, at in columns:
                pltpu.make_async_copy(
                    weights.at[s, src : src + size, which * PAIR : (which + 1) * PAIR],
                    buffer.at[to : to + size, at + s * PAIR : at + (s + 1) * PAIR], sem,
                ).start()


def fetched(buffer, sem):
    pltpu.make_async_copy(buffer, buffer, sem).wait()


def unfill(grads, which, value):
    for s in range(grads.shape[0]):
        grads[s, :, which * PAIR : (which + 1) * PAIR] = value[:, s * PAIR : (s + 1) * PAIR]


class Place:
    def __init__(self, sizes):
        n_f, self.n_t = sizes
        self.x_size, self.y_size = n_f // 4, n_f // 2
        self.f, self.z = lax.axis_index("fsdp"), lax.axis_index("tensor")
        self.core = self.f % 2
        self.group = self.f // self.x_size
        x, y = self.group % 2, self.group // 2
        self.to_x = self.f + (1 - 2 * x) * self.x_size
        self.to_y = self.f + (1 - 2 * y) * self.y_size
        self.to_core = self.f + 1 - 2 * self.core
        self.group_x = self.group + 1 - 2 * x
        self.group_y = self.group + 2 - 4 * y
        self.group_xy = 3 - self.group

    def device(self, f, z):
        return {"fsdp": f, "tensor": z}

    def x(self):
        return self.device(self.to_x, self.z)

    def y(self):
        return self.device(self.to_y, self.z)

    def box(self, at):
        core, x, y, step = at % 2, at // 2 % 2, at // 4 % 2, at // 8
        f, place = self.f, 2 * self.group + self.core
        if core:
            f, place = f + 1 - 2 * self.core, place + 1 - 2 * self.core
        if x:
            f, place = f + self.to_x - self.f, place + 2 * (self.group_x - self.group)
        if y:
            f, place = f + self.to_y - self.f, place + 2 * (self.group_y - self.group)
        z = (self.z, self.z + 1 - 2 * lax.rem(self.z, 2), self.z + 2 - 4 * (self.z // 2), 3 - self.z)[step]
        return f, z, place * self.n_t + z

    def barrier(self, all_of_box=False):
        sem = pltpu.get_barrier_semaphore()
        if all_of_box:
            peers = [self.box(at)[:2] for at in range(1, 8 * self.n_t)]
        else:
            peers = [(self.to_x, self.z), (self.to_y, self.z), (self.to_core, self.z)]
            for step in range(1, self.n_t):
                z = lax.rem(self.z + step, self.n_t)
                peers += [(self.f, z), (self.to_core, z)]
        for f, z in peers:
            pl.semaphore_signal(sem, inc=1, device_id=self.device(f, z), device_id_type=MESH)
        pl.semaphore_wait(sem, len(peers))

    def slot(self, k):
        z, last = self.z, self.n_t - 1
        low = z * 2 <= last
        far, near = jnp.where(low, last, 0), jnp.where(low, 0, last)
        inward = jnp.where(low, 1, -1)
        if k == 0:
            return far
        if k == last:
            return z
        if k == last - 1:
            return z + inward
        return jnp.where(jnp.logical_or(z == 0, z == last), z + 2 * inward, near)

    def has(self, z):
        return jnp.logical_and(z >= 0, z < self.n_t)


def remote(src, dst, sems, at, device):
    return pltpu.make_async_remote_copy(
        src_ref=src, dst_ref=dst, send_sem=sems[0].at[at], recv_sem=sems[1].at[at], device_id=device, device_id_type=MESH
    )


def sem_pair(*shape):
    return [pltpu.SemaphoreType.DMA(shape), pltpu.SemaphoreType.DMA(shape)]


class Gather:
    steps = 6

    @staticmethod
    def scratch(n_t):
        return [
            pltpu.SemaphoreType.DMA((2, n_t)), pltpu.SemaphoreType.DMA((n_t,)),
            *sem_pair(n_t, 6), pltpu.SemaphoreType.DMA,
        ]

    def __init__(self, place, own, whole, scratch):
        self.place, self.own, self.whole = place, own, whole
        self.z_send, self.z_recv, s, r, self.local = scratch
        self.xy = (s, r)

    def rows(self, slot, group, half=None):
        size = self.own.shape[0]
        if half is None:
            return self.whole.at[slot, pl.ds(pl.multiple_of(group * size, 16), size)]
        return self.whole.at[slot, pl.ds(pl.multiple_of(group * size + half * (size // 2), 16), size // 2)]

    def along_z(self, slot, step, mine=False):
        p = self.place
        to = self.rows(slot, p.group)
        return pltpu.make_async_remote_copy(
            src_ref=self.own if mine else to, dst_ref=to, send_sem=self.z_send.at[(step + 1) // 2, slot],
            recv_sem=self.z_recv.at[slot], device_id=p.device(p.f, p.z + step), device_id_type=MESH,
        )

    def copy(self, slot, at, mine=False):
        p, size = self.place, self.own.shape[0]
        if at < 4:
            half = (0, 1, 1, 0)[at]
            to = self.rows(slot, p.group, half)
            src = self.own.at[pl.ds(half * (size // 2), size // 2)] if mine else to
        else:
            src = to = self.rows(slot, p.group_y, 1) if at == 4 else self.rows(slot, p.group_x, 0)
        return remote(src, to, self.xy, (slot, at), p.x() if at in (0, 1, 4) else p.y())

    def send_xy(self, slot, mine=False):
        for at in (0, 2, 1, 3):
            self.copy(slot, at, mine).start()

    def forward_xy(self, slot):
        self.copy(slot, 0).wait_recv()
        self.copy(slot, 5).start()
        self.copy(slot, 2).wait_recv()
        self.copy(slot, 4).start()

    def arrived(self, r, act):
        p = self.place
        for step in (-1, 1):
            slot = p.z + step * r
            pl.when(p.has(slot))(functools.partial(act, slot, step))

    def complete(self, slot):
        for at in (1, 3, 4, 5):
            self.copy(slot, at).wait_recv()

    def run(self, k, arrivals=True):
        p = self.place
        if k == 0:
            for step in (-1, 1):
                pl.when(p.has(p.z + step))(lambda step=step: self.along_z(p.z, step, True).start())
            self.send_xy(p.z, True)
            pltpu.make_async_copy(self.own, self.rows(p.z, p.group), self.local).start()
            return
        if k <= 3:

            def passed(slot, step):
                copy = self.along_z(slot, -step)
                copy.wait_recv()
                pl.when(p.has(p.z - step))(copy.start)
                self.send_xy(slot)

            self.arrived(k, passed)
        if k == 1:
            self.forward_xy(p.z)
            pltpu.make_async_copy(self.own, self.rows(p.z, p.group), self.local).wait()
        elif k <= 4:
            self.arrived(k - 1, lambda slot, step: self.forward_xy(slot))
        else:
            for slot in range(p.n_t):
                if arrivals:
                    self.complete(slot)
                for at in range(6):
                    self.copy(slot, at).wait_send()
                for step in (-1, 1):
                    sent = jnp.logical_and(p.has(p.z + step), (p.z - slot) * step >= 0)
                    pl.when(sent)(self.along_z(slot, step).wait_send)


class Clips:
    @staticmethod
    def scratch(count):
        return [*sem_pair(count), pltpu.SemaphoreType.DMA((count,))]

    def __init__(self, place, stored, here, scratch):
        self.place, self.pairs, self.sems, self.local = place, list(zip(stored, here)), scratch[:2], scratch[2]

    def copies(self, i, local):
        p, (stored, here) = self.place, self.pairs[i]
        src = stored.at[lax.rem(p.z, stored.shape[0])]
        if local:
            return pltpu.make_async_copy(src, here, self.local.at[i])
        return remote(src, here, self.sems, i, p.device(p.to_core, p.z))

    def owner(self):
        p = self.place
        return p.z // self.pairs[0][0].shape[0] == p.core

    def start(self):
        @pl.when(self.owner())
        def _():
            for i in range(len(self.pairs)):
                self.copies(i, True).start()
                self.copies(i, False).start()

    def finish(self):
        @pl.when(self.owner())
        def _():
            for i in range(len(self.pairs)):
                self.copies(i, True).wait()
                self.copies(i, False).wait_send()

        @pl.when(jnp.logical_not(self.owner()))
        def _():
            for i in range(len(self.pairs)):
                self.copies(i, False).wait_recv()


class Spread:
    steps = 6

    @staticmethod
    def scratch(clips):
        return [pltpu.SemaphoreType.DMA, *sem_pair(1), pltpu.SemaphoreType.DMA((2, clips)), pltpu.SemaphoreType.DMA((clips,))]

    def __init__(self, place, half, whole, scratch):
        self.place, self.half, self.whole = place, half, whole
        self.local, a, b, self.z_send, self.z_recv = scratch
        self.halves = (a, b)
        self.clips = whole.shape[0]
        self.mine = place.z // self.clips == place.core

    def columns(self, core):
        wide = self.half.shape[1]
        return self.whole.at[lax.rem(self.place.z, self.clips), :, pl.ds(pl.multiple_of(core * wide, 128), wide)]

    def to_owner(self, core):
        p = self.place
        return remote(self.half, self.columns(core), self.halves, 0, p.device(p.to_core, p.z))

    def along_z(self, z, step):
        p = self.place
        clip = lax.rem(z, self.clips)
        return pltpu.make_async_remote_copy(
            src_ref=self.whole.at[clip], dst_ref=self.whole.at[clip], send_sem=self.z_send.at[(step + 1) // 2, clip],
            recv_sem=self.z_recv.at[clip], device_id=p.device(p.f, p.z + step), device_id_type=MESH,
        )

    def run(self, k):
        p = self.place
        if k == 0:
            keep = pltpu.make_async_copy(self.half, self.columns(p.core), self.local)
            pl.when(self.mine)(keep.start)
            pl.when(jnp.logical_not(self.mine))(lambda: self.to_owner(p.core).start())
        elif k == 1:

            @pl.when(self.mine)
            def _():
                pltpu.make_async_copy(self.half, self.columns(p.core), self.local).wait()
                self.to_owner(1 - p.core).wait_recv()
                for step in (-1, 1):
                    pl.when(p.has(p.z + step))(lambda step=step: self.along_z(p.z, step).start())

        elif k <= 4:
            for step in (-1, 1):
                z = p.z + step * (k - 1)

                @pl.when(jnp.logical_and(p.has(z), z // self.clips == p.core))
                def _():
                    self.along_z(z, -step).wait_recv()
                    pl.when(p.has(p.z - step))(lambda: self.along_z(z, -step).start())

        else:
            pl.when(jnp.logical_not(self.mine))(lambda: self.to_owner(p.core).wait_send())
            for i in range(self.clips):
                z = p.core * self.clips + i
                for step in (-1, 1):
                    sent = jnp.logical_and(p.has(p.z + step), (p.z - z) * step >= 0)
                    pl.when(sent)(lambda: self.along_z(z, step).wait_send())


class Frames:
    @staticmethod
    def scratch(n_t, clips):
        return [pltpu.SemaphoreType.DMA, pltpu.SemaphoreType.DMA((n_t,)), pltpu.SemaphoreType.DMA((clips, 2))]

    def __init__(self, place, half, whole, part, scratch):
        self.place, self.half, self.whole, self.part = place, half, whole, part
        self.local, self.send, self.recv = scratch
        self.clips = whole.shape[0]
        self.mine = place.z // self.clips == place.core

    def to(self, clip, core):
        wide = self.half.shape[1]
        return self.whole.at[clip, :, pl.ds(pl.multiple_of(core * wide, 128), wide)]

    def rows(self, z):
        return self.half.at[pl.ds(pl.multiple_of(self.part * z // 16 * 16, 16), self.whole.shape[1])]

    def keep(self):
        p = self.place
        return pltpu.make_async_copy(self.rows(p.z), self.to(lax.rem(p.z, self.clips), p.core), self.local)

    def copy(self, step):
        p = self.place
        clip, z = lax.rem(p.z, self.clips), lax.rem(p.z + step, p.n_t)
        f = p.to_core if step == 0 else p.f - p.core + p.z // self.clips
        return pltpu.make_async_remote_copy(
            src_ref=self.rows(z), dst_ref=self.to(clip, p.core), send_sem=self.send.at[step],
            recv_sem=self.recv.at[clip, p.core], device_id=p.device(f, z), device_id_type=MESH,
        )

    def arriving(self, clip, core):
        p = self.place
        return pltpu.make_async_remote_copy(
            src_ref=self.rows(p.z), dst_ref=self.to(clip, core), send_sem=self.send.at[0],
            recv_sem=self.recv.at[clip, core], device_id=p.device(p.to_core, p.z), device_id_type=MESH,
        )

    def start(self, step):
        if step:
            self.copy(step).start()
        else:
            pl.when(self.mine)(lambda: self.keep().start())
            pl.when(jnp.logical_not(self.mine))(lambda: self.copy(0).start())

    def finish(self):
        p = self.place
        for step in range(1, p.n_t):
            self.copy(step).wait_send()
        pl.when(self.mine)(lambda: self.keep().wait())
        pl.when(jnp.logical_not(self.mine))(lambda: self.copy(0).wait_send())
        for clip in range(self.clips):
            for core in range(2):
                own = jnp.logical_and(p.core * self.clips + clip == p.z, p.core == core)
                pl.when(jnp.logical_not(own))(lambda: self.arriving(clip, core).wait_recv())


class Total:
    @staticmethod
    def scratch(shape):
        return [pltpu.VMEM(shape, F32), *sem_pair(shape[0]), *sem_pair(shape[0])]

    def __init__(self, place, packed, total, scratch):
        self.place, self.packed, self.total, self.came = place, packed, total, scratch[0]
        self.to_sum, self.to_all = scratch[1:3], scratch[3:5]
        self.me = place.box(0)[2]
        self.peers = [place.box(at) for at in range(1, packed.shape[0])]

    def out(self, peer):
        f, z, at = peer
        return pltpu.make_async_remote_copy(
            src_ref=self.packed.at[at], dst_ref=self.came.at[self.me], send_sem=self.to_sum[0].at[at],
            recv_sem=self.to_sum[1].at[self.me], device_id=self.place.device(f, z), device_id_type=MESH,
        )

    def back(self, peer):
        f, z, at = peer
        return pltpu.make_async_remote_copy(
            src_ref=self.total.at[self.me], dst_ref=self.total.at[self.me], send_sem=self.to_all[0].at[at],
            recv_sem=self.to_all[1].at[self.me], device_id=self.place.device(f, z), device_id_type=MESH,
        )

    def arrived(self, sems, buffer, peer):
        f, z, at = peer
        pltpu.make_async_remote_copy(
            src_ref=buffer.at[at], dst_ref=buffer.at[at], send_sem=sems[0].at[at], recv_sem=sems[1].at[at],
            device_id=self.place.device(f, z), device_id_type=MESH,
        ).wait_recv()

    def run(self, k):
        if k == 0:
            for peer in self.peers:
                self.out(peer).start()
            self.came[self.me] = self.packed[self.me]
        elif k == 1:
            for peer in self.peers:
                self.arrived(self.to_sum, self.came, peer)
            self.total[self.me] = jnp.sum(self.came[...], axis=0)
        elif k == 2:
            for peer in self.peers:
                self.back(peer).start()
        else:
            for peer in self.peers:
                self.arrived(self.to_all, self.total, peer)
                self.out(peer).wait_send()
                self.back(peer).wait_send()


class Scatter:
    steps = 7

    @staticmethod
    def scratch(n_t, size, wide):
        half = size // 2
        return [
            pltpu.VMEM((n_t, 2, half, wide), BF16), pltpu.VMEM((n_t, 2, half, wide), BF16),
            pltpu.VMEM((n_t, half, wide), BF16), pltpu.VMEM((n_t, half, wide), BF16),
            pltpu.VMEM((n_t, size, wide), BF16), pltpu.VMEM((2, n_t, size, wide), BF16),
            pltpu.VMEM((n_t, 4, half, wide), BF16), pltpu.SemaphoreType.DMA((n_t, 4)),
            *sem_pair(n_t, 6), *sem_pair(2, n_t),
        ]

    def __init__(self, place, grads, own, scratch):
        self.place, self.grads, self.own = place, grads, own
        self.came_y, self.came_x, self.last_x, self.last_y, self.sums, self.came_z, self.held, self.load, a, b, c, d = scratch
        self.xy, self.zs = (a, b), (c, d)
        self.half = own.shape[0] // 2

    def at(self, group, half):
        return pl.ds(pl.multiple_of((2 * group + half) * self.half, 16), self.half)

    def copy(self, slot, at):
        p, g = self.place, self.grads
        by_y = at in (0, 2, 5)
        if at < 4:
            half = 0 if by_y else 1
            group = p.group_xy if at < 2 else (p.group_y if by_y else p.group_x)
            came = self.came_y if by_y else self.came_x
            src, to = g.at[slot, self.at(group, half)], came.at[slot, 1 if at < 2 else 0]
        else:
            src = self.came_x.at[slot, 1] if by_y else self.came_y.at[slot, 1]
            to = self.last_y.at[slot] if by_y else self.last_x.at[slot]
        return remote(src, to, self.xy, (slot, at), p.y() if by_y else p.x())

    def along_z(self, slot, way):
        p = self.place
        return remote(
            self.sums.at[slot], self.came_z.at[way, slot], self.zs, (way, slot), p.device(p.f, p.z + 2 * way - 1)
        )

    def over(self, rows, body):
        step = 32

        def one(i, carry):
            body(pl.multiple_of(i * step, step), step)
            return carry

        lax.fori_loop(0, rows // step, one, 0)

    def hold(self, slot, at):
        p = self.place
        rows = self.at((p.group_x, p.group_y, p.group, p.group)[at], (0, 1, 0, 1)[at])
        return pltpu.make_async_copy(self.grads.at[slot, rows], self.held.at[slot, at], self.load.at[slot, at])

    def first(self, slot):
        for at in range(4):
            self.copy(slot, at).start()
        for at in range(4):
            self.hold(slot, at).start()

    def second(self, slot):
        for at in range(2):
            self.hold(slot, at).wait()
            self.copy(slot, at).wait_recv()

        def body(at, step):
            to = pl.ds(at, step)
            for i, came in enumerate((self.came_y, self.came_x)):
                came[slot, 1, to] = add(came[slot, 1, to], self.held[slot, i, to])

        self.over(self.half, body)
        self.copy(slot, 4).start()
        self.copy(slot, 5).start()

    def third(self, slot):
        p = self.place
        for at in (2, 3, 4, 5):
            self.copy(slot, at).wait_recv()
        for at in (2, 3):
            self.hold(slot, at).wait()

        def body(at, step):
            to = pl.ds(at, step)
            for came, last, half in ((self.came_y, self.last_x, 0), (self.came_x, self.last_y, 1)):
                total = self.held[slot, 2 + half, to].astype(F32) + came[slot, 0, to].astype(F32) + last[slot, to].astype(F32)
                self.sums[slot, pl.ds(pl.multiple_of(half * self.half + at, step), step)] = total.astype(BF16)

        self.over(self.half, body)
        for way in range(2):
            step = 2 * way - 1

            @pl.when((slot - p.z) * step > 0)
            def _():
                @pl.when(p.has(p.z - step))
                def _():
                    self.along_z(slot, way).wait_recv()

                    def body(at, step):
                        to = pl.ds(at, step)
                        self.sums[slot, to] = add(self.sums[slot, to], self.came_z[way, slot, to])

                    self.over(2 * self.half, body)

                self.along_z(slot, way).start()

    def run(self, k):
        p = self.place
        n = p.n_t
        if k == 0:
            self.first(self.place.slot(0))
            self.first(self.place.slot(1))
            return
        if k <= n:
            self.second(self.place.slot(k - 1))
        if k + 1 < n:
            self.first(self.place.slot(k + 1))
        if 2 <= k <= n + 1:
            self.third(self.place.slot(k - 2))
        if k == n + 2:
            z = p.z

            def begin(at, step):
                to = pl.ds(at, step)
                self.own[to] = self.sums[z, to].astype(F32)

            self.over(2 * self.half, begin)
            for way in range(2):
                step = 2 * way - 1

                @pl.when(p.has(z - step))
                def _():
                    self.along_z(z, way).wait_recv()

                    def body(at, step):
                        to = pl.ds(at, step)
                        self.own[to] += self.came_z[way, z, to].astype(F32)

                    self.over(2 * self.half, body)

            for slot in range(n):
                for at in range(6):
                    self.copy(slot, at).wait_send()
                for way in range(2):
                    pl.when((slot - z) * (2 * way - 1) > 0)(self.along_z(slot, way).wait_send)


def hook_of(steps):
    def hook(p, pairs):
        for k, functions in steps.items():

            @pl.when(p == k)
            def _():
                for function in functions:
                    function()

    return hook


def step(job, k):
    return functools.partial(job.run, k)


def swap(place, part, came, sems):
    return pltpu.make_async_remote_copy(
        src_ref=part, dst_ref=came, send_sem=sems.at[0], recv_sem=sems.at[1],
        device_id=place.device(place.to_core, place.z), device_id_type=MESH,
    )


def row_step(m):
    return 32 if m % 32 == 0 else m


def over_rows(m, body):
    step = row_step(m)

    def run(i, carry):
        return body(pl.ds(pl.multiple_of(i * step, step), step), carry)

    return lambda carry: lax.fori_loop(0, m // step, run, carry)


def normal(values):
    centre = values - jnp.mean(values, axis=-1, keepdims=True)
    inverse = lax.rsqrt(jnp.mean(centre * centre, axis=-1, keepdims=True) + EPSILON)
    return centre * inverse, inverse


def norm_rows(value_at, gain, shift, normed, kept=None):
    gain_row, shift_row = gain[...], shift[...]

    def body(at, carry):
        value = value_at(at)
        if kept is not None:
            kept[at, :] = value
        normed[at, :] = (normal(value)[0] * gain_row + shift_row).astype(BF16)
        return carry

    over_rows(normed.shape[0], body)(0)


def norm_back_rows(own, came, values, gain, upstream, grad_ref, low_ref, sums):
    gain_row = gain[...]
    wide = values.shape[1]

    def body(at, carry):
        q = own[at, :].astype(F32) + came[at, :].astype(F32)
        n, inverse = normal(values[at, :].astype(F32))
        up = upstream[at, :].astype(F32)
        v = q * gain_row
        back = inverse * (v - jnp.mean(v, axis=-1, keepdims=True) - n * jnp.mean(v * n, axis=-1, keepdims=True))
        grad = up + back
        grad_ref[at, :] = grad.astype(grad_ref.dtype)
        if low_ref is not None:
            low_ref[at, :] = grad.astype(BF16)
        terms = (q * n, q, grad, up)
        return tuple(c + jnp.sum(t, axis=0, keepdims=True) for c, t in zip(carry, terms))

    totals = over_rows(values.shape[0], body)(tuple(jnp.zeros((1, wide), F32) for _ in range(4)))
    row = lax.broadcasted_iota(jnp.int32, sums.shape, 0)
    value = jnp.zeros(sums.shape, F32)
    for at, total in enumerate(totals):
        value = jnp.where(row == at, total, value)
    sums[...] = value


def lane_mask(shape, h):
    return (lax.broadcasted_iota(jnp.int32, shape, 1) // HEAD_DIM) == h


def mask_scores(scores, causal, valid):
    size = scores.shape[0]
    if causal:
        key_at = lax.broadcasted_iota(jnp.int32, scores.shape, 0)
        query_at = lax.broadcasted_iota(jnp.int32, scores.shape, 1)
        return jnp.where(key_at <= query_at, scores, MASKED)
    if valid < size:
        edge = valid // 8 * 8
        tail = scores[edge:, :]
        key_at = lax.broadcasted_iota(jnp.int32, tail.shape, 0) + edge
        return jnp.concatenate([scores[:edge, :], jnp.where(key_at < valid, tail, -jnp.inf)], axis=0)
    return scores


def attend(q_ref, k_ref, v_ref, mixed_ref, log_ref, score_buf, causal, blocks, valid, hook):
    size = k_ref.shape[0] // blocks
    pairs = q_ref.shape[1] // PAIR

    def one_pair(p, carry):
        at = pl.ds(pl.multiple_of(p * PAIR, PAIR), PAIR)
        q_all = q_ref[:, at].astype(F32) * SCALE
        result = None
        for h in range(2):
            queries = jnp.where(lane_mask(q_all.shape, h), q_all, 0.0).astype(BF16)
            top = None
            for i in range(blocks):
                rows = slice(i * size, (i + 1) * size)
                scores = mask_scores(dot(k_ref[rows, at], queries, NT), causal, valid - i * size)
                score_buf[rows, :] = scores
                now = jnp.max(scores, axis=0, keepdims=True)
                top = now if top is None else jnp.maximum(top, now)
            total, mixed = None, None
            for i in range(blocks):
                rows = slice(i * size, (i + 1) * size)
                raised = jnp.exp(score_buf[rows, :] - top)
                now = jnp.sum(raised, axis=0, keepdims=True)
                total = now if total is None else total + now
                now = dot(v_ref[rows, at], raised.astype(BF16), TN)
                mixed = now if mixed is None else mixed + now
            log_ref[2 * p + h] = jnp.broadcast_to(top + jnp.log(total), log_ref.shape[1:])
            mixed = mixed / total
            if result is None:
                result = mixed
            else:
                row = lax.broadcasted_iota(jnp.int32, mixed.shape, 0)
                result = jnp.where(row < HEAD_DIM, result, mixed)
        mixed_ref[:, at] = jnp.transpose(result).astype(BF16)
        hook(p, pairs)
        return carry

    lax.fori_loop(0, pairs, one_pair, 0)


def attend_back(q_ref, k_ref, v_ref, up_ref, mixed_ref, log_ref, dq_ref, dk_ref, dv_ref, sums, causal, blocks, valid, hook):
    size = k_ref.shape[0] // blocks
    pairs = q_ref.shape[1] // PAIR

    def one_pair(p, carry):
        at = pl.ds(pl.multiple_of(p * PAIR, PAIR), PAIR)
        q_all = q_ref[:, at].astype(F32) * SCALE
        up_all = up_ref[:, at].astype(F32)
        product = up_all * mixed_ref[:, at].astype(F32)
        queries, upstream, inner, logs = [], [], [], []
        for h in range(2):
            chosen = lane_mask(q_all.shape, h)
            queries.append(jnp.where(chosen, q_all, 0.0).astype(BF16))
            upstream.append(jnp.where(chosen, up_all, 0.0).astype(BF16))
            ones = jnp.where(lane_mask((8, PAIR), h), 1.0, 0.0)
            inner.append(
                lax.dot_general(ones, product, NT, precision=lax.Precision.HIGHEST, preferred_element_type=F32)[0:1, :]
            )
            logs.append(log_ref[2 * p + h][0:1, :])
        query_grads = [None, None]
        value_sum = None
        for i in range(blocks):
            rows = slice(i * size, (i + 1) * size)
            keys, values = k_ref[rows, at], v_ref[rows, at]
            key_grad, value_grad = None, None
            for h in range(2):
                chance = jnp.exp(mask_scores(dot(keys, queries[h], NT), causal, valid - i * size) - logs[h])
                now = dot(chance.astype(BF16), upstream[h])
                value_grad = now if value_grad is None else value_grad + now
                grad = dot(values, upstream[h], NT)
                score_grad = (chance * (grad - inner[h])).astype(BF16)
                now = dot(score_grad, queries[h])
                key_grad = now if key_grad is None else key_grad + now
                now = dot(keys, score_grad, TN)
                query_grads[h] = now if query_grads[h] is None else query_grads[h] + now
            dk_ref[rows, at] = key_grad.astype(BF16)
            dv_ref[rows, at] = value_grad.astype(BF16)
            now = jnp.sum(value_grad, axis=0, keepdims=True)
            value_sum = now if value_sum is None else value_sum + now
        row = lax.broadcasted_iota(jnp.int32, query_grads[0].shape, 0)
        query_grad = jnp.transpose(jnp.where(row < HEAD_DIM, query_grads[0], query_grads[1])) * SCALE
        dq_ref[:, at] = query_grad.astype(BF16)
        query_sum = jnp.sum(query_grad, axis=0, keepdims=True)
        row = lax.broadcasted_iota(jnp.int32, (8, PAIR), 0)
        sums[:, at] = jnp.where(row == 0, query_sum, jnp.where(row == 1, value_sum, 0.0))
        hook(p, pairs)
        return carry

    lax.fori_loop(0, pairs, one_pair, 0)


def gather_kernel(sizes, own, *refs):
    stored, whole, here, scratch = refs[:3], refs[3], refs[4:7], refs[7:]
    place = Place(sizes)
    clips = Clips(place, stored, here, scratch[:3])
    job = Gather(place, own, whole, scratch[3:])
    place.barrier()
    job.run(0)
    clips.start()
    for k in range(1, Gather.steps):
        job.run(k)
    clips.finish()


def gather(sizes, own, stored):
    n_t = sizes[1]
    return call(
        functools.partial(gather_kernel, sizes), "gather",
        [((n_t, GROUPS * own.shape[0], own.shape[1]), BF16)] + [(v.shape[1:], v.dtype) for v in stored], [own, *stored],
        scratch=Clips.scratch(len(stored)) + Gather.scratch(n_t), remote=0, anywhere=((0, 1, 2, 3), (0,)),
    )


def self_forward_kernel(
    sizes, own, start, gain, shift, bias, weights, whole, normed, qkv, mixed, logs, part, came, w_in, w_out, score_buf,
    sems, loads, *scratch,
):
    place = Place(sizes)
    job = Gather(place, own, whole, scratch)
    wide = mixed.shape[1]
    fetch(weights, w_in, [(0, 0), (1, wide), (2, 2 * wide)], loads.at[0])
    fetch(weights, w_out, [(3, 0)], loads.at[1])
    place.barrier()
    job.run(0)
    norm_rows(lambda at: start[at, :].astype(F32), gain, shift, normed)
    fetched(w_in, loads.at[0])
    fetched(w_out, loads.at[1])
    qkv[...] = (dot(normed[...], w_in[...]) + bias[...]).astype(BF16)
    job.run(1)
    q, k, v = (qkv.at[:, i * wide : (i + 1) * wide] for i in range(3))
    attend(q, k, v, mixed, logs, score_buf, True, 1, start.shape[0], hook_of({2: [step(job, 2)]}))
    part[...] = dot(mixed[...], w_out[...], NT).astype(BF16)
    job.run(3)
    exchange = swap(place, part, came, sems)
    exchange.start()
    job.run(4)
    job.run(5)
    exchange.wait()


def self_forward(sizes, own, start, gain, shift, bias, weights):
    m, d = start.shape
    n_t = sizes[1]
    wide = bias.shape[1] // 3
    heads = wide // HEAD_DIM
    return call(
        functools.partial(self_forward_kernel, sizes), "self_forward",
        [((n_t, GROUPS * own.shape[0], own.shape[1]), BF16), ((m, d), BF16), ((m, 3 * wide), BF16), ((m, wide), BF16),
         ((heads, 8, m), F32), ((m, d), BF16), ((m, d), BF16)],
        [own, start, gain, shift, bias, weights],
        scratch=[
            pltpu.VMEM((d, 3 * wide), BF16), pltpu.VMEM((d, wide), BF16), pltpu.VMEM((m, m), F32),
            pltpu.SemaphoreType.DMA((2,)), pltpu.SemaphoreType.DMA((2,)), *Gather.scratch(n_t),
        ],
        flops=2 * m * d * 4 * wide + 4 * m * m * wide * 2, remote=1, anywhere=((0, 5), (0,)),
    )


def cross_forward_kernel(
    sizes, blocks, valid, own_weights, start, own, came, branch, gain, shift, bias, bias_kv, memory, weights,
    branch_two, gain_two, shift_two, upstream, hidden_bias,
    grads, middle, normed, q, kv, mixed, logs, later, out_part, out_came, grad_part, grad_came, sums,
    whole, normed_three, out_acc, grad_acc, stage, part, part_came, w_in, w_kv, w_out, score_buf, sems, loads, stores,
    out_sems, grad_sems, *scratch,
):
    place = Place(sizes)
    job = Gather(place, own_weights, whole, scratch)
    wide = mixed.shape[1]
    fetch(weights, w_kv, [(1, 0), (2, wide)], loads.at[0])
    fetch(weights, w_in, [(0, 0)], loads.at[1])
    fetch(weights, w_out, [(3, 0)], loads.at[2])
    place.barrier()
    job.run(0)
    fetched(w_kv, loads.at[0])
    size = memory.shape[0] // blocks

    def one_block(i, carry):
        at = pl.ds(pl.multiple_of(i * size, size), size)
        kv[at, :] = (dot(memory[at, :], w_kv[...]) + bias_kv[...]).astype(BF16)
        return carry

    lax.fori_loop(0, blocks, one_block, 0)
    job.run(1)
    branch_row = branch[...]
    norm_rows(
        lambda at: start[at, :].astype(F32) + (own[at, :].astype(F32) + came[at, :].astype(F32)) + branch_row,
        gain, shift, normed, middle,
    )
    fetched(w_in, loads.at[1])
    fetched(w_out, loads.at[2])
    q[...] = (dot(normed[...], w_in[...]) + bias[...]).astype(BF16)

    attend(
        q, kv.at[:, :wide], kv.at[:, wide:], mixed, logs, score_buf, False, blocks, valid, hook_of({1: [step(job, 2)]})
    )
    part[...] = dot(mixed[...], w_out[...], NT).astype(BF16)
    exchange = swap(place, part, part_came, sems)
    job.run(3)
    exchange.start()
    out_acc[...] = jnp.zeros(out_acc.shape, F32)
    grad_acc[...] = jnp.zeros(grad_acc.shape, F32)
    exchange.wait()
    branch_two_row = branch_two[...]
    norm_rows(
        lambda at: middle[at, :] + (part[at, :].astype(F32) + part_came[at, :].astype(F32)) + branch_two_row,
        gain_two, shift_two, normed_three, later,
    )
    slots, width = place.n_t, hidden_bias.shape[2]
    order = [place.slot(slots - 1 - i) for i in range(slots)]

    def store(i, slot):
        return pltpu.make_async_copy(stage.at[lax.rem(i, 2)], grads.at[slot], stores.at[lax.rem(i, 2)])

    def one_slot(i, carry):
        slot = order[-1]
        for at in range(slots - 1):
            slot = jnp.where(i == at, order[at], slot)
        pl.when(i == slots - 1)(step(job, 4))
        job.complete(slot)
        pl.when(i >= 2)(lambda: store(i, slot).wait())
        expanded = dot(normed_three[...], whole[slot, :, :width]) + hidden_bias[slot]
        phi = 0.5 * (1.0 + lax.erf(expanded * (0.5**0.5)))
        activated = (expanded * phi).astype(BF16)
        density = jnp.exp(expanded * expanded * -0.5) * ((2.0 * math.pi) ** -0.5)
        slope = phi + expanded * density
        expanded_grad = dot(upstream[...], whole[slot, :, width:]) * slope
        expanded_low = expanded_grad.astype(BF16)
        sums[slot] = jnp.broadcast_to(jnp.sum(expanded_grad, axis=0, keepdims=True), sums.shape[1:])
        out_acc[...] += dot(activated, whole[slot, :, width:], NT)
        grad_acc[...] += dot(expanded_low, whole[slot, :, :width], NT)
        held = stage.at[lax.rem(i, 2)]
        held[:, :width] = dot(normed_three[...], expanded_low, TN).astype(BF16)
        held[:, width:] = dot(upstream[...], activated, TN).astype(BF16)
        store(i, slot).start()
        return carry

    lax.fori_loop(0, slots, one_slot, 0)
    grad_part[...] = grad_acc[...].astype(BF16)
    out_part[...] = out_acc[...].astype(BF16)
    job.run(5, False)
    grad_exchange = swap(place, grad_part, grad_came, grad_sems)
    out_exchange = swap(place, out_part, out_came, out_sems)
    grad_exchange.start()
    out_exchange.start()
    store(0, 0).wait()
    store(1, 0).wait()
    grad_exchange.wait()
    out_exchange.wait()


def cross_forward(
    sizes, own_weights, start, own, came, branch, gain, shift, bias, bias_kv, memory, weights, branch_two, gain_two,
    shift_two, upstream, hidden_bias, blocks, valid,
):
    m, d = start.shape
    n_t = sizes[1]
    n, wide = memory.shape[0], bias.shape[1]
    feed_wide = own_weights.shape[1]
    heads = wide // HEAD_DIM
    return call(
        functools.partial(cross_forward_kernel, sizes, blocks, valid), "cross_and_feed",
        [((n_t, d, feed_wide), BF16), ((m, d), F32), ((m, d), BF16),
         ((m, wide), BF16), ((n, 2 * wide), BF16), ((m, wide), BF16), ((heads, 8, m), F32), ((m, d), F32)]
        + [((m, d), BF16)] * 4 + [((n_t, 8, feed_wide // 2), F32)],
        [own_weights, start, own, came, branch, gain, shift, bias, bias_kv, memory, weights, branch_two, gain_two,
         shift_two, upstream, hidden_bias],
        scratch=[
            pltpu.VMEM((n_t, GROUPS * own_weights.shape[0], feed_wide), BF16), pltpu.VMEM((m, d), BF16),
            pltpu.VMEM((m, d), F32), pltpu.VMEM((m, d), F32), pltpu.VMEM((2, d, feed_wide), BF16),
            pltpu.VMEM((m, d), BF16), pltpu.VMEM((m, d), BF16),
            pltpu.VMEM((d, wide), BF16), pltpu.VMEM((d, 2 * wide), BF16), pltpu.VMEM((d, wide), BF16),
            pltpu.VMEM((n, m), F32), pltpu.SemaphoreType.DMA((2,)), pltpu.SemaphoreType.DMA((3,)),
            *[pltpu.SemaphoreType.DMA((2,))] * 3, *Gather.scratch(n_t),
        ],
        flops=6 * m * d * feed_wide * n_t + 2 * m * d * 2 * wide + 4 * n * d * wide + 4 * m * n * wide * 2, remote=2, anywhere=((0, 10), (0,)),
    )


def cross_back_kernel(
    sizes, blocks, valid, own, came, later, gain, upstream, q, kv, mixed, logs, weights, normed, memory, feed_grads,
    out_part, out_came, branch,
    output, memory_came, later_grad, sums, head_sums, part, part_came, grads, keep, feed_own,
    later_low, dq, dkv, w_one, w_two, w_kv, mixed_grad, piece, out_half, send, sems, memory_sems, loads, *scratch,
):
    place = Place(sizes)
    spread = Spread(place, out_half, output, scratch[:5])
    job = Scatter(place, feed_grads, feed_own, scratch[5:])
    wide = q.shape[1]
    n, d = memory.shape
    fetch(weights, w_one, [(3, 0)], loads.at[0])
    fetch(weights, w_two, [(0, 0)], loads.at[1])
    fetch(weights, w_kv, [(1, 0), (2, wide)], loads.at[2])
    place.barrier()
    job.run(0)
    out_wide = out_half.shape[1]
    out_at = pl.ds(pl.multiple_of(place.core * out_wide, out_wide), out_wide)
    branch_half = branch[:, out_at]

    def one_row(at, carry):
        total = later[at, out_at] + (out_part[at, out_at].astype(F32) + out_came[at, out_at].astype(F32)) + branch_half
        out_half[at, :] = total.astype(BF16)
        return carry

    over_rows(out_half.shape[0], one_row)(0)
    norm_back_rows(own, came, later, gain, upstream, later_grad, later_low, sums)
    spread.run(0)
    for at, buffer in enumerate((w_one, w_two, w_kv)):
        fetched(buffer, loads.at[at])
    mixed_grad[...] = dot(later_low[...], w_one[...]).astype(BF16)
    attend_back(
        q, kv.at[:, :wide], kv.at[:, wide:], mixed_grad, mixed, logs, dq, dkv.at[:, :wide], dkv.at[:, wide:],
        head_sums, False, blocks, valid, hook_of({0: [step(job, 1), step(spread, 1)], 2: [step(job, 2), step(spread, 2)]}),
    )
    part[...] = dot(dq[...], w_two[...], NT).astype(BF16)
    unfill(grads, 3, dot(later_low[...], mixed[...], TN).astype(BF16))
    exchange = swap(place, part, part_came, sems)
    exchange.start()
    unfill(grads, 0, dot(normed[...], dq[...], TN).astype(BF16))
    job.run(3)
    spread.run(3)
    size = n // blocks
    own_half = pl.ds(pl.multiple_of(place.core * (d // 2), d // 2), d // 2)
    other_half = pl.ds(pl.multiple_of((1 - place.core) * (d // 2), d // 2), d // 2)

    def one_block(i, carry):
        rows = pl.ds(pl.multiple_of(i * size, size), size)
        piece[...] = dot(dkv[rows, :], w_kv[...], NT).astype(BF16)
        keep[rows, :] = piece[:, own_half]
        send[rows, :] = piece[:, other_half]
        return carry

    lax.fori_loop(0, blocks, one_block, 0)
    spread.run(4)
    memory_exchange = swap(place, send, memory_came, memory_sems)
    memory_exchange.start()
    unfill(grads, 1, dot(memory[...], dkv[:, :wide], TN).astype(BF16))
    unfill(grads, 2, dot(memory[...], dkv[:, wide:], TN).astype(BF16))
    for k in (4, 5, 6):
        job.run(k)
    spread.run(5)
    exchange.wait()
    memory_exchange.wait()


def cross_back(
    sizes, own, came, later, gain, upstream, q, kv, mixed, logs, weights, normed, memory, feed_grads, out_part, out_came,
    branch, clips, blocks, valid,
):
    m, d = later.shape
    n_t = sizes[1]
    n, wide = memory.shape[0], q.shape[1]
    size, feed_wide = d // GROUPS, feed_grads.shape[2]
    return call(
        functools.partial(cross_back_kernel, sizes, blocks, valid), "cross_back",
        [((clips, m, d), BF16), ((n, d // 2), BF16), ((m, d), F32), ((8, d), F32), ((8, wide), F32), ((m, d), BF16),
         ((m, d), BF16), ((n_t, d, 4 * PAIR), BF16), ((n, d // 2), BF16), ((size, feed_wide), F32)],
        [own, came, later, gain, upstream, q, kv, mixed, logs, weights, normed, memory, feed_grads, out_part, out_came,
         branch],
        scratch=[
            pltpu.VMEM((m, d), BF16), pltpu.VMEM((m, wide), BF16), pltpu.VMEM((n, 2 * wide), BF16),
            pltpu.VMEM((d, wide), BF16), pltpu.VMEM((d, wide), BF16), pltpu.VMEM((d, 2 * wide), BF16),
            pltpu.VMEM((m, wide), BF16), pltpu.VMEM((n // blocks, d), BF16), pltpu.VMEM((m, d // 2), BF16),
            pltpu.VMEM((n, d // 2), BF16), pltpu.SemaphoreType.DMA((2,)), pltpu.SemaphoreType.DMA((2,)),
            pltpu.SemaphoreType.DMA((3,)), *Spread.scratch(clips), *Scatter.scratch(n_t, size, feed_wide),
        ],
        flops=8 * m * d * wide + 10 * m * n * wide * 2 + 8 * n * d * wide, remote=3, anywhere=((9, 12), (0, 1)),
    )


def self_back_kernel(
    sizes, frames, own, came, middle, gain, upstream, qkv, mixed, logs, weights, normed, cross_grads, keep, keep_came,
    start, start_gain,
    whole, half_grad, start_sums, sums, head_sums, grads, cross_own,
    middle_grad, grad, part, part_came, middle_low, dqkv, w_in, w_out, mixed_grad, memory_sum, sems, loads, *scratch,
):
    place = Place(sizes)
    memory_job = Frames(place, memory_sum, whole, frames, scratch[:3])
    job = Scatter(place, cross_grads, cross_own, scratch[3:])
    wide = mixed.shape[1]
    fetch(weights, w_in, [(0, 0), (1, wide), (2, 2 * wide)], loads.at[0])
    fetch(weights, w_out, [(3, 0)], loads.at[1])
    place.barrier()
    job.run(0)

    def one_row(at, carry):
        memory_sum[at, :] = add(keep[at, :], keep_came[at, :])
        return carry

    over_rows(memory_sum.shape[0], one_row)(0)
    fetched(w_in, loads.at[0])
    fetched(w_out, loads.at[1])
    for at in (1, 3, 0):
        memory_job.start(at)
    norm_back_rows(own, came, middle, gain, upstream, middle_grad, middle_low, sums)
    job.run(1)
    mixed_grad[...] = dot(middle_low[...], w_out[...]).astype(BF16)
    cut = [slice(i * wide, (i + 1) * wide) for i in range(3)]
    attend_back(
        *(qkv.at[:, c] for c in cut), mixed_grad, mixed, logs, *(dqkv.at[:, c] for c in cut), head_sums, True, 1,
        middle.shape[0], hook_of({0: [step(job, 2)], 2: [step(job, 3)]}),
    )
    part[...] = dot(dqkv[...], w_in[...], NT).astype(BF16)
    job.run(4)
    exchange = swap(place, part, part_came, sems)
    exchange.start()
    unfill(grads, 3, dot(middle_low[...], mixed[...], TN).astype(BF16))
    unfill(grads, 0, dot(normed[...], dqkv[:, cut[0]], TN).astype(BF16))
    job.run(5)
    memory_job.start(2)
    exchange.wait()
    norm_back_rows(part, part_came, start, start_gain, middle_grad, grad, None, start_sums)
    half = half_grad.shape[1]
    half_grad[...] = grad[:, pl.ds(pl.multiple_of(place.core * half, half), half)]
    for which in (1, 2):
        unfill(grads, which, dot(normed[...], dqkv[:, cut[which]], TN).astype(BF16))
    job.run(6)
    memory_job.finish()


def self_back(
    sizes, own, came, middle, gain, upstream, qkv, mixed, logs, weights, normed, cross_grads, keep, keep_came, start, start_gain,
    clips, frames,
):
    m, d = middle.shape
    n_t = sizes[1]
    wide = mixed.shape[1]
    size, cross_wide = d // GROUPS, cross_grads.shape[2]
    return call(
        functools.partial(self_back_kernel, sizes, frames), "self_back",
        [((clips, (frames + 30) // 16 * 16, d), BF16), ((m, d // 2), BF16), ((8, d), F32), ((8, d), F32), ((8, wide), F32),
         ((n_t, d, 4 * PAIR), BF16), ((size, cross_wide), F32)],
        [own, came, middle, gain, upstream, qkv, mixed, logs, weights, normed, cross_grads, keep, keep_came,
         start, start_gain],
        scratch=[
            pltpu.VMEM((m, d), F32), *[pltpu.VMEM((m, d), BF16)] * 4,
            pltpu.VMEM((m, 3 * wide), BF16), pltpu.VMEM((d, 3 * wide), BF16),
            pltpu.VMEM((d, wide), BF16), pltpu.VMEM((m, wide), BF16), pltpu.VMEM(keep.shape, BF16),
            pltpu.SemaphoreType.DMA((2,)), pltpu.SemaphoreType.DMA((2,)), *Frames.scratch(n_t, clips), *Scatter.scratch(n_t, size, cross_wide),
        ],
        flops=16 * m * d * wide + 10 * m * m * wide * 2, remote=4, anywhere=((8, 10), (0,)),
    )


def finish_kernel(sizes, self_grads, half_grad, packed, whole, total, self_own, *scratch):
    place = Place(sizes)
    spread = Spread(place, half_grad, whole, scratch[:5])
    all_sum = Total(place, packed, total, scratch[5:10])
    job = Scatter(place, self_grads, self_own, scratch[10:])
    place.barrier(True)
    all_sum.run(0)
    spread.run(0)
    job.run(0)
    spread.run(1)
    job.run(1)
    all_sum.run(1)
    spread.run(2)
    job.run(2)
    all_sum.run(2)
    spread.run(3)
    job.run(3)
    spread.run(4)
    for k in (4, 5, 6):
        job.run(k)
    spread.run(5)
    all_sum.run(3)


def finish(sizes, half_grad, self_grads, packed, clips):
    m, half = half_grad.shape
    n_t, d, wide = self_grads.shape
    size = d // GROUPS
    return call(
        functools.partial(finish_kernel, sizes), "finish",
        [((clips, m, 2 * half), BF16), (packed.shape, F32), ((size, wide), F32)], [self_grads, half_grad, packed],
        scratch=[*Spread.scratch(clips), *Total.scratch(packed.shape), *Scatter.scratch(n_t, size, wide)],
        remote=5, anywhere=((0,), (0,)),
    )


def flip(x, bit, size):
    return lax.ppermute(x, "fsdp", [(i, i ^ (1 << bit)) for i in range(size)])


def half(x, index, axis):
    size = x.shape[axis] // 2
    return lax.dynamic_slice_in_dim(x, index * size, size, axis=axis)


def add(a, b):
    return (a.astype(F32) + b.astype(F32)).astype(BF16)


def on_device(
    n_f, n_t,
    tokens, encoder, cotangent, self_weights, self_biases, self_output, cross_query, cross_memory,
    cross_biases, cross_output, hidden_weight, hidden_bias, reduce_weight, norm_gains, norm_shifts, branch_biases,
):
    bits = n_f.bit_length() - 1
    x_bit, y_bit = bits - 2, bits - 1
    f = lax.axis_index("fsdp")
    z = lax.axis_index("tensor")
    core = f % 2
    sizes = (n_f, n_t)
    length, d = tokens.shape[1], tokens.shape[2]
    frames = encoder.shape[1]
    own_clips = tokens.shape[0]
    assert own_clips * 2 == n_t == 4 and bits >= 3
    per = d // n_f
    units_here = hidden_bias.shape[1]
    units = units_here * n_f
    heads_here = self_biases.shape[2]
    inner = n_f // GROUPS

    def begin(weights, extra=None, waits=()):
        keep = jnp.concatenate([half(w, core, 1) for w in weights], axis=1)
        send = jnp.concatenate([half(w, 1 - core, 1) for w in weights], axis=1)
        width = keep.shape[1]
        now, more = keep, extra
        for bit in range(bits - 2):
            rows = now.shape[0]
            out = send if bit == 0 else now
            if more is not None:
                out = jnp.concatenate([out, more.reshape(-1, width)])
            if waits:
                out = after(out, *waits)
            came = flip(out, bit, n_f)
            low = (f >> bit) % 2 == 0
            a, b = now, came[:rows]
            now = jnp.where(low, jnp.concatenate([a, b]), jnp.concatenate([b, a]))
            if more is not None:
                b = came[rows:]
                more = jnp.where(low, jnp.concatenate([more, b]), jnp.concatenate([b, more]))
        return now if more is None else jnp.concatenate([now, more])

    small = jnp.concatenate(
        [v.reshape(-1) for v in (norm_gains, norm_shifts, branch_biases, hidden_bias, self_biases, cross_biases)]
    )
    lanes = 4 * PAIR
    small_rows = -(-small.shape[0] // (16 * lanes)) * 16
    small = jnp.pad(small, (0, small_rows * lanes - small.shape[0])).reshape(small_rows, lanes)

    first = begin([self_weights[0], self_weights[1], self_weights[2], self_output.T], small)
    second = begin([cross_query, cross_memory[0], cross_memory[1], cross_output.T])
    third = begin([hidden_weight, reduce_weight.T])
    wide_half = units // 2
    pad = -(-frames // 512) * 512 - frames
    w_self, start, upstream, memory = gather(
        sizes, first, [tokens, cotangent, jnp.pad(encoder, ((0, 0), (0, pad), (0, 0)))]
    )

    rows = d // GROUPS
    table = w_self.reshape(n_t, GROUPS, -1, lanes)[:, :, rows:].reshape(n_t, n_f, -1).astype(F32)
    features = table[0, :, : 9 * per].reshape(n_f, 9, per).transpose(1, 0, 2).reshape(9, d)
    at = 9 * per
    hidden_slots = half(table[:, :, at : at + units_here].reshape(n_t, 1, units), core, 2)
    at += units_here

    def head_slots(at):
        v = table[:, :, at : at + 2 * heads_here].reshape(n_t, n_f, 2, heads_here).transpose(2, 0, 1, 3)
        return half(v.reshape(2, n_t, n_f * heads_here), core, 2).reshape(2, 1, -1)

    self_bias = head_slots(at)
    cross_bias = head_slots(at + 2 * heads_here)
    zero = jnp.zeros_like(self_bias[0])
    qkv_bias = jnp.concatenate([self_bias[0], zero, self_bias[1]], axis=1)
    kv_bias = jnp.concatenate([zero, cross_bias[1]], axis=1)
    gain, shift, branch = ([features[3 * i + j : 3 * i + j + 1] for j in range(3)] for i in range(3))

    part_frames = frames // n_t

    def scatter_end(now):
        for bit in range(bits - 3, 0, -1):
            up = (f >> bit) % 2
            now = half(now, up, 0) + flip(half(now, 1 - up, 0).astype(BF16), bit, n_f).astype(F32)
        return half(now, core, 0), flip(half(now, 1 - core, 0), 0, n_f)

    def unpack(shares, widths):
        keep, came = shares
        result, at = [], 0
        for width in widths:
            a, b = keep[:, at : at + width], came[:, at : at + width]
            result.append(jnp.where(core == 0, jnp.concatenate([a, b], 1), jnp.concatenate([b, a], 1)))
            at += width
        return result

    w_cross, normed_one, qkv, mixed_one, log_one, part, came = self_forward(
        sizes, second, start, gain[0], shift[0], qkv_bias, w_self
    )
    (
        g_feed, middle, normed_two, cross_q, kv, mixed_two, log_two, later, out_part, out_came, part, came, hidden_sums,
    ) = cross_forward(
        sizes, third, start, part, came, branch[0], gain[1], shift[1], cross_bias[0], kv_bias, memory, w_cross, branch[1],
        gain[2], shift[2], upstream, hidden_slots, n_t, frames,
    )

    output, memory_came, later_grad, sums_three, cross_sums, part, part_came, g_cross, memory_keep, feed_own = cross_back(
        sizes, part, came, later, gain[2], upstream, cross_q, kv, mixed_two, log_two, w_cross, normed_two, memory,
        g_feed, out_part, out_came, branch[2], own_clips, n_t, frames,
    )
    memory_share, half_grad, sums_one, sums_two, self_sums, g_self, cross_own = self_back(
        sizes, part, part_came, middle, gain[1], later_grad, qkv, mixed_one, log_one, w_self, normed_one, g_cross,
        memory_keep, memory_came, start, gain[0], own_clips, part_frames,
    )

    lead = jnp.where(core == 0, 1.0, 0.0).astype(F32)
    feature_sums = jnp.stack(
        [sums_one[0], sums_two[0], sums_three[0], sums_one[1], sums_two[1], sums_three[1],
         sums_two[2], sums_three[2], sums_three[3]]
    ) * lead

    def from_slots(v):
        natural = jnp.swapaxes(v, 0, 1)
        wide = jnp.zeros((*natural.shape[:2], 2 * natural.shape[2]), F32)
        return lax.dynamic_update_slice(wide, natural, (0, 0, core * natural.shape[2]))

    def by_slot(v):
        return v[:2].reshape(2, n_t, -1).transpose(1, 0, 2)

    unit_sums = [from_slots(hidden_sums[:, :1]), from_slots(by_slot(self_sums)), from_slots(by_slot(cross_sums))]
    packed = jnp.concatenate([feature_sums.reshape(-1)] + [u.reshape(-1) for u in unit_sums])
    boxes = -(-packed.size // (32 * 1024))
    packed = jnp.pad(packed.reshape(-1), (0, boxes * 32 * 1024 - packed.size)).reshape(32, 8 * boxes, 128)
    tokens_grad, packed, self_own = finish(sizes, half_grad, g_self, packed, own_clips)
    for bit in range(1, bits - 2):
        packed = packed + flip(packed, bit, n_f)
    packed = packed.reshape(-1)
    feature_share = lax.dynamic_slice(packed[: 9 * d].reshape(9, d), (0, f * per), (9, per))

    def unit_share(at, count, total):
        block = packed[at : at + count * n_t * total].reshape(count, n_t, total)
        return lax.dynamic_slice(block, (0, z, f * (total // n_f)), (count, 1, total // n_f))

    at = 9 * d
    hidden_bias_share = unit_share(at, 1, units)[0]
    at += n_t * units
    self_bias_share = unit_share(at, 2, heads_here * n_f)
    at += 2 * n_t * heads_here * n_f
    cross_bias_share = unit_share(at, 2, heads_here * n_f)

    hidden_share, reduce_t = unpack(scatter_end(feed_own), [wide_half, wide_half])
    cq_share, ck_share, cv_share, cross_out_t = unpack(scatter_end(cross_own), [PAIR] * 4)
    q_share, k_share, v_share, self_out_t = unpack(scatter_end(self_own), [PAIR] * 4)

    memory_share = lax.dynamic_slice_in_dim(memory_share, part_frames * z % 16, part_frames, axis=1)

    return (
        output,
        tokens_grad,
        memory_share,
        jnp.stack([q_share, k_share, v_share]),
        self_bias_share,
        self_out_t.T,
        cq_share,
        jnp.stack([ck_share, cv_share]),
        cross_bias_share,
        cross_out_t.T,
        hidden_share,
        hidden_bias_share,
        reduce_t.T,
        feature_share[0:3],
        feature_share[3:6],
        feature_share[6:9],
    )


def solution(mesh):
    n_f, n_t = mesh.shape["fsdp"], mesh.shape["tensor"]
    clips = P("fsdp", None, None)
    stacked = P(None, "fsdp", "tensor")
    biases = P(None, "tensor", "fsdp")
    up, down, rows = P("fsdp", "tensor"), P("tensor", "fsdp"), P(None, "fsdp")
    return jax.shard_map(
        functools.partial(on_device, n_f, n_t),
        mesh=mesh,
        in_specs=(
            clips, clips, clips, stacked, biases, down, up, stacked, biases, down, up, down, down, rows, rows, rows,
        ),
        out_specs=(
            clips, clips, P("fsdp", "tensor", None), stacked, biases, down, up, stacked, biases, down, up, down,
            down, rows, rows, rows,
        ),
        check_vma=False,
    )
```
